512 devices in a mesh: strike: 128 (over z, y, core), dip: 4 (over x).
Axes of the slice: x: 4, y: 8, z: 8, core: 2. Of those that a mesh axis runs over, the one named last changes fastest.
Arguments:
- slip: float32 [4096, 2048], P('strike', 'dip'), may hold values from 0 to 2
- rate: float32 [4096, 2048], P('strike', 'dip'), may hold values from 0 to 2
- prestress: float32 [4096, 2048], P('strike', 'dip'), may hold values from 0 to 1.5
- normal_stress: float32 [4096, 2048], P('strike', 'dip'), may hold values from 0.5 to 1.5
- history: float32 [8, 2, 4096, 2048], P(None, None, 'strike', 'dip'), may hold values from -6 to 6
- fric_flag: int32 [4096, 2048], P('strike', 'dip'), may hold values 0 or 1
- row_dest: int32 [4, 524288, 1], P('dip', 'strike'), may hold values from 0 to 127; in each aligned block of 4096 rows (0 to 4095, 4096 to 8191, ..., all dimensions but the last counted through in order) at most 64 rows name the same one
- row_node: int32 [4, 524288], P('dip', 'strike'), may hold values from 0 to 16383
- fe_traction: float32 [4, 524288], P('dip', 'strike'), may hold values from -8 to 8
- fe_count: int32 [4, 128], P('dip', 'strike'), may hold values from 1 to 4096, 393216 in all within a row
Outputs:
- new_rate: float32 [4096, 2048], P('strike', 'dip')
- stress: float32 [4096, 2048], P('strike', 'dip')
- fe_rate: float32 [4, 524288], P('dip', 'strike')
The draws below stay inside these ranges and needn't reach their ends.
Inputs may be any that keep to these rules, and one draw needn't show every extreme that they name: `row_dest`: among the 4096 rows of one partition at most 64 name the same strike block, and some partition has exactly 64 rows naming one block. `fe_count`: the counts of one dip row sum to 3 * 4096 * P // 4 with P the number of strike devices; some partition is full.
All inputs are finite; a program needn't handle non-finite values. No bound on the sum of `fric_flag` on one device may be relied on, other than what follows from the above.
Results may differ from the reference program's by a relative error of at most 0.0003.
Values sent between devices are 32-bit elements; how exact they have to be, the bound alone decides.
No kernel may reach another device: no remote copies, remote signals or barrier semaphores. Data moves between devices by JAX's collectives and lax.ppermute only.
A program may use at most 64 MiB of HBM per device.

```python
import math
import jax
import jax.numpy as jnp
import numpy as np
from jax import lax

NS = 4096
ND = 2048
LAGS = 8
ROWS = 4096
CAP = 64
N_STRIKE = 128
N_DIP = 4


def with_ends(drawn, key, low, largest):
    index_at = [jax.random.randint(jax.random.fold_in(key, axis), (), 0, length) for axis, length in enumerate(drawn.shape)]
    longest = drawn.shape.index(max(drawn.shape))
    beside = index_at[:longest] + [(index_at[longest] + 1) % drawn.shape[longest]] + index_at[longest + 1:]
    return drawn.at[tuple(index_at)].set(low).at[tuple(beside)].set(largest)


def steps_of(own_key, shape, split, low, top_value):
    loudness = 1.0
    for axis_at, parts in split:
        draws = jax.random.uniform(jax.random.fold_in(jax.random.fold_in(own_key, 6), axis_at), (parts,), jnp.float32, low / len(split), top_value / len(split))
        loudness = loudness * jnp.repeat(jnp.exp(draws), shape[axis_at] // parts).reshape((-1,) + (1,) * (len(shape) - 1 - axis_at))
    return loudness


def split_up(count, total, most, skew):
    loads = [(1 << 20) // math.isqrt(rank ** skew) + 1 for rank in range(2, count + 1)]
    surplus, counts = total - most - (count - 1), [1] * (count - 1)
    while surplus > 0:
        free = [i for i in range(count - 1) if counts[i] < most]
        mass, budget = sum([loads[i] for i in free]), surplus
        for i in free:
            extra = min(most - counts[i], max(1, budget * loads[i] // mass), surplus)
            counts[i] = counts[i] + extra
            surplus = surplus - extra
    return np.array([most] + counts)


def uneven_parts(rng, number_of, total, bound, slope):
    if number_of == 2:
        one = jax.random.randint(rng, (), max(1, total - bound), min(bound, total - 1) + 1)
        return jnp.stack([one, total - one])
    lengths = jnp.asarray(split_up(number_of, total, bound, slope), jnp.int32)
    twos = (number_of - 1) // 2
    source_of, receiver = lengths[1:1 + 2 * twos:2], lengths[2:2 + 2 * twos:2]
    room = jnp.minimum(source_of - 1, bound - receiver)
    shifted = jax.random.randint(jax.random.fold_in(rng, 1), (twos,), 0, 1 << 20) % (room + 1)
    lengths = lengths.at[1:1 + 2 * twos:2].set(source_of - shifted).at[2:2 + 2 * twos:2].set(receiver + shifted)
    return lengths[jax.random.permutation(jax.random.fold_in(rng, 2), number_of)]


def routed_block(stream_key, own, number, rows, number_of, top, bound, lean):
    sequence = jax.random.permutation(stream_key, number_of)
    crowded, usual = shares(number_of, rows * top, bound, lean, True), shares(number_of, rows * top, bound, lean, False)
    places = jnp.arange(number_of)

    def named(sizes, rotation):
        used = int((sizes > 0).sum())
        fixed = max(1, used // 4)
        moved = fixed + (places - fixed + rotation * (used - fixed)) % max(1, number_of - fixed)
        return jnp.zeros((number_of,), jnp.int32).at[sequence[jnp.where(places < fixed, places, moved)]].set(jnp.asarray(sizes, jnp.int32))

    sizes = jnp.where(number % 4 == 0, named(crowded, number // 4), named(usual, number - number // 4 - 1))
    mixed = jax.random.permutation(jax.random.fold_in(own, 3), number_of)
    giver, sink = mixed[0:number_of // 2 * 2:2], mixed[1:number_of // 2 * 2:2]
    slack = jnp.minimum(sizes[giver] - 1, bound - sizes[sink]) // 2
    slack = jnp.where((giver == sequence[0]) | (sink == sequence[0]) | (sizes[sink] == 0), 0, jnp.maximum(slack, 0))
    moved = jax.random.randint(jax.random.fold_in(own, 4), (number_of // 2,), 0, 1 << 20) % (slack + 1)
    sizes = sizes.at[giver].add(-moved).at[sink].add(moved)
    labels = jnp.searchsorted(jnp.cumsum(sizes), jnp.arange(rows * top), side="right").astype(jnp.int32)
    grid = labels.reshape(top, rows).T
    grid = grid[jax.random.permutation(jax.random.fold_in(own, 1), rows)]
    rotation = jax.random.randint(jax.random.fold_in(own, 2), (rows, 1), 0, top)
    return jnp.take_along_axis(grid, (jnp.arange(top)[None, :] + rotation) % top, axis=1)


def shares(amount, total, most, slope, full):
    loads = [(1 << 20) // math.isqrt(rank ** slope) + 1 for rank in range(1, amount + 1)]
    largest = most if full else min(most, max(-(-total // amount), total * loads[0] // sum(loads)))
    least = 1 if total - largest >= amount - 1 else 0
    given, rest = [largest] + [least] * (amount - 1), total - largest - least * (amount - 1)
    while rest > 0:
        free = [i for i in range(1, amount) if given[i] < largest] or [i for i in range(1, amount) if given[i] < most]
        mass, left = sum([loads[i] for i in free]), rest
        for i in free:
            addition = min(most - given[i], max(1, left * loads[i] // mass), rest)
            given[i] = given[i] + addition
            rest = rest - addition
    return np.array(given)


def noise(own_key, dims, width, most, shards=(), kind=jnp.bfloat16):
    values = jax.random.normal(own_key, dims, jnp.float32) * width
    if len(shards) > 0:
        values = steps_of(own_key, dims, shards, -0.22, 0.18) * values
    return jnp.clip(values, min=-most, max=most).astype(kind)


def setup_inputs(seed: int = 0) -> dict:
    key_list = jax.random.split(jax.random.key(seed), 11)
    slip = jnp.clip(2.0 * jax.random.uniform(key_list[0], (NS, ND), jnp.float32) ** steps_of(key_list[0], (NS, ND), ((0, 128), (1, 4)), -0.2, 0.2), 0.0, 2.0)
    rate = jnp.clip(2.0 * jax.random.uniform(key_list[1], (NS, ND), jnp.float32) ** steps_of(key_list[1], (NS, ND), ((0, 128), (1, 4)), -0.2, 0.2), 0.0, 2.0)
    prestress = jnp.clip(1.5 * jax.random.uniform(key_list[2], (NS, ND), jnp.float32) ** steps_of(key_list[2], (NS, ND), ((0, 128), (1, 4)), -0.2, 0.2), 0.0, 1.5)
    normal_stress = jnp.clip(0.5 + 1.0 * jax.random.uniform(key_list[3], (NS, ND), jnp.float32) ** steps_of(key_list[3], (NS, ND), ((0, 128), (1, 4)), -0.2, 0.2), 0.5, 1.5)
    history = noise(key_list[4], (LAGS, 2, NS, ND), 1.0, 6.0, ((2, 128), (3, 4)), jnp.float32)
    fric_flag = with_ends((jax.random.randint(key_list[5], (NS, ND), 0, 4) < 3).astype(jnp.int32), jax.random.fold_in(key_list[5], 1), 0, 1)
    row_dest_keys = jax.random.split(jax.random.fold_in(key_list[6], 1), N_DIP * (N_STRIKE * ROWS) // ROWS)
    row_dest_turns = jax.random.permutation(jax.random.fold_in(key_list[6], 3), N_DIP * (N_STRIKE * ROWS) // ROWS)
    row_dest = jax.vmap(lambda own, number: routed_block(jax.random.fold_in(key_list[6], 2), own, number, ROWS, N_STRIKE, 1, CAP, 2))(row_dest_keys, row_dest_turns).reshape((N_DIP, N_STRIKE * ROWS, 1))
    row_node = with_ends(jax.random.randint(key_list[7], (N_DIP, N_STRIKE * ROWS), 0, NS * ND // (N_STRIKE * N_DIP)), jax.random.fold_in(key_list[7], 1), 0, (NS * ND // (N_STRIKE * N_DIP)) - 1).astype(jnp.int32)
    fe_traction = noise(key_list[8], (N_DIP, N_STRIKE * ROWS), 2.0, 8.0, ((0, 4), (1, 128)), jnp.float32)
    fe_count = jax.vmap(lambda own: uneven_parts(own, N_STRIKE, 3 * ROWS * N_STRIKE // 4, ROWS, 2))(jax.random.split(key_list[9], N_DIP)).reshape((N_DIP, N_STRIKE)).astype(jnp.int32)
    return dict(slip=slip, rate=rate, prestress=prestress, normal_stress=normal_stress, history=history, fric_flag=fric_flag, row_dest=row_dest, row_node=row_node, fe_traction=fe_traction, fe_count=fe_count)


full_turn = 2.0 * math.pi
STEP_DT = 0.5
SHEAR_MOD = 1.0
DAMPING = 0.5
STATIC_FR = 0.6
DYNAMIC_FR = 0.4
KERNEL_DT = 0.5
KERNEL_DECAY = 0.15
KERNEL_FREQ = 0.9

def reverse_bits(indices, levels):
    result = indices * 0
    for bit_index in range(levels):
        result = result + indices // 2 ** bit_index % 2 * 2 ** (levels - 1 - bit_index)
    return result

def wavenumber(freq_row, freq_col, length_row, length_col):
    signed_row = jnp.where(freq_row >= length_row // 2, freq_row - length_row, freq_row).astype(jnp.float32) / length_row
    signed_col = jnp.where(freq_col >= length_col // 2, freq_col - length_col, freq_col).astype(jnp.float32) / length_col
    return full_turn * jnp.sqrt(signed_row * signed_row + signed_col * signed_col)

def memory_sum(history, wavenum):
    real_part = jnp.zeros_like(wavenum)
    imag_part = jnp.zeros_like(wavenum)
    for lag_index in range(history.shape[0]):
        spacing = (lag_index + 1) * wavenum
        weight = KERNEL_DT * jnp.exp(-KERNEL_DECAY * spacing) * jnp.cos(KERNEL_FREQ * spacing)
        real_part = real_part + weight * history[lag_index, 0]
        imag_part = imag_part + weight * history[lag_index, 1]
    return (real_part, imag_part)

def reference(slip, rate, prestress, normal_stress, history, fric_flag, row_dest, row_node, fe_traction, fe_count):
    levels = N_STRIKE.bit_length() - 1
    rows_dev = NS // N_STRIKE
    cols_dev = ND // N_DIP
    scaling = 1.0 / math.sqrt(NS * ND)
    slip_new = slip + STEP_DT * rate
    position = jnp.arange(NS, dtype=jnp.int32)
    freq_of = reverse_bits(position // rows_dev, levels) + N_STRIKE * (position % rows_dev)
    spot_of = reverse_bits(position % N_STRIKE, levels) * rows_dev + position // N_STRIKE
    natural = jnp.fft.fft2(slip_new) * scaling
    spectrum = natural[freq_of]
    freq_row = jnp.broadcast_to(freq_of[:, None], (NS, ND))
    freq_col = jnp.broadcast_to(jnp.arange(ND, dtype=jnp.int32)[None, :], (NS, ND))
    wavenum = wavenumber(freq_row, freq_col, NS, ND)
    memory_re, memory_im = memory_sum(history, wavenum)
    factor = -0.5 * SHEAR_MOD * wavenum
    func_spec = lax.complex(factor * (jnp.real(spectrum) - memory_re), factor * (jnp.imag(spectrum) - memory_im))
    functional = jnp.real(jnp.fft.ifft2(func_spec[spot_of])) * (NS * ND) * scaling
    target = row_dest[:, :, 0]
    row_pos = jnp.arange(N_STRIKE * ROWS, dtype=jnp.int32)
    active = (row_pos % ROWS)[None, :] < jnp.repeat(fe_count, ROWS, axis=1)
    strike_at = target * rows_dev + row_node // cols_dev
    dip_at = jnp.arange(N_DIP, dtype=jnp.int32)[:, None] * cols_dev + row_node % cols_dev
    traction = jnp.zeros((NS, ND), jnp.float32).at[strike_at, dip_at].add(jnp.where(active, fe_traction, 0.0))
    stress = prestress + functional + traction
    strength = normal_stress * (STATIC_FR - (STATIC_FR - DYNAMIC_FR) * jnp.minimum(slip_new, 1.0))
    new_rate = jnp.where(fric_flag == 1, jnp.maximum(stress - strength, 0.0) / DAMPING, 0.0)
    fe_rate = jnp.where(active, new_rate[strike_at, dip_at], 0.0)
    return (new_rate, stress, fe_rate)
```

```python
import math

import jax
import jax.numpy as jnp
import numpy as np
from jax import lax
from jax.experimental import pallas as pl
from jax.experimental.pallas import tpu as pltpu
from jax.sharding import Mesh
from jax.sharding import PartitionSpec as P

NS, ND = 4096, 2048
PS, QD = 128, 4
ROWS_DEV, COLS_DEV = NS // PS, ND // QD
GROUP = PS * QD
RATE_DT = 0.5
LEVELS = 7
CAP = 64
ROWS = 4096
CHUNK = 512
SCALE = 1.0 / math.sqrt(NS * ND)
bf16 = jnp.bfloat16
f32 = jnp.float32
NN = (((1,), (0,)), ((), ()))
NT = (((1,), (1,)), ((), ()))


def np_split(table):
    hi = table.astype(np.float32).astype(jnp.bfloat16)
    lo = (table - hi.astype(np.float64)).astype(np.float32).astype(jnp.bfloat16)
    return np.stack([hi, lo])


def np_rev(p):
    return sum(((p >> b) & 1) << (LEVELS - 1 - b) for b in range(LEVELS))


def dip_tables():
    i = np.arange(COLS_DEV)
    ang = 2 * np.pi * ((i[:, None] * i[None, :]) % ND) / ND
    return np.concatenate([np_split(np.cos(ang)), np_split(np.sin(ang))])


def strike_tables():
    p = np.arange(PS)
    k1 = np_rev(p)
    ang = 2 * np.pi * ((k1[:, None] * p[None, :]) % PS) / PS
    first = np.concatenate([np.cos(ang), -np.sin(ang)])
    r = np.arange(ROWS_DEV)
    tw = 2 * np.pi * (k1[:, None] * r[None, :]) / NS
    twiddle = np.stack([np.tile(np.cos(tw), (1, 4)), np.tile(np.sin(tw), (1, 4))]).astype(np.float32)
    small = 2 * np.pi * ((r[:, None] * r[None, :]) % ROWS_DEV) / ROWS_DEV
    cb = np.kron(np.eye(4), np.cos(small))
    sb = np.kron(np.eye(4), np.sin(small))
    second = np.block([[cb, -sb], [sb, cb]])
    second_inv = np.block([[cb, sb], [-sb, cb]])
    return np_split(first), np_split(first.T), twiddle, np_split(second), np_split(second_inv)


def memory_tables():
    out = np.zeros((2, 2 * PS, 2 * PS), np.float32)
    eye = np.eye(ROWS_DEV)
    for special in range(2):
        home = {0: 0, 1: 1, 2: 3, 3: 2} if special else {j: j for j in range(4)}
        partner = {0: 0, 3: 3, 1: 2, 2: 1} if special else {0: 3, 3: 0, 1: 2, 2: 1}
        for slot in range(4):
            own, other = home[slot], home[partner[slot]]
            for slab, part, w_re, w_im in ((own, 0, 0.5, 0.5), (own, 1, -0.5, 0.5), (other, 0, 0.5, -0.5), (other, 1, 0.5, 0.5)):
                rows = slice(64 * slab + 32 * part, 64 * slab + 32 * part + 32)
                out[special, rows, 32 * slot : 32 * slot + 32] += w_re * eye
                out[special, rows, PS + 32 * slot : PS + 32 * slot + 32] += w_im * eye
    return out.astype(jnp.bfloat16)


def dot(a, b, dims=NN):
    return lax.dot_general(a, b, dims, preferred_element_type=f32)


def split(x):
    hi = x.astype(bf16)
    return hi, (x - hi.astype(f32)).astype(bf16)


def dot_data_table(x, t_hi, t_lo):
    hi, lo = split(x)
    return dot(hi, t_hi) + (dot(lo, t_hi) + dot(hi, t_lo))


def dot_table_data(t_hi, t_lo, x):
    hi, lo = split(x)
    return dot(t_hi, hi) + (dot(t_hi, lo) + dot(t_lo, hi))


def iota(shape, dim):
    return lax.broadcasted_iota(jnp.int32, shape, dim)


def rev_bits(p):
    out = 0
    for b in range(LEVELS):
        out = out + (((p >> b) & 1) << (LEVELS - 1 - b))
    return out


def quarter(q):
    turn = (q * iota((1, COLS_DEV), 1)) & 3
    cm = jnp.where(turn == 0, 1.0, jnp.where(turn == 2, -1.0, 0.0))
    sm = jnp.where(turn == 1, 1.0, jnp.where(turn == 3, -1.0, 0.0))
    return cm, sm


def signed(freq, length):
    return jnp.where(freq >= length // 2, freq - length, freq).astype(f32) * (1.0 / length)


def slip_part(slip, rate, tables, q):
    x = slip + RATE_DT * rate
    phase = iota((ROWS_DEV, COLS_DEV), 1) & 3
    x4 = jnp.concatenate([jnp.where(phase == b, x, 0.0) for b in range(4)], axis=0)
    c = dot_data_table(x4, tables[0], tables[1])
    s = dot_data_table(x4, tables[2], tables[3])
    cm, sm = quarter(q)
    c, s = cm * c - sm * s, sm * c + cm * s
    cs = [c[32 * b : 32 * b + 32] for b in range(4)]
    ss = [s[32 * b : 32 * b + 32] for b in range(4)]
    c_even, c_odd = cs[0] + cs[2], cs[1] + cs[3]
    s_sum = (ss[0] + ss[2]) + (ss[1] + ss[3])
    h_a = (c_even + c_odd) + s_sum
    first = iota((ROWS_DEV, COLS_DEV), 1) == 0
    h_d = (c_even + jnp.where(first, -c_odd, c_odd)) - s_sum
    even = cs[0] - cs[2] + ss[3] - ss[1]
    odd = ss[0] - ss[2] + cs[1] - cs[3]
    return jnp.concatenate([h_a, even + odd, even - odd, h_d], axis=0).T


def memory_part(history, p, q):
    ks = rev_bits(p) + PS * iota((ROWS_DEV, COLS_DEV), 0)
    kd = q * COLS_DEV + iota((ROWS_DEV, COLS_DEV), 1)
    fs, fd = signed(ks, NS), signed(kd, ND)
    wave = (2.0 * math.pi) * jnp.sqrt(fs * fs + fd * fd)
    grow = jnp.exp(-0.15 * wave)
    ang = 0.9 * wave
    z_re, z_im = grow * jnp.cos(ang), grow * jnp.sin(ang)
    w_re, w_im = 0.5 * z_re, 0.5 * z_im
    m_re, m_im = w_re * history(0, 0), w_re * history(0, 1)
    for lag in range(1, 8):
        w_re, w_im = w_re * z_re - w_im * z_im, w_re * z_im + w_im * z_re
        m_re = m_re + w_re * history(lag, 0)
        m_im = m_im + w_re * history(lag, 1)
    both = jnp.concatenate([m_re, m_im], axis=0)
    odd = (q & 1) == 1
    both = jnp.concatenate([jnp.where(odd, 0.0, both), jnp.where(odd, both, 0.0)], axis=0)
    row = iota((COLS_DEV, COLS_DEV), 0)
    from_col = jnp.where(q < 2, row, (COLS_DEV - row) & (COLS_DEV - 1))
    perm = (iota((COLS_DEV, COLS_DEV), 1) == from_col).astype(f32).astype(bf16)
    hi, lo = split(both)
    return dot(perm, hi, NT) + dot(perm, lo, NT)


def send_kernel(idx, slip, rate, history, tables, out):
    p, q = idx[0], idx[1]
    out[pl.ds(0, GROUP, stride=2), :] = slip_part(slip[...], rate[...], [tables[i] for i in range(4)], q)
    out[pl.ds(1, GROUP, stride=2), :] = memory_part(lambda lag, part: history[lag, part], p, q)


def strike_part(slip_recv, mem_recv, first, first_t, twiddle, second, second_inv, mem_table, ell):
    n = PS
    u = (slip_recv[0:n] + slip_recv[n : 2 * n]) + (slip_recv[2 * n : 3 * n] + slip_recv[3 * n :])
    mem = jnp.concatenate([mem_recv[0:n] + mem_recv[n : 2 * n], mem_recv[2 * n : 3 * n] + mem_recv[3 * n :]], axis=1)
    m_hi, m_lo = split(mem)
    w = dot(m_hi, mem_table) + dot(m_lo, mem_table)
    a = dot_table_data(first[0], first[1], u)
    a_re, a_im = a[:n], a[n:]
    tc, ts = twiddle[0], twiddle[1]
    b = jnp.concatenate([a_re * tc + a_im * ts, a_im * tc - a_re * ts], axis=1)
    spec = dot_data_table(b, second[0], second[1])
    lane = iota((n, n), 1)
    fs = signed(rev_bits(iota((n, n), 0)) + PS * (lane & 31), NS)
    slot = lane >> 5
    kd = jnp.where((slot == 1) | (slot == 2), COLS_DEV + ell, ell)
    kd = jnp.where((slot == 3) & (ell == 0), 2 * COLS_DEV, kd)
    fd = kd.astype(f32) * (1.0 / ND)
    wave = (2.0 * math.pi) * jnp.sqrt(fs * fs + fd * fd)
    factor = (-0.5 * SCALE) * wave
    factor = jnp.concatenate([factor, factor], axis=1)
    g = factor * (SCALE * spec - w)
    b = dot_data_table(g, second_inv[0], second_inv[1])
    b_re, b_im = b[:, :n], b[:, n:]
    b = jnp.concatenate([b_re * tc - b_im * ts, b_re * ts + b_im * tc], axis=0)
    return dot_table_data(first_t[0], first_t[1], b)


def strike_kernel(idx, recv, outbox, first, first_t, twiddle, second, second_inv, mem_table, out):
    p, q = idx[0], idx[1]
    ell = PS * q + p
    special = jnp.where(ell == 0, 1, 0)
    t = strike_part(
        recv[pl.ds(0, GROUP, stride=2), :],
        recv[pl.ds(1, GROUP, stride=2), :],
        first,
        first_t,
        twiddle,
        second,
        second_inv,
        mem_table[special],
        ell,
    )
    box = outbox[...]
    for qd in range(QD):
        out[pl.ds(2 * PS * qd, PS, stride=2), :] = t
        out[pl.ds(2 * PS * qd + 1, PS, stride=2), :] = jnp.where(q == qd, box, 0.0)


def route_part(dest, node, value, count):
    dest = [dest[:, CHUNK * i : CHUNK * (i + 1)] for i in range(ROWS // CHUNK)]
    upto = (iota((CHUNK, CHUNK), 0) <= iota((CHUNK, CHUNK), 1)).astype(f32).astype(bf16)
    carry = jnp.zeros((PS, 1), f32)
    box = jnp.zeros((PS, 2 * CAP), f32)
    ranks = []
    for i in range(ROWS // CHUNK):
        cut = slice(CHUNK * i, CHUNK * (i + 1))
        named = iota((PS, CHUNK), 0) == dest[i]
        onehot = named.astype(f32).astype(bf16)
        upto_here = dot(onehot, upto) + carry
        rank = jnp.sum(jnp.where(named, upto_here, 0.0), axis=0, keepdims=True).astype(jnp.int32) - 1
        carry = upto_here[:, CHUNK - 1 : CHUNK]
        ranks.append(rank)
        live = (CHUNK * i + iota((1, CHUNK), 1)) < count
        v = jnp.where(live, value[:, cut], 0.0)
        v_hi = v.astype(bf16).astype(f32)
        v_lo = v - v_hi
        at = node[:, cut]
        n_hi = ((((at >> 7) & 3) << 5) + (at >> 9)) << 7
        n_lo = at & 127
        here = iota((CAP, CHUNK), 0) == rank
        part_1 = jnp.concatenate([jnp.where(here, v_hi, 0.0), jnp.where(here, n_hi.astype(f32), 0.0)], axis=0)
        part_2 = jnp.concatenate([jnp.where(here, v_lo, 0.0), jnp.where(here, n_lo.astype(f32), 0.0)], axis=0)
        box = box + (dot(onehot, part_1.astype(bf16), NT) + dot(onehot, part_2.astype(bf16), NT))
    return box, jnp.concatenate(ranks, axis=1)


def route_kernel(count, dest, node, value, out, rank):
    out[...], rank[...] = route_part(dest[...], node[...], value[...], count[0, 0])


def functional_part(recv, tables, q):
    t = recv.T
    a, b, c, d = [t[32 * j : 32 * j + 32] for j in range(4)]
    s1, d1, s2, d2 = a + d, a - d, b + c, b - c
    fix = jnp.where(iota((ROWS_DEV, COLS_DEV), 1) == 0, 2.0 * d, 0.0)
    even = jnp.concatenate([s1 + s2, s1 + d2 - fix, s1 - s2, s1 - d2 - fix], axis=0)
    odd = jnp.concatenate([d1 + d2, d1 - s2, d1 - d2, d1 + s2], axis=0)
    cm, sm = quarter(q)
    even, odd = cm * even + sm * odd, cm * odd - sm * even
    f = dot_data_table(even, tables[0], tables[1]) + dot_data_table(odd, tables[2], tables[3])
    phase = iota((ROWS_DEV, COLS_DEV), 1) & 3
    f = [jnp.where(phase == i, f[32 * i : 32 * i + 32], 0.0) for i in range(4)]
    return (f[0] + f[1]) + (f[2] + f[3])


def unpack_rows(fe, roll):
    top, bot = fe[0:CAP], fe[CAP:PS]
    left = iota((CAP, PS), 1) < CAP
    value = jnp.where(left, top, roll(bot))
    node = jnp.where(left, roll(top), bot).astype(jnp.int32)
    return value, node >> 7, node & 127


def lanes_of(x, group):
    return jnp.concatenate([x[4 * group + i : 4 * group + i + 1] for i in range(4)], axis=1)


def column_onehot(lo):
    return (iota((PS, CHUNK), 0) == lo).astype(f32).astype(bf16)


def traction_step(value, hi, onehot):
    named = iota((PS, CHUNK), 0) == hi
    v_hi = value.astype(bf16).astype(f32)
    rows = jnp.concatenate([jnp.where(named, v_hi, 0.0), jnp.where(named, value - v_hi, 0.0)], axis=0).astype(bf16)
    return dot(rows, onehot, NT)


def sample_step(rate_parts, hi, onehot):
    got = dot(rate_parts, jnp.concatenate([onehot, onehot], axis=0))
    return jnp.sum(jnp.where(iota((PS, CHUNK), 0) == hi, got, 0.0), axis=0, keepdims=True)


def owner_kernel(idx, recv, slip, rate, prestress, normal, flag, tables, new_rate, stress, sampled, onehots):
    q = idx[1]
    roll = lambda x: pltpu.roll(x, CAP, 1)
    fe = recv[pl.ds(1, GROUP, stride=2), :]
    fe = (fe[0:PS] + fe[PS : 2 * PS]) + (fe[2 * PS : 3 * PS] + fe[3 * PS :])
    value, hi, lo = unpack_rows(fe, roll)
    acc = jnp.zeros((2 * PS, PS), f32)
    groups = CAP // 4
    for g in range(groups):
        onehot = column_onehot(lanes_of(lo, g))
        onehots[g] = onehot
        acc = acc + traction_step(lanes_of(value, g), lanes_of(hi, g), onehot)
    acc = acc[:PS] + acc[PS:]
    traction = jnp.concatenate([acc[32 * i : 32 * i + 32] for i in range(4)], axis=1)
    f = functional_part(recv[pl.ds(0, GROUP, stride=2), :], [tables[i] for i in range(4)], q)
    slip_new = slip[...] + RATE_DT * rate[...]
    total = prestress[...] + f + traction
    strength = normal[...] * (0.6 - (0.6 - 0.4) * jnp.minimum(slip_new, 1.0))
    fresh = jnp.where(flag[...] == 1, jnp.maximum(total - strength, 0.0) * 2.0, 0.0)
    stress[...] = total
    new_rate[...] = fresh
    stacked = jnp.concatenate([fresh[:, PS * i : PS * (i + 1)] for i in range(4)], axis=0)
    parts = jnp.concatenate(split(stacked), axis=1)
    for g in range(groups):
        got = sample_step(parts, lanes_of(hi, g), onehots[g])
        for i in range(4):
            sampled[4 * g + i : 4 * g + i + 1, :] = got[:, PS * i : PS * (i + 1)]
    sampled[CAP:PS, :] = roll(sampled[0:CAP, :])


def return_part(got, dest, rank, count):
    parts = jnp.concatenate(split(got.T[:CAP]), axis=1)
    out = []
    for i in range(ROWS // CHUNK):
        cut = slice(CHUNK * i, CHUNK * (i + 1))
        onehot = (iota((PS, CHUNK), 0) == dest[:, cut]).astype(f32).astype(bf16)
        here = dot(parts, jnp.concatenate([onehot, onehot], axis=0))
        here = jnp.sum(jnp.where(iota((CAP, CHUNK), 0) == rank[:, cut], here, 0.0), axis=0, keepdims=True)
        live = (CHUNK * i + iota((1, CHUNK), 1)) < count
        out.append(jnp.where(live, here, 0.0))
    return jnp.concatenate(out, axis=1)


def return_kernel(count, got, dest, rank, out):
    out[...] = return_part(got[...], dest[...], rank[...], count[0, 0])


STRIKE = ("z", "y", "c")
ALL = ("dip", "z", "y", "c")


def call(kernel, out_shape, smem, vmem, scratch=(), name=None):
    specs = [pl.BlockSpec(memory_space=pltpu.SMEM)] * smem + [pl.BlockSpec(memory_space=pltpu.VMEM)] * vmem
    outs = jax.tree.map(lambda _: pl.BlockSpec(memory_space=pltpu.VMEM), out_shape)
    return pl.pallas_call(kernel, out_shape=out_shape, in_specs=specs, out_specs=outs, scratch_shapes=scratch, name=name)


def sds(shape, dtype=f32):
    return jax.ShapeDtypeStruct(shape, dtype)


def body(slip, rate, prestress, normal_stress, history, fric_flag, row_dest, row_node, fe_traction, fe_count):
    p = lax.axis_index(STRIKE).astype(jnp.int32)
    q = lax.axis_index("dip").astype(jnp.int32)
    idx = jnp.stack([p, q])
    tables = jnp.asarray(dip_tables())
    first, first_t, twiddle, second, second_inv = [jnp.asarray(t) for t in strike_tables()]
    mem_table = jnp.asarray(memory_tables())

    sent = call(send_kernel, sds((2 * GROUP, PS)), 1, 4, name="send")(idx, slip, rate, history, tables)
    recv = lax.all_to_all(sent.reshape(GROUP, 2, PS), ALL, 0, 0, tiled=True).reshape(2 * GROUP, PS)
    dest = row_dest.reshape(1, ROWS)
    box, rank = call(route_kernel, (sds((PS, PS)), sds((1, ROWS), jnp.int32)), 1, 3, name="route")(
        fe_count, dest, row_node, fe_traction
    )
    sent = call(strike_kernel, sds((2 * GROUP, PS)), 1, 8, name="strike")(
        idx, recv, box, first, first_t, twiddle, second, second_inv, mem_table
    )
    recv = lax.all_to_all(sent.reshape(GROUP, 2, PS), ALL, 0, 0, tiled=True).reshape(2 * GROUP, PS)
    new_rate, stress, sampled = call(
        owner_kernel,
        (sds((ROWS_DEV, COLS_DEV)), sds((ROWS_DEV, COLS_DEV)), sds((PS, PS))),
        1,
        7,
        scratch=[pltpu.VMEM((CAP // 4, PS, CHUNK), bf16)],
        name="owner",
    )(idx, recv, slip, rate, prestress, normal_stress, fric_flag, tables)
    got = lax.all_to_all(sampled.reshape(PS, 1, PS), STRIKE, 0, 0, tiled=True).reshape(PS, PS)
    fe_rate = call(return_kernel, sds((1, ROWS)), 1, 3, name="back")(fe_count, got, dest, rank)
    return new_rate, stress, fe_rate


def solution(mesh):
    fine = Mesh(mesh.devices.reshape(8, 8, 2, 4), ("z", "y", "c", "dip"))
    field = P(STRIKE, "dip")
    rows = P("dip", STRIKE)
    in_specs = (field, field, field, field, P(None, None, STRIKE, "dip"), field, P("dip", STRIKE, None), rows, rows, rows)
    return jax.shard_map(body, mesh=fine, in_specs=in_specs, out_specs=(field, field, rows), check_vma=False)
```

```python
import math

import jax
import jax.numpy as jnp
import numpy as np
from jax import lax
from jax.experimental import pallas as pl
from jax.experimental.pallas import tpu as pltpu
from jax.sharding import Mesh
from jax.sharding import PartitionSpec as P

NS, ND = 4096, 2048
PS, QD = 128, 4
ROWS_DEV, COLS_DEV = NS // PS, ND // QD
RATE_DT = 0.5
LEVELS = 7
CAP = 64
ROWS = 4096
CHUNK = 512
SEND, BACK = 6, 5
SCALE = 1.0 / math.sqrt(NS * ND)
bf16 = jnp.bfloat16
f32 = jnp.float32
NN = (((1,), (0,)), ((), ()))
NT = (((1,), (1,)), ((), ()))


def np_split(table):
    hi = table.astype(np.float32).astype(jnp.bfloat16)
    lo = (table - hi.astype(np.float64)).astype(np.float32).astype(jnp.bfloat16)
    return np.stack([hi, lo])


def np_rev(p):
    return sum(((p >> b) & 1) << (LEVELS - 1 - b) for b in range(LEVELS))


def dip_tables():
    i = np.arange(COLS_DEV)
    ang = 2 * np.pi * ((i[:, None] * i[None, :]) % ND) / ND
    return np.concatenate([np_split(np.cos(ang)), np_split(np.sin(ang))])


def strike_tables():
    p = np.arange(PS)
    k1 = np_rev(p)
    ang = 2 * np.pi * ((k1[:, None] * p[None, :]) % PS) / PS
    first = np.concatenate([np.cos(ang), -np.sin(ang)])
    r = np.arange(ROWS_DEV)
    tw = 2 * np.pi * (k1[:, None] * r[None, :]) / NS
    twiddle = np.stack([np.tile(np.cos(tw), (1, 4)), np.tile(np.sin(tw), (1, 4))]).astype(np.float32)
    small = 2 * np.pi * ((r[:, None] * r[None, :]) % ROWS_DEV) / ROWS_DEV
    cb = np.kron(np.eye(4), np.cos(small))
    sb = np.kron(np.eye(4), np.sin(small))
    second = np.block([[cb, -sb], [sb, cb]])
    second_inv = np.block([[cb, sb], [-sb, cb]])
    return np_split(first), np_split(first.T), twiddle, np_split(second), np_split(second_inv)


def memory_tables():
    out = np.zeros((8, 64, 2 * PS), np.float32)
    eye = np.eye(ROWS_DEV)
    for special in range(2):
        home = {0: 0, 1: 1, 2: 3, 3: 2} if special else {j: j for j in range(4)}
        partner = {0: 0, 3: 3, 1: 2, 2: 1} if special else {0: 3, 3: 0, 1: 2, 2: 1}
        for slab in range(4):
            own = home[slab]
            for slot, part, w_re, w_im in (
                (own, 0, 0.5, 0.5),
                (own, 1, -0.5, 0.5),
                (partner[own], 0, 0.5, -0.5),
                (partner[own], 1, 0.5, 0.5),
            ):
                rows = slice(32 * part, 32 * part + 32)
                out[4 * special + slab, rows, 32 * slot : 32 * slot + 32] += w_re * eye
                out[4 * special + slab, rows, PS + 32 * slot : PS + 32 * slot + 32] += w_im * eye
    return out.astype(jnp.bfloat16)


def dot(a, b, dims=NN):
    return lax.dot_general(a, b, dims, preferred_element_type=f32)


def split(x):
    hi = x.astype(bf16)
    return hi, (x - hi.astype(f32)).astype(bf16)


def dot_data_table(x, t_hi, t_lo):
    hi, lo = split(x)
    return dot(hi, t_hi) + (dot(lo, t_hi) + dot(hi, t_lo))


def dot_table_data(t_hi, t_lo, x):
    hi, lo = split(x)
    return dot(t_hi, hi) + (dot(t_hi, lo) + dot(t_lo, hi))


def iota(shape, dim):
    return lax.broadcasted_iota(jnp.int32, shape, dim)


def rev_bits(p):
    out = 0
    for b in range(LEVELS):
        out = out + (((p >> b) & 1) << (LEVELS - 1 - b))
    return out


def quarter(q):
    turn = (q * iota((1, COLS_DEV), 1)) & 3
    cm = jnp.where(turn == 0, 1.0, jnp.where(turn == 2, -1.0, 0.0))
    sm = jnp.where(turn == 1, 1.0, jnp.where(turn == 3, -1.0, 0.0))
    return cm, sm


def signed(freq, length):
    return jnp.where(freq >= length // 2, freq - length, freq).astype(f32) * (1.0 / length)


def slip_part(slip, rate, tables, q):
    x = slip + RATE_DT * rate
    phase = iota((ROWS_DEV, COLS_DEV), 1) & 3
    x4 = jnp.concatenate([jnp.where(phase == b, x, 0.0) for b in range(4)], axis=0)
    c = dot_data_table(x4, tables[0], tables[1])
    s = dot_data_table(x4, tables[2], tables[3])
    cm, sm = quarter(q)
    c, s = cm * c - sm * s, sm * c + cm * s
    cs = [c[32 * b : 32 * b + 32] for b in range(4)]
    ss = [s[32 * b : 32 * b + 32] for b in range(4)]
    c_even, c_odd = cs[0] + cs[2], cs[1] + cs[3]
    s_sum = (ss[0] + ss[2]) + (ss[1] + ss[3])
    h_a = (c_even + c_odd) + s_sum
    first = iota((ROWS_DEV, COLS_DEV), 1) == 0
    h_d = (c_even + jnp.where(first, -c_odd, c_odd)) - s_sum
    even = cs[0] - cs[2] + ss[3] - ss[1]
    odd = ss[0] - ss[2] + cs[1] - cs[3]
    return jnp.concatenate([h_a, even + odd, even - odd, h_d], axis=0).T


def memory_part(history, p, q):
    ks = rev_bits(p) + PS * iota((ROWS_DEV, COLS_DEV), 0)
    kd = q * COLS_DEV + iota((ROWS_DEV, COLS_DEV), 1)
    fs, fd = signed(ks, NS), signed(kd, ND)
    wave = (2.0 * math.pi) * jnp.sqrt(fs * fs + fd * fd)
    grow = jnp.exp(-0.15 * wave)
    ang = 0.9 * wave
    z_re, z_im = grow * jnp.cos(ang), grow * jnp.sin(ang)
    w_re, w_im = 0.5 * z_re, 0.5 * z_im
    m_re, m_im = w_re * history(0, 0), w_re * history(0, 1)
    for lag in range(1, 8):
        w_re, w_im = w_re * z_re - w_im * z_im, w_re * z_im + w_im * z_re
        m_re = m_re + w_re * history(lag, 0)
        m_im = m_im + w_re * history(lag, 1)
    both = jnp.concatenate([m_re, m_im], axis=0)
    zero = jnp.zeros_like(both)
    lower, upper = split(jnp.concatenate([both, zero], axis=0)), split(jnp.concatenate([zero, both], axis=0))
    row = iota((COLS_DEV, COLS_DEV), 0)
    from_col = jnp.where(q < 2, row, (COLS_DEV - row) & (COLS_DEV - 1))
    perm = (iota((COLS_DEV, COLS_DEV), 1) == from_col).astype(f32).astype(bf16)
    out = []
    for h in range(2):
        even, odd = perm[2 * h * PS : (2 * h + 1) * PS], perm[(2 * h + 1) * PS : (2 * h + 2) * PS]
        out.append((dot(even, lower[0], NT) + dot(odd, upper[0], NT)) + (dot(even, lower[1], NT) + dot(odd, upper[1], NT)))
    return out


def send_kernel(idx, slip, rate, history, tables, out):
    p, q = idx[0], idx[1]
    lines = slip_part(slip[...], rate[...], [tables[i] for i in range(4)], q)
    for i in range(4):
        out[pl.ds(i, PS, stride=SEND), :] = lines[PS * i : PS * (i + 1)]
    for h, part in enumerate(memory_part(lambda lag, part: history[lag, part], p, q)):
        out[pl.ds(4 + h, PS, stride=SEND), :] = part


def strike_part(lines, mems, first, first_t, twiddle, second, second_inv, mem_table, p, q):
    n = PS
    w = []
    for h in range(2):
        m_hi, m_lo = split(mems[h])
        for parity in range(2):
            special = jnp.where(p == 0, 4, 0) if h == 0 and parity == 0 else 0
            table = mem_table(special + q)
            zero = jnp.zeros_like(table)
            table = jnp.concatenate([zero, table] if parity else [table, zero], axis=0)
            w.append(dot(m_hi, table) + dot(m_lo, table))
    w = jnp.concatenate(w, axis=0)
    a = dot_table_data(first[0], first[1], jnp.concatenate(lines, axis=1))
    tc, ts = twiddle[0], twiddle[1]
    b = []
    for i in range(4):
        a_re, a_im = a[:n, n * i : n * (i + 1)], a[n:, n * i : n * (i + 1)]
        b.append(jnp.concatenate([a_re * tc + a_im * ts, a_im * tc - a_re * ts], axis=1))
    spec = dot_data_table(jnp.concatenate(b, axis=0), second[0], second[1])
    lane = iota((n, n), 1)
    fs = signed(rev_bits(iota((n, n), 0)) + PS * (lane & 31), NS)
    fs = fs * fs
    slot = lane >> 5
    factor = []
    for i in range(4):
        ell = p + PS * i
        kd = jnp.where((slot == 1) | (slot == 2), COLS_DEV + ell, ell)
        kd = jnp.where((slot == 3) & (ell == 0), 2 * COLS_DEV, kd)
        fd = kd.astype(f32) * (1.0 / ND)
        wave = (2.0 * math.pi) * jnp.sqrt(fs + fd * fd)
        wave = (-0.5 * SCALE) * wave
        factor.append(jnp.concatenate([wave, wave], axis=1))
    g = jnp.concatenate(factor, axis=0) * (SCALE * spec - w)
    b = dot_data_table(g, second_inv[0], second_inv[1])
    turned = []
    for i in range(4):
        b_re, b_im = b[n * i : n * (i + 1), :n], b[n * i : n * (i + 1), n:]
        turned.append(jnp.concatenate([b_re * tc - b_im * ts, b_re * ts + b_im * tc], axis=0))
    return dot_table_data(first_t[0], first_t[1], jnp.concatenate(turned, axis=1))


def strike_kernel(idx, recv, outbox, first, first_t, twiddle, second, second_inv, mem_table, out):
    t = strike_part(
        [recv[pl.ds(i, PS, stride=SEND), :] for i in range(4)],
        [recv[pl.ds(4 + h, PS, stride=SEND), :] for h in range(2)],
        first,
        first_t,
        twiddle,
        second,
        second_inv,
        lambda i: mem_table[i],
        idx[0],
        idx[1],
    )
    for i in range(4):
        out[pl.ds(i, PS, stride=BACK), :] = t[:, PS * i : PS * (i + 1)]
    out[pl.ds(4, PS, stride=BACK), :] = outbox[...]


def route_part(dest, node, value, count):
    dest = [dest[:, CHUNK * i : CHUNK * (i + 1)] for i in range(ROWS // CHUNK)]
    upto = (iota((CHUNK, CHUNK), 0) <= iota((CHUNK, CHUNK), 1)).astype(f32).astype(bf16)
    carry = jnp.zeros((PS, 1), f32)
    box = jnp.zeros((PS, 2 * CAP), f32)
    ranks = []
    for i in range(ROWS // CHUNK):
        cut = slice(CHUNK * i, CHUNK * (i + 1))
        named = iota((PS, CHUNK), 0) == dest[i]
        onehot = named.astype(f32).astype(bf16)
        upto_here = dot(onehot, upto) + carry
        rank = jnp.sum(jnp.where(named, upto_here, 0.0), axis=0, keepdims=True).astype(jnp.int32) - 1
        carry = upto_here[:, CHUNK - 1 : CHUNK]
        ranks.append(rank)
        live = (CHUNK * i + iota((1, CHUNK), 1)) < count
        v = jnp.where(live, value[:, cut], 0.0)
        v_hi = v.astype(bf16).astype(f32)
        v_lo = v - v_hi
        at = node[:, cut]
        n_hi = ((((at >> 7) & 3) << 5) + (at >> 9)) << 7
        n_lo = at & 127
        here = iota((CAP, CHUNK), 0) == rank
        part_1 = jnp.concatenate([jnp.where(here, v_hi, 0.0), jnp.where(here, n_hi.astype(f32), 0.0)], axis=0)
        part_2 = jnp.concatenate([jnp.where(here, v_lo, 0.0), jnp.where(here, n_lo.astype(f32), 0.0)], axis=0)
        box = box + (dot(onehot, part_1.astype(bf16), NT) + dot(onehot, part_2.astype(bf16), NT))
    return box, jnp.concatenate(ranks, axis=1)


def route_kernel(count, dest, node, value, out, rank):
    out[...], rank[...] = route_part(dest[...], node[...], value[...], count[0, 0])


def dip_inverse_part(recv, tables):
    t = recv.T
    a, b, c, d = [t[32 * j : 32 * j + 32] for j in range(4)]
    s1, d1, s2, d2 = a + d, a - d, b + c, b - c
    fix = jnp.where(iota((ROWS_DEV, COLS_DEV), 1) == 0, 2.0 * d, 0.0)
    even = jnp.concatenate([s1 + s2, s1 + d2 - fix, s1 - s2, s1 - d2 - fix], axis=0)
    odd = jnp.concatenate([d1 + d2, d1 - s2, d1 - d2, d1 + s2], axis=0)
    turns = [quarter(qd) for qd in range(QD)]
    evens = jnp.concatenate([cm * even + sm * odd for cm, sm in turns], axis=0)
    odds = jnp.concatenate([cm * odd - sm * even for cm, sm in turns], axis=0)
    f = dot_data_table(evens, tables[0], tables[1]) + dot_data_table(odds, tables[2], tables[3])
    phase = iota((ROWS_DEV, COLS_DEV), 1) & 3
    out = []
    for qd in range(QD):
        g = [jnp.where(phase == i, f[PS * qd + 32 * i : PS * qd + 32 * i + 32], 0.0) for i in range(4)]
        out.append((g[0] + g[1]) + (g[2] + g[3]))
    return out


def dip_kernel(recv, tables, out):
    lines = jnp.concatenate([recv[pl.ds(i, PS, stride=BACK), :] for i in range(4)], axis=0)
    for qd, share in enumerate(dip_inverse_part(lines, [tables[i] for i in range(4)])):
        out[qd] = share


def unpack_rows(fe, roll):
    top, bot = fe[0:CAP], fe[CAP:PS]
    left = iota((CAP, PS), 1) < CAP
    value = jnp.where(left, top, roll(bot))
    node = jnp.where(left, roll(top), bot).astype(jnp.int32)
    return value, node >> 7, node & 127


def lanes_of(x, group):
    return jnp.concatenate([x[4 * group + i : 4 * group + i + 1] for i in range(4)], axis=1)


def column_onehot(lo):
    return (iota((PS, CHUNK), 0) == lo).astype(f32).astype(bf16)


def traction_step(value, hi, onehot):
    named = iota((PS, CHUNK), 0) == hi
    v_hi = value.astype(bf16).astype(f32)
    rows = jnp.concatenate([jnp.where(named, v_hi, 0.0), jnp.where(named, value - v_hi, 0.0)], axis=0).astype(bf16)
    return dot(rows, onehot, NT)


def sample_step(rate_parts, hi, onehot):
    got = dot(rate_parts, jnp.concatenate([onehot, onehot], axis=0))
    return jnp.sum(jnp.where(iota((PS, CHUNK), 0) == hi, got, 0.0), axis=0, keepdims=True)


def roll_half(x):
    return pltpu.roll(x, CAP, 1)


def traction_kernel(recv, traction, onehots, spots):
    value, hi, lo = unpack_rows(recv[pl.ds(4, PS, stride=BACK), :], roll_half)
    spots[...] = hi
    acc = jnp.zeros((2 * PS, PS), f32)
    for g in range(CAP // 4):
        onehot = column_onehot(lanes_of(lo, g))
        onehots[g] = onehot
        acc = acc + traction_step(lanes_of(value, g), lanes_of(hi, g), onehot)
    acc = acc[:PS] + acc[PS:]
    traction[...] = jnp.concatenate([acc[32 * i : 32 * i + 32] for i in range(4)], axis=1)


def owner_kernel(shares, traction, onehots, spots, slip, rate, prestress, normal, flag, new_rate, stress, sampled):
    f = (shares[0] + shares[1]) + (shares[2] + shares[3])
    slip_new = slip[...] + RATE_DT * rate[...]
    total = prestress[...] + f + traction[...]
    strength = normal[...] * (0.6 - (0.6 - 0.4) * jnp.minimum(slip_new, 1.0))
    fresh = jnp.where(flag[...] == 1, jnp.maximum(total - strength, 0.0) * 2.0, 0.0)
    stress[...] = total
    new_rate[...] = fresh
    stacked = jnp.concatenate([fresh[:, PS * i : PS * (i + 1)] for i in range(4)], axis=0)
    parts = jnp.concatenate(split(stacked), axis=1)
    hi = spots[...]
    for g in range(CAP // 4):
        got = sample_step(parts, lanes_of(hi, g), onehots[g])
        for i in range(4):
            sampled[4 * g + i : 4 * g + i + 1, :] = got[:, PS * i : PS * (i + 1)]
    sampled[CAP:PS, :] = roll_half(sampled[0:CAP, :])


def return_part(got, dest, rank, count):
    parts = jnp.concatenate(split(got.T[:CAP]), axis=1)
    out = []
    for i in range(ROWS // CHUNK):
        cut = slice(CHUNK * i, CHUNK * (i + 1))
        onehot = (iota((PS, CHUNK), 0) == dest[:, cut]).astype(f32).astype(bf16)
        here = dot(parts, jnp.concatenate([onehot, onehot], axis=0))
        here = jnp.sum(jnp.where(iota((CAP, CHUNK), 0) == rank[:, cut], here, 0.0), axis=0, keepdims=True)
        live = (CHUNK * i + iota((1, CHUNK), 1)) < count
        out.append(jnp.where(live, here, 0.0))
    return jnp.concatenate(out, axis=1)


def return_kernel(count, got, dest, rank, out):
    out[...] = return_part(got[...], dest[...], rank[...], count[0, 0])


STRIKE = ("z", "y", "c")


def call(kernel, out_shape, smem, vmem, name):
    specs = [pl.BlockSpec(memory_space=pltpu.SMEM)] * smem + [pl.BlockSpec(memory_space=pltpu.VMEM)] * vmem
    outs = jax.tree.map(lambda _: pl.BlockSpec(memory_space=pltpu.VMEM), out_shape)
    return pl.pallas_call(kernel, out_shape=out_shape, in_specs=specs, out_specs=outs, name=name)


def sds(shape, dtype=f32):
    return jax.ShapeDtypeStruct(shape, dtype)


def over_strike(x, width):
    unit = 2 if width % 2 == 0 else 1
    return lax.all_to_all(x.reshape(PS * width // unit, unit, PS), STRIKE, 0, 0, tiled=True).reshape(PS * width, PS)


def body(slip, rate, prestress, normal_stress, history, fric_flag, row_dest, row_node, fe_traction, fe_count):
    p = lax.axis_index(STRIKE).astype(jnp.int32)
    q = lax.axis_index("dip").astype(jnp.int32)
    idx = jnp.stack([p, q])
    tables = jnp.asarray(dip_tables())
    strike = [jnp.asarray(t) for t in strike_tables()] + [jnp.asarray(memory_tables())]

    sent = call(send_kernel, sds((PS * SEND, PS)), 1, 4, "send")(idx, slip, rate, history, tables)
    recv = over_strike(sent, SEND)
    dest = row_dest.reshape(1, ROWS)
    box, rank = call(route_kernel, (sds((PS, PS)), sds((1, ROWS), jnp.int32)), 1, 3, "route")(
        fe_count, dest, row_node, fe_traction
    )
    sent = call(strike_kernel, sds((PS * BACK, PS)), 1, 8, "strike")(idx, recv, box, *strike)
    recv = over_strike(sent, BACK)
    shares = call(dip_kernel, sds((QD, ROWS_DEV, COLS_DEV)), 0, 2, "dip")(recv, tables)
    shares = lax.all_to_all(shares, "dip", 0, 0, tiled=True)
    traction, onehots, spots = call(
        traction_kernel,
        (sds((ROWS_DEV, COLS_DEV)), sds((CAP // 4, PS, CHUNK), bf16), sds((CAP, PS), jnp.int32)),
        0,
        1,
        "traction",
    )(recv)
    new_rate, stress, sampled = call(
        owner_kernel, (sds((ROWS_DEV, COLS_DEV)), sds((ROWS_DEV, COLS_DEV)), sds((PS, PS))), 0, 9, "owner"
    )(shares, traction, onehots, spots, slip, rate, prestress, normal_stress, fric_flag)
    got = over_strike(sampled, 1)
    fe_rate = call(return_kernel, sds((1, ROWS)), 1, 3, "back")(fe_count, got, dest, rank)
    return new_rate, stress, fe_rate


def solution(mesh):
    fine = Mesh(mesh.devices.reshape(8, 8, 2, 4), ("z", "y", "c", "dip"))
    field = P(STRIKE, "dip")
    rows = P("dip", STRIKE)
    in_specs = (field, field, field, field, P(None, None, STRIKE, "dip"), field, P("dip", STRIKE, None), rows, rows, rows)
    return jax.shard_map(body, mesh=fine, in_specs=in_specs, out_specs=(field, field, rows), check_vma=False)
```

```python
import math

import jax
import jax.numpy as jnp
import numpy as np
from jax import lax
from jax.experimental import pallas as pl
from jax.experimental.pallas import tpu as pltpu
from jax.sharding import Mesh
from jax.sharding import PartitionSpec as P

NS, ND = 4096, 2048
PS, QD = 128, 4
ROWS_DEV, COLS_DEV = NS // PS, ND // QD
RATE_DT = 0.5
LEVELS = 7
CAP = 64
ROWS = 4096
CHUNK = 512
VMEM_LIMIT = 24 << 20
STRIKE = ("z", "y", "c")
SEND, BACK = 6, 5
SCALE = 1.0 / math.sqrt(NS * ND)
bf16 = jnp.bfloat16
f32 = jnp.float32
NN = (((1,), (0,)), ((), ()))
NT = (((1,), (1,)), ((), ()))


def np_split(table):
    hi = table.astype(np.float32).astype(jnp.bfloat16)
    lo = (table - hi.astype(np.float64)).astype(np.float32).astype(jnp.bfloat16)
    return np.stack([hi, lo])


def np_rev(p):
    return sum(((p >> b) & 1) << (LEVELS - 1 - b) for b in range(LEVELS))


def dip_tables():
    ell = np.arange(COLS_DEV)
    ang = 2 * np.pi * ((np.arange(COLS_DEV // 4)[:, None] * ell[None, :]) % COLS_DEV) / COLS_DEV
    b = np.tile(np.arange(4), QD)[:, None]
    q = np.repeat(np.arange(QD), 4)[:, None]
    turn = 2 * np.pi * ((ell * b + COLS_DEV * q * ell) % ND) / ND
    tables = np.concatenate([np_split(np.cos(ang)), np_split(np.sin(ang))])
    return tables, np.stack([np.cos(turn), np.sin(turn)]).astype(np.float32)


def strike_tables():
    p = np.arange(PS)
    k1 = np_rev(p)
    ang = 2 * np.pi * ((k1[:, None] * p[None, :]) % PS) / PS
    first = np.concatenate([np.cos(ang), -np.sin(ang)])
    r = np.arange(ROWS_DEV)
    tw = 2 * np.pi * (k1[:, None] * r[None, :]) / NS
    twiddle = np.stack([np.tile(np.cos(tw), (1, 4)), np.tile(np.sin(tw), (1, 4))]).astype(np.float32)
    small = 2 * np.pi * ((r[:, None] * r[None, :]) % ROWS_DEV) / ROWS_DEV
    cb = np.kron(np.eye(4), np.cos(small))
    sb = np.kron(np.eye(4), np.sin(small))
    second = np.block([[cb, -sb], [sb, cb]])
    second_inv = np.block([[cb, sb], [-sb, cb]])
    return np_split(first), np_split(first.T), twiddle, np_split(second), np_split(second_inv)


def memory_tables():
    out = np.zeros((8, 64, 2 * PS), np.float32)
    eye = np.eye(ROWS_DEV)
    for special in range(2):
        home = {0: 0, 1: 1, 2: 3, 3: 2} if special else {j: j for j in range(4)}
        partner = {0: 0, 3: 3, 1: 2, 2: 1} if special else {0: 3, 3: 0, 1: 2, 2: 1}
        for slab in range(4):
            own = home[slab]
            for slot, part, w_re, w_im in (
                (own, 0, 0.5, 0.5),
                (own, 1, -0.5, 0.5),
                (partner[own], 0, 0.5, -0.5),
                (partner[own], 1, 0.5, 0.5),
            ):
                rows = slice(32 * part, 32 * part + 32)
                out[4 * special + slab, rows, 32 * slot : 32 * slot + 32] += w_re * eye
                out[4 * special + slab, rows, PS + 32 * slot : PS + 32 * slot + 32] += w_im * eye
    return out.astype(jnp.bfloat16)


def dot(a, b, dims=NN):
    return lax.dot_general(a, b, dims, preferred_element_type=f32)


def split(x):
    hi = x.astype(bf16)
    return hi, (x - hi.astype(f32)).astype(bf16)


def dot_data_table(x, t_hi, t_lo):
    hi, lo = split(x)
    return dot(hi, t_hi) + (dot(lo, t_hi) + dot(hi, t_lo))


def dot_table_data(t_hi, t_lo, x):
    hi, lo = split(x)
    return dot(t_hi, hi) + (dot(t_hi, lo) + dot(t_lo, hi))


def iota(shape, dim):
    return lax.broadcasted_iota(jnp.int32, shape, dim)


def position():
    return lax.axis_index(STRIKE), lax.axis_index("dip")


def rev_bits(p):
    out = 0
    for b in range(LEVELS):
        out = out + (((p >> b) & 1) << (LEVELS - 1 - b))
    return out


def turn_rows(turns, q):
    return [(turns(0, 4 * q + b), turns(1, 4 * q + b)) for b in range(4)]


def interleave(dims):
    pos = iota((COLS_DEV, COLS_DEV), dims)
    return (iota((COLS_DEV, COLS_DEV), 1 - dims) == 4 * (pos & (PS - 1)) + (pos >> 7)).astype(f32).astype(bf16)


def by_class(x):
    return jnp.concatenate([x[:, PS * b : PS * (b + 1)] for b in range(4)], axis=0)


def signed(freq, length):
    return jnp.where(freq >= length // 2, freq - length, freq).astype(f32) * (1.0 / length)


def slip_part(slip, rate, tables, turns, q):
    x = slip + RATE_DT * rate
    parts = dot(jnp.concatenate(split(x), axis=0), interleave(1)).astype(bf16)
    hi, lo = by_class(parts[:ROWS_DEV]), by_class(parts[ROWS_DEV:])
    c = dot(hi, tables[0]) + (dot(lo, tables[0]) + dot(hi, tables[1]))
    s = dot(hi, tables[2]) + (dot(lo, tables[2]) + dot(hi, tables[3]))
    cs, ss = [], []
    for b, (ct, st) in enumerate(turn_rows(turns, q)):
        c_b, s_b = c[32 * b : 32 * b + 32], s[32 * b : 32 * b + 32]
        cs.append(ct * c_b - st * s_b)
        ss.append(st * c_b + ct * s_b)
    c_even, c_odd = cs[0] + cs[2], cs[1] + cs[3]
    s_sum = (ss[0] + ss[2]) + (ss[1] + ss[3])
    h_a = (c_even + c_odd) + s_sum
    first = iota((ROWS_DEV, COLS_DEV), 1) == 0
    h_d = (c_even + jnp.where(first, -c_odd, c_odd)) - s_sum
    even = cs[0] - cs[2] + ss[3] - ss[1]
    odd = ss[0] - ss[2] + cs[1] - cs[3]
    return jnp.concatenate([h_a, even + odd, even - odd, h_d], axis=0).T


def memory_part(history, p, q):
    ks = rev_bits(p) + PS * iota((ROWS_DEV, COLS_DEV), 0)
    kd = q * COLS_DEV + iota((ROWS_DEV, COLS_DEV), 1)
    fs, fd = signed(ks, NS), signed(kd, ND)
    wave = (2.0 * math.pi) * jnp.sqrt(fs * fs + fd * fd)
    grow = jnp.exp(-0.15 * wave)
    ang = 0.9 * wave
    z_re, z_im = grow * jnp.cos(ang), grow * jnp.sin(ang)
    w_re, w_im = 0.5 * z_re, 0.5 * z_im
    m_re, m_im = w_re * history(0, 0), w_re * history(0, 1)
    for lag in range(1, 8):
        w_re, w_im = w_re * z_re - w_im * z_im, w_re * z_im + w_im * z_re
        m_re = m_re + w_re * history(lag, 0)
        m_im = m_im + w_re * history(lag, 1)
    both = jnp.concatenate([m_re, m_im], axis=0)
    zero = jnp.zeros_like(both)
    lower, upper = split(jnp.concatenate([both, zero], axis=0)), split(jnp.concatenate([zero, both], axis=0))
    row = iota((COLS_DEV, COLS_DEV), 0)
    from_col = jnp.where(q < 2, row, (COLS_DEV - row) & (COLS_DEV - 1))
    perm = (iota((COLS_DEV, COLS_DEV), 1) == from_col).astype(f32).astype(bf16)
    out = []
    for h in range(2):
        even, odd = perm[2 * h * PS : (2 * h + 1) * PS], perm[(2 * h + 1) * PS : (2 * h + 2) * PS]
        out.append((dot(even, lower[0], NT) + dot(odd, upper[0], NT)) + (dot(even, lower[1], NT) + dot(odd, upper[1], NT)))
    return out


def send_kernel(slip_in, rate_in, history_in, tables_in, turns_in, out, slip, rate, history, tables, turns, sems):
    p, q = position()
    lags = history.shape[0]
    lag_copies = [pltpu.make_async_copy(history_in.at[i], history.at[i], sems.at[i]) for i in range(lags)]
    pairs = ((slip_in, slip), (rate_in, rate), (tables_in, tables), (turns_in, turns))
    copies = [pltpu.make_async_copy(src, dst, sems.at[lags + i]) for i, (src, dst) in enumerate(pairs)]
    for copy in lag_copies + copies:
        copy.start()

    def read(lag, part):
        if part == 0:
            lag_copies[lag].wait()
        return history[lag, part]

    for h, part in enumerate(memory_part(read, p, q)):
        out[pl.ds(4 + h, PS, stride=SEND), :] = part
    for copy in copies:
        copy.wait()
    lines = slip_part(slip[...], rate[...], tables, lambda i, row: turns[i, pl.ds(row, 1), :], q)
    for i in range(4):
        out[pl.ds(i, PS, stride=SEND), :] = lines[PS * i : PS * (i + 1)]


def strike_part(lines, mems, first, first_t, twiddle, second, second_inv, mem_table, p, q):
    n = PS
    w = []
    for h in range(2):
        m_hi, m_lo = split(mems[h])
        for parity in range(2):
            special = jnp.where(p == 0, 4, 0) if h == 0 and parity == 0 else 0
            table = mem_table(special + q)
            zero = jnp.zeros_like(table)
            table = jnp.concatenate([zero, table] if parity else [table, zero], axis=0)
            w.append(dot(m_hi, table) + dot(m_lo, table))
    w = jnp.concatenate(w, axis=0)
    a = dot_table_data(first[0], first[1], jnp.concatenate(lines, axis=1))
    tc, ts = twiddle[0], twiddle[1]
    b = []
    for i in range(4):
        a_re, a_im = a[:n, n * i : n * (i + 1)], a[n:, n * i : n * (i + 1)]
        b.append(jnp.concatenate([a_re * tc + a_im * ts, a_im * tc - a_re * ts], axis=1))
    spec = dot_data_table(jnp.concatenate(b, axis=0), second[0], second[1])
    lane = iota((n, n), 1)
    fs = signed(rev_bits(iota((n, n), 0)) + PS * (lane & 31), NS)
    fs = fs * fs
    slot = lane >> 5
    factor = []
    for i in range(4):
        ell = p + PS * i
        kd = jnp.where((slot == 1) | (slot == 2), COLS_DEV + ell, ell)
        kd = jnp.where((slot == 3) & (ell == 0), 2 * COLS_DEV, kd)
        fd = kd.astype(f32) * (1.0 / ND)
        wave = (2.0 * math.pi) * jnp.sqrt(fs + fd * fd)
        wave = (-0.5 * SCALE) * wave
        factor.append(jnp.concatenate([wave, wave], axis=1))
    g = jnp.concatenate(factor, axis=0) * (SCALE * spec - w)
    b = dot_data_table(g, second_inv[0], second_inv[1])
    turned = []
    for i in range(4):
        b_re, b_im = b[n * i : n * (i + 1), :n], b[n * i : n * (i + 1), n:]
        turned.append(jnp.concatenate([b_re * tc - b_im * ts, b_re * ts + b_im * tc], axis=0))
    return dot_table_data(first_t[0], first_t[1], jnp.concatenate(turned, axis=1))


def strike_kernel(recv, outbox, first, first_t, twiddle, second, second_inv, mem_table, out):
    t = strike_part(
        [recv[pl.ds(i, PS, stride=SEND), :] for i in range(4)],
        [recv[pl.ds(4 + h, PS, stride=SEND), :] for h in range(2)],
        first,
        first_t,
        twiddle,
        second,
        second_inv,
        lambda i: mem_table[i],
        *position(),
    )
    for i in range(4):
        out[pl.ds(i, PS, stride=BACK), :] = t[:, PS * i : PS * (i + 1)]
    out[pl.ds(4, PS, stride=BACK), :] = outbox[...]


def route_part(dest, node, value, count):
    dest = [dest[:, CHUNK * i : CHUNK * (i + 1)] for i in range(ROWS // CHUNK)]
    upto = (iota((CHUNK, CHUNK), 0) <= iota((CHUNK, CHUNK), 1)).astype(f32).astype(bf16)
    carry = jnp.zeros((PS, 1), f32)
    box = jnp.zeros((PS, 2 * CAP), f32)
    ranks = []
    for i in range(ROWS // CHUNK):
        cut = slice(CHUNK * i, CHUNK * (i + 1))
        named = iota((PS, CHUNK), 0) == dest[i]
        onehot = named.astype(f32).astype(bf16)
        upto_here = dot(onehot, upto) + carry
        rank = jnp.sum(jnp.where(named, upto_here, 0.0), axis=0, keepdims=True).astype(jnp.int32) - 1
        carry = upto_here[:, CHUNK - 1 : CHUNK]
        ranks.append(rank)
        live = (CHUNK * i + iota((1, CHUNK), 1)) < count
        v = jnp.where(live, value[:, cut], 0.0)
        v_hi = v.astype(bf16).astype(f32)
        v_lo = v - v_hi
        at = node[:, cut]
        n_hi = ((((at >> 7) & 3) << 5) + (at >> 9)) << 7
        n_lo = at & 127
        here = iota((CAP, CHUNK), 0) == rank
        part_1 = jnp.concatenate([jnp.where(here, v_hi, 0.0), jnp.where(here, n_hi.astype(f32), 0.0)], axis=0)
        part_2 = jnp.concatenate([jnp.where(here, v_lo, 0.0), jnp.where(here, n_lo.astype(f32), 0.0)], axis=0)
        box = box + (dot(onehot, part_1.astype(bf16), NT) + dot(onehot, part_2.astype(bf16), NT))
    return box, jnp.concatenate(ranks, axis=1)


def route_kernel(count, dest, node, value, out, rank):
    out[...], rank[...] = route_part(dest[...], node[...], value[...], count[0, 0])


def dip_inverse_part(recv, tables, turns):
    t = recv.T
    a, b, c, d = [t[32 * j : 32 * j + 32] for j in range(4)]
    s1, d1, s2, d2 = a + d, a - d, b + c, b - c
    fix = jnp.where(iota((ROWS_DEV, COLS_DEV), 1) == 0, 2.0 * d, 0.0)
    even = [s1 + s2, s1 + d2 - fix, s1 - s2, s1 - d2 - fix]
    odd = [d1 + d2, d1 - s2, d1 - d2, d1 + s2]
    evens, odds = [], []
    for qd in range(QD):
        for i, (ct, st) in enumerate(turn_rows(turns, qd)):
            evens.append(ct * even[i] + st * odd[i])
            odds.append(ct * odd[i] - st * even[i])
    f = 0.0
    for x, k in ((evens, 0), (odds, 2)):
        hi, lo = split(jnp.concatenate(x, axis=0))
        f = f + (dot(hi, tables[k], NT) + (dot(lo, tables[k], NT) + dot(hi, tables[k + 1], NT)))
    rows = 32
    f = [[f[rows * (4 * qd + i) : rows * (4 * qd + i + 1)] for i in range(4)] for qd in range(QD)]
    f = jnp.concatenate([jnp.concatenate(x, axis=1) for x in f], axis=0)
    hi, lo = split(f)
    back = interleave(0)
    f = dot(hi, back) + dot(lo, back)
    return [f[rows * qd : rows * (qd + 1)] for qd in range(QD)]


def dip_kernel(recv, tables, turns, out):
    lines = jnp.concatenate([recv[pl.ds(i, PS, stride=BACK), :] for i in range(4)], axis=0)
    shares = dip_inverse_part(lines, tables, lambda i, row: turns[i, row : row + 1, :])
    for qd, share in enumerate(shares):
        out[qd] = share


def unpack_rows(fe, roll):
    top, bot = fe[0:CAP], fe[CAP:PS]
    left = iota((CAP, PS), 1) < CAP
    value = jnp.where(left, top, roll(bot))
    node = jnp.where(left, roll(top), bot).astype(jnp.int32)
    return value, node >> 7, node & 127


def lanes_of(x, group):
    return jnp.concatenate([x[4 * group + i : 4 * group + i + 1] for i in range(4)], axis=1)


def column_onehot(lo):
    return (iota((PS, CHUNK), 0) == lo).astype(f32).astype(bf16)


def traction_step(value, hi, onehot):
    named = iota((PS, CHUNK), 0) == hi
    v_hi = value.astype(bf16).astype(f32)
    rows = jnp.concatenate([jnp.where(named, v_hi, 0.0), jnp.where(named, value - v_hi, 0.0)], axis=0).astype(bf16)
    return dot(rows, onehot, NT)


def sample_step(rate_parts, hi, onehot):
    got = dot(rate_parts, jnp.concatenate([onehot, onehot], axis=0))
    return jnp.sum(jnp.where(iota((PS, CHUNK), 0) == hi, got, 0.0), axis=0, keepdims=True)


def roll_half(x):
    return pltpu.roll(x, CAP, 1)


def traction_kernel(recv, traction, spots):
    value, hi, lo = unpack_rows(recv[pl.ds(4, PS, stride=BACK), :], roll_half)
    spots[0], spots[1] = hi, lo
    acc = jnp.zeros((2 * PS, PS), f32)
    for g in range(CAP // 4):
        onehot = column_onehot(lanes_of(lo, g))
        acc = acc + traction_step(lanes_of(value, g), lanes_of(hi, g), onehot)
    acc = acc[:PS] + acc[PS:]
    traction[...] = jnp.concatenate([acc[32 * i : 32 * i + 32] for i in range(4)], axis=1)


def owner_kernel(
    shares, traction, spots, slip, rate, prestress, normal, flag, new_rate_out, stress_out, sampled, new_rate, stress, sems
):
    f = (shares[0] + shares[1]) + (shares[2] + shares[3])
    slip_new = slip[...] + RATE_DT * rate[...]
    total = prestress[...] + f + traction[...]
    strength = normal[...] * (0.6 - (0.6 - 0.4) * jnp.minimum(slip_new, 1.0))
    fresh = jnp.where(flag[...] == 1, jnp.maximum(total - strength, 0.0) * 2.0, 0.0)
    stress[...] = total
    new_rate[...] = fresh
    copies = [
        pltpu.make_async_copy(new_rate, new_rate_out, sems.at[0]),
        pltpu.make_async_copy(stress, stress_out, sems.at[1]),
    ]
    for copy in copies:
        copy.start()
    stacked = jnp.concatenate([fresh[:, PS * i : PS * (i + 1)] for i in range(4)], axis=0)
    parts = jnp.concatenate(split(stacked), axis=1)
    hi, lo = spots[0], spots[1]
    for g in range(CAP // 4):
        got = sample_step(parts, lanes_of(hi, g), column_onehot(lanes_of(lo, g)))
        for i in range(4):
            sampled[4 * g + i : 4 * g + i + 1, :] = got[:, PS * i : PS * (i + 1)]
    sampled[CAP:PS, :] = roll_half(sampled[0:CAP, :])
    for copy in copies:
        copy.wait()


def return_part(got, dest, rank, count):
    parts = jnp.concatenate(split(got.T[:CAP]), axis=1)
    out = []
    for i in range(ROWS // CHUNK):
        cut = slice(CHUNK * i, CHUNK * (i + 1))
        onehot = (iota((PS, CHUNK), 0) == dest[:, cut]).astype(f32).astype(bf16)
        here = dot(parts, jnp.concatenate([onehot, onehot], axis=0))
        here = jnp.sum(jnp.where(iota((CAP, CHUNK), 0) == rank[:, cut], here, 0.0), axis=0, keepdims=True)
        live = (CHUNK * i + iota((1, CHUNK), 1)) < count
        out.append(jnp.where(live, here, 0.0))
    return jnp.concatenate(out, axis=1)


def return_kernel(count, got, rank, dest, out):
    out[...] = return_part(got[...], dest[...], rank[...], count[0, 0])


def call(kernel, out_shape, operands, name, scalars=(), args=(), far=(), far_outs=0, scratch=()):
    spec = pl.BlockSpec(memory_space=pltpu.VMEM)
    hbm = pl.BlockSpec(memory_space=pltpu.HBM)
    in_specs = [pl.BlockSpec(memory_space=pltpu.SMEM)] * len(scalars) + [hbm] * len(far) + [spec] * (len(operands) + len(args))
    outs = tuple(hbm if i < far_outs else spec for i in range(len(out_shape))) if isinstance(out_shape, tuple) else spec
    far = [pltpu.with_memory_space_constraint(x, pltpu.HBM) for x in far]
    operands = [pltpu.with_memory_space_constraint(x, pltpu.VMEM) for x in operands]
    return pl.pallas_call(
        kernel,
        out_shape=out_shape,
        in_specs=in_specs,
        out_specs=outs,
        name=name,
        scratch_shapes=scratch,
        compiler_params=pltpu.CompilerParams(vmem_limit_bytes=VMEM_LIMIT),
    )(*scalars, *far, *operands, *args)


def sds(shape, dtype=f32):
    return pltpu.VMEM(shape, dtype)


def over_strike(x, width):
    unit = 2 if width % 2 == 0 else 1
    return lax.all_to_all(x.reshape(PS * width // unit, unit, PS), STRIKE, 0, 0, tiled=True).reshape(PS * width, PS)


def body(slip, rate, prestress, normal_stress, history, fric_flag, row_dest, row_node, fe_traction, fe_count):
    tables, turns = [jnp.asarray(t) for t in dip_tables()]
    strike = [jnp.asarray(t) for t in strike_tables()] + [jnp.asarray(memory_tables())]
    dest = row_dest.reshape(1, ROWS)

    inputs = (slip, rate, history, tables, turns)
    scratch = [pltpu.VMEM(x.shape, x.dtype) for x in inputs] + [pltpu.SemaphoreType.DMA((history.shape[0] + 4,))]
    sent = call(send_kernel, sds((PS * SEND, PS)), (), "send", far=inputs, scratch=scratch)
    recv = over_strike(sent, SEND)
    box, rank = call(
        route_kernel, (sds((PS, PS)), sds((1, ROWS), jnp.int32)), (), "route", (fe_count,), (dest, row_node, fe_traction)
    )
    sent = call(strike_kernel, sds((PS * BACK, PS)), (recv, box), "strike", args=strike)
    recv = over_strike(sent, BACK)
    shares = call(dip_kernel, sds((QD, ROWS_DEV, COLS_DEV)), (recv,), "dip", args=(tables, turns))
    shares = lax.all_to_all(shares, "dip", 0, 0, tiled=True)
    traction, spots = call(
        traction_kernel,
        (sds((ROWS_DEV, COLS_DEV)), sds((2, CAP, PS), jnp.int32)),
        (recv,),
        "traction",
    )
    new_rate, stress, sampled = call(
        owner_kernel,
        (jax.ShapeDtypeStruct(slip.shape, f32), jax.ShapeDtypeStruct(slip.shape, f32), sds((PS, PS))),
        (shares, traction, spots),
        "owner",
        args=(slip, rate, prestress, normal_stress, fric_flag),
        far_outs=2,
        scratch=[sds(slip.shape), sds(slip.shape), pltpu.SemaphoreType.DMA((2,))],
    )
    got = over_strike(sampled, 1)
    fe_rate = call(return_kernel, jax.ShapeDtypeStruct((1, ROWS), f32), (got, rank), "back", (fe_count,), (dest,))
    return new_rate, stress, fe_rate


def solution(mesh):
    fine = Mesh(mesh.devices.reshape(8, 8, 2, 4), ("z", "y", "c", "dip"))
    field = P(STRIKE, "dip")
    rows = P("dip", STRIKE)
    in_specs = (field, field, field, field, P(None, None, STRIKE, "dip"), field, P("dip", STRIKE, None), rows, rows, rows)
    return jax.shard_map(body, mesh=fine, in_specs=in_specs, out_specs=(field, field, rows), check_vma=False)
```

```python
import math

import jax
import jax.numpy as jnp
import numpy as np
from jax import lax
from jax.experimental import pallas as pl
from jax.experimental.pallas import tpu as pltpu
from jax.sharding import Mesh
from jax.sharding import PartitionSpec as P

NS, ND = 4096, 2048
PS, QD = 128, 4
ROWS_DEV, COLS_DEV = NS // PS, ND // QD
RATE_DT = 0.5
LEVELS = 7
CAP = 64
ROWS = 4096
CHUNK = 512
VMEM_LIMIT = 24 << 20
STRIKE = ("z", "y", "c")
SEND, BACK = 4, 3
SCALE = 1.0 / math.sqrt(NS * ND)
bf16 = jnp.bfloat16
f32 = jnp.float32
NN = (((1,), (0,)), ((), ()))
NT = (((1,), (1,)), ((), ()))


def np_split(table):
    hi = table.astype(np.float32).astype(jnp.bfloat16)
    lo = (table - hi.astype(np.float64)).astype(np.float32).astype(jnp.bfloat16)
    return np.stack([hi, lo])


def np_rev(p):
    return sum(((p >> b) & 1) << (LEVELS - 1 - b) for b in range(LEVELS))


def dip_tables():
    ell = np.arange(COLS_DEV)
    ang = 2 * np.pi * ((np.arange(COLS_DEV // 4)[:, None] * ell[None, :]) % COLS_DEV) / COLS_DEV
    b = np.tile(np.arange(4), QD)[:, None]
    q = np.repeat(np.arange(QD), 4)[:, None]
    turn = 2 * np.pi * ((ell * b + COLS_DEV * q * ell) % ND) / ND
    tables = np.concatenate([np_split(np.cos(ang)), np_split(np.sin(ang))])
    return tables, np.stack([np.cos(turn), np.sin(turn)]).astype(np.float32)


def strike_tables():
    p = np.arange(PS)
    k1 = np_rev(p)
    ang = 2 * np.pi * ((k1[:, None] * p[None, :]) % PS) / PS
    first = np.concatenate([np.cos(ang), -np.sin(ang)])
    r = np.arange(ROWS_DEV)
    tw = 2 * np.pi * (k1[:, None] * r[None, :]) / NS
    twiddle = np.stack([np.tile(np.cos(tw), (1, 4)), np.tile(np.sin(tw), (1, 4))]).astype(np.float32)
    small = 2 * np.pi * ((r[:, None] * r[None, :]) % ROWS_DEV) / ROWS_DEV
    cb = np.kron(np.eye(4), np.cos(small))
    sb = np.kron(np.eye(4), np.sin(small))
    second = np.block([[cb, -sb], [sb, cb]])
    second_inv = np.block([[cb, sb], [-sb, cb]])
    return np_split(first), np_split(first.T), twiddle, np_split(second), np_split(second_inv)


def memory_tables():
    out = np.zeros((4, 2, 2, 32, 2, 2, 2, 32), np.float32)
    eye = np.eye(ROWS_DEV)
    for case in range(4):
        own = case & 1
        for parity in range(2):
            other = own if case >= 2 and parity == 0 else 1 - own
            for slot, part, w_re, w_im in ((own, 0, 0.5, 0.5), (own, 1, -0.5, 0.5), (other, 0, 0.5, -0.5), (other, 1, 0.5, 0.5)):
                out[case, parity, part, :, 0, parity, slot, :] += w_re * eye
                out[case, parity, part, :, 1, parity, slot, :] += w_im * eye
    return out.reshape(4, PS, 2 * PS).astype(jnp.bfloat16)


def dot(a, b, dims=NN):
    return lax.dot_general(a, b, dims, preferred_element_type=f32)


def split(x):
    hi = x.astype(bf16)
    return hi, (x - hi.astype(f32)).astype(bf16)


def dot_data_table(x, t_hi, t_lo):
    hi, lo = split(x)
    return dot(hi, t_hi) + (dot(lo, t_hi) + dot(hi, t_lo))


def dot_table_data(t_hi, t_lo, x):
    hi, lo = split(x)
    return dot(t_hi, hi) + (dot(t_hi, lo) + dot(t_lo, hi))


def iota(shape, dim):
    return lax.broadcasted_iota(jnp.int32, shape, dim)


def position():
    return lax.axis_index(STRIKE), lax.axis_index("dip")


def rev_bits(p):
    out = 0
    for b in range(LEVELS):
        out = out + (((p >> b) & 1) << (LEVELS - 1 - b))
    return out


def turn_rows(turns, q):
    return [(turns(0, 4 * q + b), turns(1, 4 * q + b)) for b in range(4)]


def interleave(dims):
    pos = iota((COLS_DEV, COLS_DEV), dims)
    return (iota((COLS_DEV, COLS_DEV), 1 - dims) == 4 * (pos & (PS - 1)) + (pos >> 7)).astype(f32).astype(bf16)


def by_class(x):
    return jnp.concatenate([x[:, PS * b : PS * (b + 1)] for b in range(4)], axis=0)


def signed(freq, length):
    return jnp.where(freq >= length // 2, freq - length, freq).astype(f32) * (1.0 / length)


def outer_modes(ell, q):
    return jnp.where(ell == 0, 1 - (q & 1), 1 - ((q ^ (q >> 1)) & 1)) == 1


def slip_part(own, other, tables, turns, q):
    parts = jnp.concatenate(split(own) + split(other), axis=0)
    parts = dot(parts, interleave(1)).astype(bf16)
    own_hi, own_lo, other_hi, other_lo = [by_class(parts[ROWS_DEV * i : ROWS_DEV * (i + 1)]) for i in range(4)]
    hi, lo = jnp.concatenate([own_hi, other_hi], axis=0), jnp.concatenate([own_lo, other_lo], axis=0)
    c = dot(hi, tables[0]) + (dot(lo, tables[0]) + dot(hi, tables[1]))
    s = dot(hi, tables[2]) + (dot(lo, tables[2]) + dot(hi, tables[3]))
    cs, ss = [0.0] * 4, [0.0] * 4
    for block, block_q in enumerate((q, q ^ 1)):
        for b, (ct, st) in enumerate(turn_rows(turns, block_q)):
            rows = slice(PS * block + 32 * b, PS * block + 32 * b + 32)
            cs[b] = cs[b] + (ct * c[rows] - st * s[rows])
            ss[b] = ss[b] + (st * c[rows] + ct * s[rows])
    c_even, c_odd = cs[0] + cs[2], cs[1] + cs[3]
    s_sum = (ss[0] + ss[2]) + (ss[1] + ss[3])
    ell = iota((ROWS_DEV, COLS_DEV), 1)
    h_a = (c_even + c_odd) + s_sum
    h_d = (c_even + jnp.where(ell == 0, -c_odd, c_odd)) - s_sum
    even = cs[0] - cs[2] + ss[3] - ss[1]
    odd = ss[0] - ss[2] + cs[1] - cs[3]
    outer = outer_modes(ell, q)
    both = jnp.concatenate([jnp.where(outer, h_a, even + odd), jnp.where(outer, h_d, even - odd)], axis=0)
    both = [both[:, PS * i : PS * (i + 1)] for i in range(4)]
    return [jnp.concatenate(both[2 * h : 2 * h + 2], axis=0).T for h in range(2)]


def memory_part(history, p, q):
    ks = rev_bits(p) + PS * iota((ROWS_DEV, COLS_DEV), 0)
    kd = q * COLS_DEV + iota((ROWS_DEV, COLS_DEV), 1)
    fs, fd = signed(ks, NS), signed(kd, ND)
    wave = (2.0 * math.pi) * jnp.sqrt(fs * fs + fd * fd)
    grow = jnp.exp(-0.15 * wave)
    ang = 0.9 * wave
    z_re, z_im = grow * jnp.cos(ang), grow * jnp.sin(ang)
    w_re, w_im = 0.5 * z_re, 0.5 * z_im
    m_re, m_im = w_re * history(0, 0), w_re * history(0, 1)
    for lag in range(1, 8):
        w_re, w_im = w_re * z_re - w_im * z_im, w_re * z_im + w_im * z_re
        m_re = m_re + w_re * history(lag, 0)
        m_im = m_im + w_re * history(lag, 1)
    both = jnp.concatenate([m_re, m_im], axis=0)
    zero = jnp.zeros_like(both)
    lower, upper = split(jnp.concatenate([both, zero], axis=0)), split(jnp.concatenate([zero, both], axis=0))
    row = iota((COLS_DEV, COLS_DEV), 0)
    from_col = jnp.where(q < 2, row, (COLS_DEV - row) & (COLS_DEV - 1))
    perm = (iota((COLS_DEV, COLS_DEV), 1) == from_col).astype(f32).astype(bf16)
    out = []
    for h in range(2):
        even, odd = perm[2 * h * PS : (2 * h + 1) * PS], perm[(2 * h + 1) * PS : (2 * h + 2) * PS]
        out.append((dot(even, lower[0], NT) + dot(odd, upper[0], NT)) + (dot(even, lower[1], NT) + dot(odd, upper[1], NT)))
    return out


def memory_kernel(history_in, out, history, sems):
    p, q = position()
    copies = [pltpu.make_async_copy(history_in.at[i], history.at[i], sems.at[i]) for i in range(history.shape[0])]
    for copy in copies:
        copy.start()

    def read(lag, part):
        if part == 0:
            copies[lag].wait()
        return history[lag, part]

    for h, part in enumerate(memory_part(read, p, q)):
        out[PS * h : PS * (h + 1), :] = part


def send_kernel(own, other, mem, tables, turns, out):
    q = position()[1]
    lines = slip_part(own[...], other[...], tables, lambda i, row: turns[i, pl.ds(row, 1), :], q)
    for h in range(2):
        out[pl.ds(h, PS, stride=SEND), :] = lines[h]
        out[pl.ds(2 + h, PS, stride=SEND), :] = mem[PS * h : PS * (h + 1), :]


def strike_part(lines, mems, first, first_t, twiddle, second, second_inv, mem_table, p, q):
    n = PS
    w = []
    for h in range(2):
        m_hi, m_lo = split(mems[h])
        alone = jnp.where((p == 0) & ((q & 1) == 0), 2, 0) if h == 0 else 0
        table = mem_table(alone + (q >> 1))
        w.append(dot(m_hi, table) + dot(m_lo, table))
    w = jnp.concatenate(w, axis=0)
    a = dot_table_data(first[0], first[1], jnp.concatenate(lines, axis=1))
    tc, ts = twiddle[0], twiddle[1]
    b = []
    for h in range(2):
        a_re, a_im = a[:n, n * h : n * (h + 1)], a[n:, n * h : n * (h + 1)]
        b.append(jnp.concatenate([a_re * tc + a_im * ts, a_im * tc - a_re * ts], axis=1))
    spec = dot_data_table(jnp.concatenate(b, axis=0), second[0], second[1])
    lane = iota((n, n), 1)
    fs = signed(rev_bits(iota((n, n), 0)) + PS * (lane & 31), NS)
    fs = fs * fs
    parity, slot = lane >> 6, (lane >> 5) & 1
    factor = []
    for h in range(2):
        ell = p + PS * (2 * h + parity)
        kd = jnp.where(outer_modes(ell, q), jnp.where((ell == 0) & (slot == 1), 2 * COLS_DEV, ell), COLS_DEV + ell)
        fd = kd.astype(f32) * (1.0 / ND)
        wave = (2.0 * math.pi) * jnp.sqrt(fs + fd * fd)
        wave = (-0.5 * SCALE) * wave
        factor.append(jnp.concatenate([wave, wave], axis=1))
    g = jnp.concatenate(factor, axis=0) * (SCALE * spec - w)
    b = dot_data_table(g, second_inv[0], second_inv[1])
    turned = []
    for h in range(2):
        b_re, b_im = b[n * h : n * (h + 1), :n], b[n * h : n * (h + 1), n:]
        turned.append(jnp.concatenate([b_re * tc - b_im * ts, b_re * ts + b_im * tc], axis=0))
    return dot_table_data(first_t[0], first_t[1], jnp.concatenate(turned, axis=1))


def strike_kernel(recv, outbox, first, first_t, twiddle, second, second_inv, mem_table, out):
    t = strike_part(
        [recv[pl.ds(h, PS, stride=SEND), :] for h in range(2)],
        [recv[pl.ds(2 + h, PS, stride=SEND), :] for h in range(2)],
        first,
        first_t,
        twiddle,
        second,
        second_inv,
        lambda i: mem_table[i],
        *position(),
    )
    for h in range(2):
        out[pl.ds(h, PS, stride=BACK), :] = t[:, PS * h : PS * (h + 1)]
    out[pl.ds(2, PS, stride=BACK), :] = outbox[...]


def route_part(dest, node, value, count):
    dest = [dest[:, CHUNK * i : CHUNK * (i + 1)] for i in range(ROWS // CHUNK)]
    upto = (iota((CHUNK, CHUNK), 0) <= iota((CHUNK, CHUNK), 1)).astype(f32).astype(bf16)
    carry = jnp.zeros((PS, 1), f32)
    box = jnp.zeros((PS, 2 * CAP), f32)
    ranks = []
    for i in range(ROWS // CHUNK):
        cut = slice(CHUNK * i, CHUNK * (i + 1))
        named = iota((PS, CHUNK), 0) == dest[i]
        onehot = named.astype(f32).astype(bf16)
        upto_here = dot(onehot, upto) + carry
        rank = jnp.sum(jnp.where(named, upto_here, 0.0), axis=0, keepdims=True).astype(jnp.int32) - 1
        carry = upto_here[:, CHUNK - 1 : CHUNK]
        ranks.append(rank)
        live = (CHUNK * i + iota((1, CHUNK), 1)) < count
        v = jnp.where(live, value[:, cut], 0.0)
        v_hi = v.astype(bf16).astype(f32)
        v_lo = v - v_hi
        at = node[:, cut]
        n_hi = ((((at >> 7) & 3) << 5) + (at >> 9)) << 7
        n_lo = at & 127
        here = iota((CAP, CHUNK), 0) == rank
        part_1 = jnp.concatenate([jnp.where(here, v_hi, 0.0), jnp.where(here, n_hi.astype(f32), 0.0)], axis=0)
        part_2 = jnp.concatenate([jnp.where(here, v_lo, 0.0), jnp.where(here, n_lo.astype(f32), 0.0)], axis=0)
        box = box + (dot(onehot, part_1.astype(bf16), NT) + dot(onehot, part_2.astype(bf16), NT))
    return box, jnp.concatenate(ranks, axis=1)


def route_kernel(count, dest, node, value, out, rank):
    out[...], rank[...] = route_part(dest[...], node[...], value[...], count[0, 0])


def dip_inverse_part(lines, tables, turns, q):
    lines = [x.T for x in lines]
    t0, t1 = [
        jnp.concatenate([lines[i >> 1][64 * (i & 1) + 32 * slot : 64 * (i & 1) + 32 * slot + 32] for i in range(4)], axis=1)
        for slot in range(2)
    ]
    ell = iota((ROWS_DEV, COLS_DEV), 1)
    outer = outer_modes(ell, q)
    total, diff = t0 + t1, t0 - t1
    s1, d1 = jnp.where(outer, total, 0.0), jnp.where(outer, diff, 0.0)
    s2, d2 = total - s1, diff - d1
    fix = jnp.where(outer & (ell == 0), 2.0 * t1, 0.0)
    even = [s1 + s2, s1 + d2 - fix, s1 - s2, s1 - d2 - fix]
    odd = [d1 + d2, d1 - s2, d1 - d2, d1 + s2]
    evens, odds = [], []
    for qd in range(QD):
        for i, (ct, st) in enumerate(turn_rows(turns, qd)):
            evens.append(ct * even[i] + st * odd[i])
            odds.append(ct * odd[i] - st * even[i])
    f = 0.0
    for x, k in ((evens, 0), (odds, 2)):
        hi, lo = split(jnp.concatenate(x, axis=0))
        f = f + (dot(hi, tables[k], NT) + (dot(lo, tables[k], NT) + dot(hi, tables[k + 1], NT)))
    rows = 32
    f = [[f[rows * (4 * qd + i) : rows * (4 * qd + i + 1)] for i in range(4)] for qd in range(QD)]
    f = jnp.concatenate([jnp.concatenate(x, axis=1) for x in f], axis=0)
    hi, lo = split(f)
    back = interleave(0)
    f = dot(hi, back) + dot(lo, back)
    return [f[rows * qd : rows * (qd + 1)] for qd in range(QD)]


def dip_kernel(recv, tables, turns, out):
    lines = [recv[pl.ds(h, PS, stride=BACK), :] for h in range(2)]
    shares = dip_inverse_part(lines, tables, lambda i, row: turns[i, row : row + 1, :], position()[1])
    for qd, share in enumerate(shares):
        out[qd] = share


def unpack_rows(fe, roll):
    top, bot = fe[0:CAP], fe[CAP:PS]
    left = iota((CAP, PS), 1) < CAP
    value = jnp.where(left, top, roll(bot))
    node = jnp.where(left, roll(top), bot).astype(jnp.int32)
    return value, node >> 7, node & 127


def lanes_of(x, group):
    return jnp.concatenate([x[4 * group + i : 4 * group + i + 1] for i in range(4)], axis=1)


def column_onehot(lo):
    return (iota((PS, CHUNK), 0) == lo).astype(f32).astype(bf16)


def traction_step(value, hi, onehot):
    named = iota((PS, CHUNK), 0) == hi
    v_hi = value.astype(bf16).astype(f32)
    rows = jnp.concatenate([jnp.where(named, v_hi, 0.0), jnp.where(named, value - v_hi, 0.0)], axis=0).astype(bf16)
    return dot(rows, onehot, NT)


def sample_step(rate_parts, hi, onehot):
    got = dot(rate_parts, jnp.concatenate([onehot, onehot], axis=0))
    return jnp.sum(jnp.where(iota((PS, CHUNK), 0) == hi, got, 0.0), axis=0, keepdims=True)


def roll_half(x):
    return pltpu.roll(x, CAP, 1)


def traction_kernel(recv, traction, spots):
    value, hi, lo = unpack_rows(recv[pl.ds(2, PS, stride=BACK), :], roll_half)
    spots[0], spots[1] = hi, lo
    acc = jnp.zeros((2 * PS, PS), f32)
    for g in range(CAP // 4):
        onehot = column_onehot(lanes_of(lo, g))
        acc = acc + traction_step(lanes_of(value, g), lanes_of(hi, g), onehot)
    acc = acc[:PS] + acc[PS:]
    traction[...] = jnp.concatenate([acc[32 * i : 32 * i + 32] for i in range(4)], axis=1)


def owner_kernel(
    shares, traction, spots, slip, rate, prestress, normal, flag, new_rate_out, stress_out, sampled, new_rate, stress, sems
):
    f = (shares[0] + shares[1]) + (shares[2] + shares[3])
    slip_new = slip[...] + RATE_DT * rate[...]
    total = prestress[...] + f + traction[...]
    strength = normal[...] * (0.6 - (0.6 - 0.4) * jnp.minimum(slip_new, 1.0))
    fresh = jnp.where(flag[...] == 1, jnp.maximum(total - strength, 0.0) * 2.0, 0.0)
    stress[...] = total
    new_rate[...] = fresh
    copies = [
        pltpu.make_async_copy(new_rate, new_rate_out, sems.at[0]),
        pltpu.make_async_copy(stress, stress_out, sems.at[1]),
    ]
    for copy in copies:
        copy.start()
    stacked = jnp.concatenate([fresh[:, PS * i : PS * (i + 1)] for i in range(4)], axis=0)
    parts = jnp.concatenate(split(stacked), axis=1)
    hi, lo = spots[0], spots[1]
    for g in range(CAP // 4):
        got = sample_step(parts, lanes_of(hi, g), column_onehot(lanes_of(lo, g)))
        for i in range(4):
            sampled[4 * g + i : 4 * g + i + 1, :] = got[:, PS * i : PS * (i + 1)]
    sampled[CAP:PS, :] = roll_half(sampled[0:CAP, :])
    for copy in copies:
        copy.wait()


def return_part(got, dest, rank, count):
    parts = jnp.concatenate(split(got.T[:CAP]), axis=1)
    out = []
    for i in range(ROWS // CHUNK):
        cut = slice(CHUNK * i, CHUNK * (i + 1))
        onehot = (iota((PS, CHUNK), 0) == dest[:, cut]).astype(f32).astype(bf16)
        here = dot(parts, jnp.concatenate([onehot, onehot], axis=0))
        here = jnp.sum(jnp.where(iota((CAP, CHUNK), 0) == rank[:, cut], here, 0.0), axis=0, keepdims=True)
        live = (CHUNK * i + iota((1, CHUNK), 1)) < count
        out.append(jnp.where(live, here, 0.0))
    return jnp.concatenate(out, axis=1)


def return_kernel(count, got, rank, dest, out):
    out[...] = return_part(got[...], dest[...], rank[...], count[0, 0])


def call(kernel, out_shape, operands, name, scalars=(), args=(), far=(), far_outs=0, scratch=()):
    spec = pl.BlockSpec(memory_space=pltpu.VMEM)
    hbm = pl.BlockSpec(memory_space=pltpu.HBM)
    in_specs = [pl.BlockSpec(memory_space=pltpu.SMEM)] * len(scalars) + [hbm] * len(far) + [spec] * (len(operands) + len(args))
    outs = tuple(hbm if i < far_outs else spec for i in range(len(out_shape))) if isinstance(out_shape, tuple) else spec
    far = [pltpu.with_memory_space_constraint(x, pltpu.HBM) for x in far]
    operands = [pltpu.with_memory_space_constraint(x, pltpu.VMEM) for x in operands]
    return pl.pallas_call(
        kernel,
        out_shape=out_shape,
        in_specs=in_specs,
        out_specs=outs,
        name=name,
        scratch_shapes=scratch,
        compiler_params=pltpu.CompilerParams(vmem_limit_bytes=VMEM_LIMIT),
    )(*scalars, *far, *operands, *args)


def sds(shape, dtype=f32):
    return pltpu.VMEM(shape, dtype)


def over_strike(x, width):
    unit = width if width in (1, 2, 4) else 1
    return lax.all_to_all(x.reshape(PS * width // unit, unit, PS), STRIKE, 0, 0, tiled=True).reshape(PS * width, PS)


def body(slip, rate, prestress, normal_stress, history, fric_flag, row_dest, row_node, fe_traction, fe_count):
    tables, turns = [jnp.asarray(t) for t in dip_tables()]
    strike = [jnp.asarray(t) for t in strike_tables()] + [jnp.asarray(memory_tables())]
    dest = row_dest.reshape(1, ROWS)

    slip_new = slip + RATE_DT * rate
    other = lax.ppermute(slip_new, "dip", [(i, i ^ 1) for i in range(QD)])
    mem = call(
        memory_kernel,
        sds((2 * PS, PS)),
        (),
        "memory",
        far=(history,),
        scratch=[sds(history.shape), pltpu.SemaphoreType.DMA((history.shape[0],))],
    )
    sent = call(send_kernel, sds((PS * SEND, PS)), (slip_new, other, mem), "send", args=(tables, turns))
    recv = over_strike(sent, SEND)
    box, rank = call(
        route_kernel, (sds((PS, PS)), sds((1, ROWS), jnp.int32)), (), "route", (fe_count,), (dest, row_node, fe_traction)
    )
    sent = call(strike_kernel, sds((PS * BACK, PS)), (recv, box), "strike", args=strike)
    recv = over_strike(sent, BACK)
    shares = call(dip_kernel, sds((QD, ROWS_DEV, COLS_DEV)), (recv,), "dip", args=(tables, turns))
    shares = lax.all_to_all(shares, "dip", 0, 0, tiled=True)
    traction, spots = call(
        traction_kernel,
        (sds((ROWS_DEV, COLS_DEV)), sds((2, CAP, PS), jnp.int32)),
        (recv,),
        "traction",
    )
    new_rate, stress, sampled = call(
        owner_kernel,
        (jax.ShapeDtypeStruct(slip.shape, f32), jax.ShapeDtypeStruct(slip.shape, f32), sds((PS, PS))),
        (shares, traction, spots),
        "owner",
        args=(slip, rate, prestress, normal_stress, fric_flag),
        far_outs=2,
        scratch=[sds(slip.shape), sds(slip.shape), pltpu.SemaphoreType.DMA((2,))],
    )
    got = over_strike(sampled, 1)
    fe_rate = call(return_kernel, jax.ShapeDtypeStruct((1, ROWS), f32), (got, rank), "back", (fe_count,), (dest,))
    return new_rate, stress, fe_rate


def solution(mesh):
    fine = Mesh(mesh.devices.reshape(8, 8, 2, 4), ("z", "y", "c", "dip"))
    field = P(STRIKE, "dip")
    rows = P("dip", STRIKE)
    in_specs = (field, field, field, field, P(None, None, STRIKE, "dip"), field, P("dip", STRIKE, None), rows, rows, rows)
    return jax.shard_map(body, mesh=fine, in_specs=in_specs, out_specs=(field, field, rows), check_vma=False)
```

```python
import math

import jax
import jax.numpy as jnp
import numpy as np
from jax import lax
from jax.experimental import pallas as pl
from jax.experimental.pallas import tpu as pltpu
from jax.sharding import Mesh
from jax.sharding import PartitionSpec as P

NS, ND = 4096, 2048
PS, QD = 128, 4
ROWS_DEV, COLS_DEV = NS // PS, ND // QD
RATE_DT = 0.5
LEVELS = 7
CAP = 64
ROWS = 4096
CHUNK = 512
VMEM_LIMIT = 24 << 20
STRIKE = ("z", "y", "c")
SEND, BACK = 6, 5
SCALE = 1.0 / math.sqrt(NS * ND)
bf16 = jnp.bfloat16
f32 = jnp.float32
NN = (((1,), (0,)), ((), ()))
NT = (((1,), (1,)), ((), ()))


def np_split(table):
    hi = table.astype(np.float32).astype(jnp.bfloat16)
    lo = (table - hi.astype(np.float64)).astype(np.float32).astype(jnp.bfloat16)
    return np.stack([hi, lo])


def np_rev(p):
    return sum(((p >> b) & 1) << (LEVELS - 1 - b) for b in range(LEVELS))


def dip_tables():
    ell = np.arange(COLS_DEV)
    ang = 2 * np.pi * ((np.arange(COLS_DEV // 4)[:, None] * ell[None, :]) % COLS_DEV) / COLS_DEV
    b = np.tile(np.arange(4), QD)[:, None]
    q = np.repeat(np.arange(QD), 4)[:, None]
    turn = 2 * np.pi * ((ell * b + COLS_DEV * q * ell) % ND) / ND
    tables = np.concatenate([np_split(np.cos(ang)), np_split(np.sin(ang))])
    return tables, np.stack([np.cos(turn), np.sin(turn)]).astype(np.float32)


def strike_tables():
    p = np.arange(PS)
    k1 = np_rev(p)
    ang = 2 * np.pi * ((k1[:, None] * p[None, :]) % PS) / PS
    first = np.concatenate([np.cos(ang), -np.sin(ang)])
    r = np.arange(ROWS_DEV)
    tw = 2 * np.pi * (k1[:, None] * r[None, :]) / NS
    twiddle = np.stack([np.tile(np.cos(tw), (1, 4)), np.tile(np.sin(tw), (1, 4))]).astype(np.float32)
    small = 2 * np.pi * ((r[:, None] * r[None, :]) % ROWS_DEV) / ROWS_DEV
    cb = np.kron(np.eye(4), np.cos(small))
    sb = np.kron(np.eye(4), np.sin(small))
    second = np.block([[cb, -sb], [sb, cb]])
    second_inv = np.block([[cb, sb], [-sb, cb]])
    return np_split(first), np_split(first.T), twiddle, np_split(second), np_split(second_inv)


def memory_tables():
    out = np.zeros((8, 64, 2 * PS), np.float32)
    eye = np.eye(ROWS_DEV)
    for special in range(2):
        home = {0: 0, 1: 1, 2: 3, 3: 2} if special else {j: j for j in range(4)}
        partner = {0: 0, 3: 3, 1: 2, 2: 1} if special else {0: 3, 3: 0, 1: 2, 2: 1}
        for slab in range(4):
            own = home[slab]
            for slot, part, w_re, w_im in (
                (own, 0, 0.5, 0.5),
                (own, 1, -0.5, 0.5),
                (partner[own], 0, 0.5, -0.5),
                (partner[own], 1, 0.5, 0.5),
            ):
                rows = slice(32 * part, 32 * part + 32)
                out[4 * special + slab, rows, 32 * slot : 32 * slot + 32] += w_re * eye
                out[4 * special + slab, rows, PS + 32 * slot : PS + 32 * slot + 32] += w_im * eye
    return out.astype(jnp.bfloat16)


def dot(a, b, dims=NN):
    return lax.dot_general(a, b, dims, preferred_element_type=f32)


def split(x):
    hi = x.astype(bf16)
    return hi, (x - hi.astype(f32)).astype(bf16)


def dot_data_table(x, t_hi, t_lo):
    hi, lo = split(x)
    return dot(hi, t_hi) + (dot(lo, t_hi) + dot(hi, t_lo))


def dot_table_data(t_hi, t_lo, x):
    hi, lo = split(x)
    return dot(t_hi, hi) + (dot(t_hi, lo) + dot(t_lo, hi))


def iota(shape, dim):
    return lax.broadcasted_iota(jnp.int32, shape, dim)


def position():
    return lax.axis_index(STRIKE), lax.axis_index("dip")


def rev_bits(p):
    out = 0
    for b in range(LEVELS):
        out = out + (((p >> b) & 1) << (LEVELS - 1 - b))
    return out


def turn_rows(turns, q):
    return [(turns(0, 4 * q + b), turns(1, 4 * q + b)) for b in range(4)]


def interleave(dims):
    pos = iota((COLS_DEV, COLS_DEV), dims)
    return (iota((COLS_DEV, COLS_DEV), 1 - dims) == 4 * (pos & (PS - 1)) + (pos >> 7)).astype(f32).astype(bf16)


def by_class(x):
    return jnp.concatenate([x[:, PS * b : PS * (b + 1)] for b in range(4)], axis=0)


def signed(freq, length):
    return jnp.where(freq >= length // 2, freq - length, freq).astype(f32) * (1.0 / length)


def slip_part(slip, rate, tables, turns, q):
    x = slip + RATE_DT * rate
    parts = dot(jnp.concatenate(split(x), axis=0), interleave(1)).astype(bf16)
    hi, lo = by_class(parts[:ROWS_DEV]), by_class(parts[ROWS_DEV:])
    c = dot(hi, tables[0]) + (dot(lo, tables[0]) + dot(hi, tables[1]))
    s = dot(hi, tables[2]) + (dot(lo, tables[2]) + dot(hi, tables[3]))
    cs, ss = [], []
    for b, (ct, st) in enumerate(turn_rows(turns, q)):
        c_b, s_b = c[32 * b : 32 * b + 32], s[32 * b : 32 * b + 32]
        cs.append(ct * c_b - st * s_b)
        ss.append(st * c_b + ct * s_b)
    c_even, c_odd = cs[0] + cs[2], cs[1] + cs[3]
    s_sum = (ss[0] + ss[2]) + (ss[1] + ss[3])
    h_a = (c_even + c_odd) + s_sum
    first = iota((ROWS_DEV, COLS_DEV), 1) == 0
    h_d = (c_even + jnp.where(first, -c_odd, c_odd)) - s_sum
    even = cs[0] - cs[2] + ss[3] - ss[1]
    odd = ss[0] - ss[2] + cs[1] - cs[3]
    return jnp.concatenate([h_a, even + odd, even - odd, h_d], axis=0).T


def memory_weights(p, q):
    ks = rev_bits(p) + PS * iota((ROWS_DEV, COLS_DEV), 0)
    kd = q * COLS_DEV + iota((ROWS_DEV, COLS_DEV), 1)
    fs, fd = signed(ks, NS), signed(kd, ND)
    wave = (2.0 * math.pi) * jnp.sqrt(fs * fs + fd * fd)
    grow = jnp.exp(-0.15 * wave)
    ang = 0.9 * wave
    return grow * jnp.cos(ang), grow * jnp.sin(ang)


def memory_part(z_re, z_im, history, q):
    w_re, w_im = 0.5 * z_re, 0.5 * z_im
    m_re, m_im = w_re * history(0, 0), w_re * history(0, 1)
    for lag in range(1, 8):
        w_re, w_im = w_re * z_re - w_im * z_im, w_re * z_im + w_im * z_re
        m_re = m_re + w_re * history(lag, 0)
        m_im = m_im + w_re * history(lag, 1)
    both = jnp.concatenate([m_re, m_im], axis=0)
    shifted = pltpu.roll(both, COLS_DEV - 1, 1)
    near = [both[:, PS * i : PS * (i + 1)] for i in range(4)]
    far = [shifted[:, PS * i : PS * (i + 1)] for i in range(4)]
    blocks = [jnp.where(q < 2, near[i], far[3 - i]) for i in range(4)]
    row = iota((PS, PS), 0)
    perm = (iota((PS, PS), 1) == jnp.where(q < 2, row, PS - 1 - row)).astype(f32).astype(bf16)
    out = []
    for h in range(2):
        hi, lo = split(jnp.concatenate(blocks[2 * h : 2 * h + 2], axis=0))
        out.append(dot(perm, hi, NT) + dot(perm, lo, NT))
    return out


def send_kernel(slip_in, rate_in, history_in, tables_in, turns_in, out, slip, rate, history, tables, turns, sems):
    p, q = position()
    lags = history.shape[0]
    pairs = ((slip_in, slip), (rate_in, rate), (tables_in, tables), (turns_in, turns))
    copies = [pltpu.make_async_copy(src, dst, sems.at[lags + i]) for i, (src, dst) in enumerate(pairs)]
    lag_copies = [pltpu.make_async_copy(history_in.at[i], history.at[i], sems.at[i]) for i in range(lags)]
    for copy in copies + lag_copies:
        copy.start()
    z_re, z_im = memory_weights(p, q)
    for copy in copies:
        copy.wait()
    lines = slip_part(slip[...], rate[...], tables, lambda i, row: turns[i, pl.ds(row, 1), :], q)
    for i in range(4):
        out[pl.ds(i, PS, stride=SEND), :] = lines[PS * i : PS * (i + 1)]

    def read(lag, part):
        if part == 0:
            lag_copies[lag].wait()
        return history[lag, part]

    for h, part in enumerate(memory_part(z_re, z_im, read, q)):
        out[pl.ds(4 + h, PS, stride=SEND), :] = part


def strike_part(lines, mems, first, first_t, twiddle, second, second_inv, mem_table, p, q):
    n = PS
    w = []
    for h in range(2):
        m_hi, m_lo = split(mems[h])
        for parity in range(2):
            special = jnp.where(p == 0, 4, 0) if h == 0 and parity == 0 else 0
            table = mem_table(special + q)
            zero = jnp.zeros_like(table)
            table = jnp.concatenate([zero, table] if parity else [table, zero], axis=0)
            w.append(dot(m_hi, table) + dot(m_lo, table))
    w = jnp.concatenate(w, axis=0)
    a = dot_table_data(first[0], first[1], jnp.concatenate(lines, axis=1))
    tc, ts = twiddle[0], twiddle[1]
    b = []
    for i in range(4):
        a_re, a_im = a[:n, n * i : n * (i + 1)], a[n:, n * i : n * (i + 1)]
        b.append(jnp.concatenate([a_re * tc + a_im * ts, a_im * tc - a_re * ts], axis=1))
    spec = dot_data_table(jnp.concatenate(b, axis=0), second[0], second[1])
    lane = iota((n, n), 1)
    fs = signed(rev_bits(iota((n, n), 0)) + PS * (lane & 31), NS)
    fs = fs * fs
    slot = lane >> 5
    factor = []
    for i in range(4):
        ell = p + PS * i
        kd = jnp.where((slot == 1) | (slot == 2), COLS_DEV + ell, ell)
        kd = jnp.where((slot == 3) & (ell == 0), 2 * COLS_DEV, kd)
        fd = kd.astype(f32) * (1.0 / ND)
        wave = (2.0 * math.pi) * jnp.sqrt(fs + fd * fd)
        wave = (-0.5 * SCALE) * wave
        factor.append(jnp.concatenate([wave, wave], axis=1))
    g = jnp.concatenate(factor, axis=0) * (SCALE * spec - w)
    b = dot_data_table(g, second_inv[0], second_inv[1])
    turned = []
    for i in range(4):
        b_re, b_im = b[n * i : n * (i + 1), :n], b[n * i : n * (i + 1), n:]
        turned.append(jnp.concatenate([b_re * tc - b_im * ts, b_re * ts + b_im * tc], axis=0))
    return dot_table_data(first_t[0], first_t[1], jnp.concatenate(turned, axis=1))


def strike_kernel(recv, outbox, first, first_t, twiddle, second, second_inv, mem_table, out):
    t = strike_part(
        [recv[pl.ds(i, PS, stride=SEND), :] for i in range(4)],
        [recv[pl.ds(4 + h, PS, stride=SEND), :] for h in range(2)],
        first,
        first_t,
        twiddle,
        second,
        second_inv,
        lambda i: mem_table[i],
        *position(),
    )
    for i in range(4):
        out[pl.ds(i, PS, stride=BACK), :] = t[:, PS * i : PS * (i + 1)]
    out[pl.ds(4, PS, stride=BACK), :] = outbox[...]


def route_part(dest, node, value, count):
    dest = [dest[:, CHUNK * i : CHUNK * (i + 1)] for i in range(ROWS // CHUNK)]
    upto = (iota((CHUNK, CHUNK), 0) <= iota((CHUNK, CHUNK), 1)).astype(f32).astype(bf16)
    carry = jnp.zeros((PS, 1), f32)
    box = jnp.zeros((PS, 2 * CAP), f32)
    ranks = []
    for i in range(ROWS // CHUNK):
        cut = slice(CHUNK * i, CHUNK * (i + 1))
        named = iota((PS, CHUNK), 0) == dest[i]
        onehot = named.astype(f32).astype(bf16)
        upto_here = dot(onehot, upto) + carry
        rank = jnp.sum(jnp.where(named, upto_here, 0.0), axis=0, keepdims=True).astype(jnp.int32) - 1
        carry = upto_here[:, CHUNK - 1 : CHUNK]
        ranks.append(rank)
        live = (CHUNK * i + iota((1, CHUNK), 1)) < count
        v = jnp.where(live, value[:, cut], 0.0)
        v_hi = v.astype(bf16).astype(f32)
        v_lo = v - v_hi
        at = node[:, cut]
        n_hi = ((((at >> 7) & 3) << 5) + (at >> 9)) << 7
        n_lo = at & 127
        here = iota((CAP, CHUNK), 0) == rank
        part_1 = jnp.concatenate([jnp.where(here, v_hi, 0.0), jnp.where(here, n_hi.astype(f32), 0.0)], axis=0)
        part_2 = jnp.concatenate([jnp.where(here, v_lo, 0.0), jnp.where(here, n_lo.astype(f32), 0.0)], axis=0)
        box = box + (dot(onehot, part_1.astype(bf16), NT) + dot(onehot, part_2.astype(bf16), NT))
    return box, jnp.concatenate(ranks, axis=1)


def route_kernel(count, dest, node, value, out, rank):
    out[...], rank[...] = route_part(dest[...], node[...], value[...], count[0, 0])


def dip_inverse_part(recv, tables, turns):
    t = recv.T
    a, b, c, d = [t[32 * j : 32 * j + 32] for j in range(4)]
    s1, d1, s2, d2 = a + d, a - d, b + c, b - c
    fix = jnp.where(iota((ROWS_DEV, COLS_DEV), 1) == 0, 2.0 * d, 0.0)
    even = [s1 + s2, s1 + d2 - fix, s1 - s2, s1 - d2 - fix]
    odd = [d1 + d2, d1 - s2, d1 - d2, d1 + s2]
    evens, odds = [], []
    for i, (ct, st) in enumerate(turn_rows(turns, 0)):
        evens.append(ct * even[i] + st * odd[i])
        odds.append(ct * odd[i] - st * even[i])
    evens, odds = split(jnp.concatenate(evens, axis=0)), split(jnp.concatenate(odds, axis=0))
    turn = iota((1, COLS_DEV), 1) & 3
    keep_even = jnp.where((turn & 1) == 0, 1.0, 0.0).astype(bf16)
    keep_odd = jnp.where((turn & 1) == 1, 1.0, 0.0).astype(bf16)
    flip_even = jnp.where(turn == 0, 1.0, jnp.where(turn == 2, -1.0, 0.0)).astype(bf16)
    flip_odd = jnp.where(turn == 1, 1.0, jnp.where(turn == 3, -1.0, 0.0)).astype(bf16)
    f = 0.0
    for k, x, y, sign in ((0, evens, odds, flip_odd), (2, odds, evens, -flip_odd)):
        hi, lo = [
            jnp.concatenate([x[i] * keep_even, x[i] * keep_odd, x[i] * flip_even, y[i] * sign], axis=0) for i in range(2)
        ]
        f = f + (dot(hi, tables[k], NT) + (dot(lo, tables[k], NT) + dot(hi, tables[k + 1], NT)))
    f = [f[PS * i : PS * (i + 1)] for i in range(4)]
    f = [f[0] + f[1], f[2] + f[3], f[0] - f[1], f[2] - f[3]]
    rows = 32
    f = jnp.concatenate([jnp.concatenate([x[rows * i : rows * (i + 1)] for i in range(4)], axis=1) for x in f], axis=0)
    hi, lo = split(f)
    back = interleave(0)
    f = dot(hi, back) + dot(lo, back)
    return [f[rows * qd : rows * (qd + 1)] for qd in range(QD)]


def dip_kernel(recv, tables, turns, out):
    lines = jnp.concatenate([recv[pl.ds(i, PS, stride=BACK), :] for i in range(4)], axis=0)
    shares = dip_inverse_part(lines, tables, lambda i, row: turns[i, row : row + 1, :])
    for qd, share in enumerate(shares):
        out[qd] = share


def unpack_rows(fe, roll):
    top, bot = fe[0:CAP], fe[CAP:PS]
    left = iota((CAP, PS), 1) < CAP
    value = jnp.where(left, top, roll(bot))
    node = jnp.where(left, roll(top), bot).astype(jnp.int32)
    return value, node >> 7, node & 127


def lanes_of(x, group):
    return jnp.concatenate([x[4 * group + i : 4 * group + i + 1] for i in range(4)], axis=1)


def column_onehot(lo):
    return (iota((PS, CHUNK), 0) == lo).astype(f32).astype(bf16)


def traction_step(value, hi, onehot):
    named = iota((PS, CHUNK), 0) == hi
    v_hi = value.astype(bf16).astype(f32)
    rows = jnp.concatenate([jnp.where(named, v_hi, 0.0), jnp.where(named, value - v_hi, 0.0)], axis=0).astype(bf16)
    return dot(rows, onehot, NT)


def sample_step(rate_parts, hi, onehot):
    got = dot(rate_parts, jnp.concatenate([onehot, onehot], axis=0))
    return jnp.sum(jnp.where(iota((PS, CHUNK), 0) == hi, got, 0.0), axis=0, keepdims=True)


def roll_half(x):
    return pltpu.roll(x, CAP, 1)


def traction_kernel(recv, traction, onehots, spots):
    value, hi, lo = unpack_rows(recv[pl.ds(4, PS, stride=BACK), :], roll_half)
    spots[...] = hi
    acc = jnp.zeros((2 * PS, PS), f32)
    for g in range(CAP // 4):
        onehot = column_onehot(lanes_of(lo, g))
        onehots[g] = onehot
        acc = acc + traction_step(lanes_of(value, g), lanes_of(hi, g), onehot)
    acc = acc[:PS] + acc[PS:]
    traction[...] = jnp.concatenate([acc[32 * i : 32 * i + 32] for i in range(4)], axis=1)


def owner_kernel(
    shares, traction, onehots, spots, slip, rate, prestress, normal, flag, new_rate_out, stress_out, sampled, new_rate, stress, sems
):
    f = (shares[0] + shares[1]) + (shares[2] + shares[3])
    slip_new = slip[...] + RATE_DT * rate[...]
    total = prestress[...] + f + traction[...]
    strength = normal[...] * (0.6 - (0.6 - 0.4) * jnp.minimum(slip_new, 1.0))
    fresh = jnp.where(flag[...] == 1, jnp.maximum(total - strength, 0.0) * 2.0, 0.0)
    stress[...] = total
    new_rate[...] = fresh
    copies = [
        pltpu.make_async_copy(new_rate, new_rate_out, sems.at[0]),
        pltpu.make_async_copy(stress, stress_out, sems.at[1]),
    ]
    for copy in copies:
        copy.start()
    stacked = jnp.concatenate([fresh[:, PS * i : PS * (i + 1)] for i in range(4)], axis=0)
    parts = jnp.concatenate(split(stacked), axis=1)
    hi = spots[...]
    for g in range(CAP // 4):
        got = sample_step(parts, lanes_of(hi, g), onehots[g])
        for i in range(4):
            sampled[4 * g + i : 4 * g + i + 1, :] = got[:, PS * i : PS * (i + 1)]
    sampled[CAP:PS, :] = roll_half(sampled[0:CAP, :])
    for copy in copies:
        copy.wait()


def return_part(got, dest, rank, count):
    parts = jnp.concatenate(split(got.T[:CAP]), axis=1)
    out = []
    for i in range(ROWS // CHUNK):
        cut = slice(CHUNK * i, CHUNK * (i + 1))
        onehot = (iota((PS, CHUNK), 0) == dest[:, cut]).astype(f32).astype(bf16)
        here = dot(parts, jnp.concatenate([onehot, onehot], axis=0))
        here = jnp.sum(jnp.where(iota((CAP, CHUNK), 0) == rank[:, cut], here, 0.0), axis=0, keepdims=True)
        live = (CHUNK * i + iota((1, CHUNK), 1)) < count
        out.append(jnp.where(live, here, 0.0))
    return jnp.concatenate(out, axis=1)


def return_kernel(count, got, rank, dest, out):
    out[...] = return_part(got[...], dest[...], rank[...], count[0, 0])


def call(kernel, out_shape, operands, name, scalars=(), args=(), far=(), far_outs=0, scratch=()):
    spec = pl.BlockSpec(memory_space=pltpu.VMEM)
    hbm = pl.BlockSpec(memory_space=pltpu.HBM)
    in_specs = [pl.BlockSpec(memory_space=pltpu.SMEM)] * len(scalars) + [hbm] * len(far) + [spec] * (len(operands) + len(args))
    outs = tuple(hbm if i < far_outs else spec for i in range(len(out_shape))) if isinstance(out_shape, tuple) else spec
    far = [pltpu.with_memory_space_constraint(x, pltpu.HBM) for x in far]
    operands = [pltpu.with_memory_space_constraint(x, pltpu.VMEM) for x in operands]
    return pl.pallas_call(
        kernel,
        out_shape=out_shape,
        in_specs=in_specs,
        out_specs=outs,
        name=name,
        scratch_shapes=scratch,
        compiler_params=pltpu.CompilerParams(vmem_limit_bytes=VMEM_LIMIT),
    )(*scalars, *far, *operands, *args)


def sds(shape, dtype=f32):
    return pltpu.VMEM(shape, dtype)


def over_strike(x, width):
    unit = 2 if width % 2 == 0 else 1
    return lax.all_to_all(x.reshape(PS * width // unit, unit, PS), STRIKE, 0, 0, tiled=True).reshape(PS * width, PS)


def body(slip, rate, prestress, normal_stress, history, fric_flag, row_dest, row_node, fe_traction, fe_count):
    tables, turns = [jnp.asarray(t) for t in dip_tables()]
    strike = [jnp.asarray(t) for t in strike_tables()] + [jnp.asarray(memory_tables())]
    dest = row_dest.reshape(1, ROWS)

    inputs = (slip, rate, history, tables, turns)
    scratch = [pltpu.VMEM(x.shape, x.dtype) for x in inputs] + [pltpu.SemaphoreType.DMA((history.shape[0] + 4,))]
    sent = call(send_kernel, sds((PS * SEND, PS)), (), "send", far=inputs, scratch=scratch)
    recv = over_strike(sent, SEND)
    box, rank = call(
        route_kernel, (sds((PS, PS)), sds((1, ROWS), jnp.int32)), (), "route", (fe_count,), (dest, row_node, fe_traction)
    )
    sent = call(strike_kernel, sds((PS * BACK, PS)), (recv, box), "strike", args=strike)
    recv = over_strike(sent, BACK)
    shares = call(dip_kernel, sds((QD, ROWS_DEV, COLS_DEV)), (recv,), "dip", args=(tables, turns))
    shares = lax.all_to_all(shares, "dip", 0, 0, tiled=True)
    traction, onehots, spots = call(
        traction_kernel,
        (sds(slip.shape), sds((CAP // 4, PS, CHUNK), bf16), sds((CAP, PS), jnp.int32)),
        (recv,),
        "traction",
    )
    new_rate, stress, sampled = call(
        owner_kernel,
        (jax.ShapeDtypeStruct(slip.shape, f32), jax.ShapeDtypeStruct(slip.shape, f32), sds((PS, PS))),
        (shares, traction, onehots, spots),
        "owner",
        args=(slip, rate, prestress, normal_stress, fric_flag),
        far_outs=2,
        scratch=[sds(slip.shape), sds(slip.shape), pltpu.SemaphoreType.DMA((2,))],
    )
    got = over_strike(sampled, 1)
    fe_rate = call(return_kernel, jax.ShapeDtypeStruct((1, ROWS), f32), (got, rank), "back", (fe_count,), (dest,))
    return new_rate, stress, fe_rate


def solution(mesh):
    fine = Mesh(mesh.devices.reshape(8, 8, 2, 4), ("z", "y", "c", "dip"))
    field = P(STRIKE, "dip")
    rows = P("dip", STRIKE)
    in_specs = (field, field, field, field, P(None, None, STRIKE, "dip"), field, P("dip", STRIKE, None), rows, rows, rows)
    return jax.shard_map(body, mesh=fine, in_specs=in_specs, out_specs=(field, field, rows), check_vma=False)
```

```python
import math

import jax
import jax.numpy as jnp
import numpy as np
from jax import lax
from jax.experimental import pallas as pl
from jax.experimental.pallas import tpu as pltpu
from jax.sharding import Mesh
from jax.sharding import PartitionSpec as P

NS, ND = 4096, 2048
PS, QD = 128, 4
ROWS_DEV, COLS_DEV = NS // PS, ND // QD
RATE_DT = 0.5
LEVELS = 7
CAP = 64
ROWS = 4096
CHUNK = 512
VMEM_LIMIT = 24 << 20
STRIKE = ("z", "y", "c")
SEND, BACK = 4, 3
SCALE = 1.0 / math.sqrt(NS * ND)
bf16 = jnp.bfloat16
f32 = jnp.float32
NN = (((1,), (0,)), ((), ()))
NT = (((1,), (1,)), ((), ()))


def np_split(table):
    hi = table.astype(np.float32).astype(jnp.bfloat16)
    lo = (table - hi.astype(np.float64)).astype(np.float32).astype(jnp.bfloat16)
    return np.stack([hi, lo])


def np_rev(p):
    return sum(((p >> b) & 1) << (LEVELS - 1 - b) for b in range(LEVELS))


def dip_tables():
    ell = np.arange(COLS_DEV)
    ang = 2 * np.pi * ((np.arange(COLS_DEV // 4)[:, None] * ell[None, :]) % COLS_DEV) / COLS_DEV
    b = np.tile(np.arange(4), QD)[:, None]
    q = np.repeat(np.arange(QD), 4)[:, None]
    turn = 2 * np.pi * ((ell * b + COLS_DEV * q * ell) % ND) / ND
    tables = np.concatenate([np_split(np.cos(ang)), np_split(np.sin(ang))])
    return tables, np.stack([np.cos(turn), np.sin(turn)]).astype(np.float32)


def strike_tables():
    p = np.arange(PS)
    k1 = np_rev(p)
    ang = 2 * np.pi * ((k1[:, None] * p[None, :]) % PS) / PS
    first = np.concatenate([np.cos(ang), -np.sin(ang)])
    r = np.arange(ROWS_DEV)
    tw = 2 * np.pi * (k1[:, None] * r[None, :]) / NS
    twiddle = np.stack([np.tile(np.cos(tw), (1, 4)), np.tile(np.sin(tw), (1, 4))]).astype(np.float32)
    small = 2 * np.pi * ((r[:, None] * r[None, :]) % ROWS_DEV) / ROWS_DEV
    cb = np.kron(np.eye(4), np.cos(small))
    sb = np.kron(np.eye(4), np.sin(small))
    second = np.block([[cb, -sb], [sb, cb]])
    second_inv = np.block([[cb, sb], [-sb, cb]])
    return np_split(first), np_split(first.T), twiddle, np_split(second), np_split(second_inv)


def memory_tables():
    out = np.zeros((4, 2, 2, 32, 2, 2, 2, 32), np.float32)
    eye = np.eye(ROWS_DEV)
    for case in range(4):
        own = case & 1
        for parity in range(2):
            other = own if case >= 2 and parity == 0 else 1 - own
            for slot, part, w_re, w_im in ((own, 0, 0.5, 0.5), (own, 1, -0.5, 0.5), (other, 0, 0.5, -0.5), (other, 1, 0.5, 0.5)):
                out[case, parity, part, :, 0, parity, slot, :] += w_re * eye
                out[case, parity, part, :, 1, parity, slot, :] += w_im * eye
    return out.reshape(4, PS, 2 * PS).astype(jnp.bfloat16)


def dot(a, b, dims=NN):
    return lax.dot_general(a, b, dims, preferred_element_type=f32)


def split(x):
    hi = x.astype(bf16)
    return hi, (x - hi.astype(f32)).astype(bf16)


def dot_data_table(x, t_hi, t_lo):
    hi, lo = split(x)
    return dot(hi, t_hi) + (dot(lo, t_hi) + dot(hi, t_lo))


def dot_table_data(t_hi, t_lo, x):
    hi, lo = split(x)
    return dot(t_hi, hi) + (dot(t_hi, lo) + dot(t_lo, hi))


def iota(shape, dim):
    return lax.broadcasted_iota(jnp.int32, shape, dim)


def position():
    return lax.axis_index(STRIKE), lax.axis_index("dip")


def rev_bits(p):
    out = 0
    for b in range(LEVELS):
        out = out + (((p >> b) & 1) << (LEVELS - 1 - b))
    return out


def turn_rows(turns, q):
    return [(turns(0, 4 * q + b), turns(1, 4 * q + b)) for b in range(4)]


def interleave():
    pos = iota((COLS_DEV, COLS_DEV), 1)
    return (iota((COLS_DEV, COLS_DEV), 0) == 4 * (pos & (PS - 1)) + (pos >> 7)).astype(f32).astype(bf16)


def by_class(x):
    return jnp.concatenate([x[:, PS * b : PS * (b + 1)] for b in range(4)], axis=0)


def signed(freq, length):
    return jnp.where(freq >= length // 2, freq - length, freq).astype(f32) * (1.0 / length)


def outer_modes(ell, q):
    return jnp.where(ell == 0, 1 - (q & 1), 1 - ((q ^ (q >> 1)) & 1)) == 1


def dip_forward_part(x, perm, tables, turns, q):
    parts = dot(jnp.concatenate(split(x), axis=0), perm).astype(bf16)
    hi, lo = by_class(parts[:ROWS_DEV]), by_class(parts[ROWS_DEV:])
    c = dot(hi, tables[0]) + (dot(lo, tables[0]) + dot(hi, tables[1]))
    s = dot(hi, tables[2]) + (dot(lo, tables[2]) + dot(hi, tables[3]))
    cs, ss = [], []
    for b, (ct, st) in enumerate(turn_rows(turns, q)):
        c_b, s_b = c[32 * b : 32 * b + 32], s[32 * b : 32 * b + 32]
        cs.append(ct * c_b - st * s_b)
        ss.append(st * c_b + ct * s_b)
    return jnp.concatenate(cs + ss, axis=0)


def slip_part(sums, q):
    sums = [sums[32 * i : 32 * i + 32] for i in range(8)]
    cs, ss = sums[:4], sums[4:]
    c_even, c_odd = cs[0] + cs[2], cs[1] + cs[3]
    s_sum = (ss[0] + ss[2]) + (ss[1] + ss[3])
    ell = iota((ROWS_DEV, COLS_DEV), 1)
    h_a = (c_even + c_odd) + s_sum
    h_d = (c_even + jnp.where(ell == 0, -c_odd, c_odd)) - s_sum
    even = cs[0] - cs[2] + ss[3] - ss[1]
    odd = ss[0] - ss[2] + cs[1] - cs[3]
    outer = outer_modes(ell, q)
    both = jnp.concatenate([jnp.where(outer, h_a, even + odd), jnp.where(outer, h_d, even - odd)], axis=0)
    both = [both[:, PS * i : PS * (i + 1)] for i in range(4)]
    return [jnp.concatenate(both[2 * h : 2 * h + 2], axis=0).T for h in range(2)]


def memory_weights(p, q):
    ks = rev_bits(p) + PS * iota((ROWS_DEV, COLS_DEV), 0)
    kd = q * COLS_DEV + iota((ROWS_DEV, COLS_DEV), 1)
    fs, fd = signed(ks, NS), signed(kd, ND)
    wave = (2.0 * math.pi) * jnp.sqrt(fs * fs + fd * fd)
    grow = jnp.exp(-0.15 * wave)
    ang = 0.9 * wave
    return grow * jnp.cos(ang), grow * jnp.sin(ang)


def memory_part(z_re, z_im, history, q):
    w_re, w_im = 0.5 * z_re, 0.5 * z_im
    m_re, m_im = w_re * history(0, 0), w_re * history(0, 1)
    for lag in range(1, 8):
        w_re, w_im = w_re * z_re - w_im * z_im, w_re * z_im + w_im * z_re
        m_re = m_re + w_re * history(lag, 0)
        m_im = m_im + w_re * history(lag, 1)
    both = jnp.concatenate([m_re, m_im], axis=0)
    shifted = pltpu.roll(both, COLS_DEV - 1, 1)
    near = [both[:, PS * i : PS * (i + 1)] for i in range(4)]
    far = [shifted[:, PS * i : PS * (i + 1)] for i in range(4)]
    blocks = [jnp.where(q < 2, near[i], far[3 - i]) for i in range(4)]
    row = iota((PS, PS), 0)
    perm = (iota((PS, PS), 1) == jnp.where(q < 2, row, PS - 1 - row)).astype(f32).astype(bf16)
    out = []
    for h in range(2):
        hi, lo = split(jnp.concatenate(blocks[2 * h : 2 * h + 2], axis=0))
        out.append(dot(perm, hi, NT) + dot(perm, lo, NT))
    return out


def near_kernel(history_in, tables_in, turns_in, own, mem, sums, perm, tables, turns, history, sems):
    p, q = position()
    lags = history.shape[0]
    far_tables = [
        pltpu.make_async_copy(tables_in, tables, sems.at[lags]),
        pltpu.make_async_copy(turns_in, turns, sems.at[lags + 1]),
    ]
    copies = [pltpu.make_async_copy(history_in.at[i], history.at[i], sems.at[i]) for i in range(lags)]
    for copy in far_tables + copies:
        copy.start()
    z_re, z_im = memory_weights(p, q)
    perm[...] = interleave()
    for copy in far_tables:
        copy.wait()
    sums[...] = dip_forward_part(own[...], perm[...], tables, lambda i, row: turns[i, pl.ds(row, 1), :], q)

    def read(lag, part):
        if part == 0:
            copies[lag].wait()
        return history[lag, part]

    for h, part in enumerate(memory_part(z_re, z_im, read, q)):
        mem[PS * h : PS * (h + 1), :] = part


def send_kernel(other, mem, sums, perm, tables, turns, out):
    q = position()[1]
    far = dip_forward_part(other[...], perm[...], tables, lambda i, row: turns[i, pl.ds(row, 1), :], q ^ 1)
    lines = slip_part(sums[...] + far, q)
    for h in range(2):
        out[pl.ds(h, PS, stride=SEND), :] = lines[h]
        out[pl.ds(2 + h, PS, stride=SEND), :] = mem[PS * h : PS * (h + 1), :]


def strike_part(lines, mems, first, first_t, twiddle, second, second_inv, mem_table, p, q):
    n = PS
    w = []
    for h in range(2):
        m_hi, m_lo = split(mems[h])
        alone = jnp.where((p == 0) & ((q & 1) == 0), 2, 0) if h == 0 else 0
        table = mem_table(alone + (q >> 1))
        w.append(dot(m_hi, table) + dot(m_lo, table))
    w = jnp.concatenate(w, axis=0)
    a = dot_table_data(first[0], first[1], jnp.concatenate(lines, axis=1))
    tc, ts = twiddle[0], twiddle[1]
    b = []
    for h in range(2):
        a_re, a_im = a[:n, n * h : n * (h + 1)], a[n:, n * h : n * (h + 1)]
        b.append(jnp.concatenate([a_re * tc + a_im * ts, a_im * tc - a_re * ts], axis=1))
    spec = dot_data_table(jnp.concatenate(b, axis=0), second[0], second[1])
    lane = iota((n, n), 1)
    fs = signed(rev_bits(iota((n, n), 0)) + PS * (lane & 31), NS)
    fs = fs * fs
    parity, slot = lane >> 6, (lane >> 5) & 1
    factor = []
    for h in range(2):
        ell = p + PS * (2 * h + parity)
        kd = jnp.where(outer_modes(ell, q), jnp.where((ell == 0) & (slot == 1), 2 * COLS_DEV, ell), COLS_DEV + ell)
        fd = kd.astype(f32) * (1.0 / ND)
        wave = (2.0 * math.pi) * jnp.sqrt(fs + fd * fd)
        wave = (-0.5 * SCALE) * wave
        factor.append(jnp.concatenate([wave, wave], axis=1))
    g = jnp.concatenate(factor, axis=0) * (SCALE * spec - w)
    b = dot_data_table(g, second_inv[0], second_inv[1])
    turned = []
    for h in range(2):
        b_re, b_im = b[n * h : n * (h + 1), :n], b[n * h : n * (h + 1), n:]
        turned.append(jnp.concatenate([b_re * tc - b_im * ts, b_re * ts + b_im * tc], axis=0))
    return dot_table_data(first_t[0], first_t[1], jnp.concatenate(turned, axis=1))


def strike_kernel(recv, outbox, first, first_t, twiddle, second, second_inv, mem_table, out):
    t = strike_part(
        [recv[pl.ds(h, PS, stride=SEND), :] for h in range(2)],
        [recv[pl.ds(2 + h, PS, stride=SEND), :] for h in range(2)],
        first,
        first_t,
        twiddle,
        second,
        second_inv,
        lambda i: mem_table[i],
        *position(),
    )
    for h in range(2):
        out[pl.ds(h, PS, stride=BACK), :] = t[:, PS * h : PS * (h + 1)]
    out[pl.ds(2, PS, stride=BACK), :] = outbox[...]


def route_part(dest, node, value, count):
    dest = [dest[:, CHUNK * i : CHUNK * (i + 1)] for i in range(ROWS // CHUNK)]
    upto = (iota((CHUNK, CHUNK), 0) <= iota((CHUNK, CHUNK), 1)).astype(f32).astype(bf16)
    carry = jnp.zeros((PS, 1), f32)
    box = jnp.zeros((PS, 2 * CAP), f32)
    ranks = []
    for i in range(ROWS // CHUNK):
        cut = slice(CHUNK * i, CHUNK * (i + 1))
        named = iota((PS, CHUNK), 0) == dest[i]
        onehot = named.astype(f32).astype(bf16)
        upto_here = dot(onehot, upto) + carry
        rank = jnp.sum(jnp.where(named, upto_here, 0.0), axis=0, keepdims=True).astype(jnp.int32) - 1
        carry = upto_here[:, CHUNK - 1 : CHUNK]
        ranks.append(rank)
        live = (CHUNK * i + iota((1, CHUNK), 1)) < count
        v = jnp.where(live, value[:, cut], 0.0)
        v_hi = v.astype(bf16).astype(f32)
        v_lo = v - v_hi
        at = node[:, cut]
        n_hi = ((((at >> 7) & 3) << 5) + (at >> 9)) << 7
        n_lo = at & 127
        here = iota((CAP, CHUNK), 0) == rank
        part_1 = jnp.concatenate([jnp.where(here, v_hi, 0.0), jnp.where(here, n_hi.astype(f32), 0.0)], axis=0)
        part_2 = jnp.concatenate([jnp.where(here, v_lo, 0.0), jnp.where(here, n_lo.astype(f32), 0.0)], axis=0)
        box = box + (dot(onehot, part_1.astype(bf16), NT) + dot(onehot, part_2.astype(bf16), NT))
    return box, jnp.concatenate(ranks, axis=1)


def route_kernel(count, dest, node, value, out, rank):
    out[...], rank[...] = route_part(dest[...], node[...], value[...], count[0, 0])


def dip_inverse_part(lines, tables, turns, perm, q):
    lines = [x.T for x in lines]
    t0, t1 = [
        jnp.concatenate([lines[i >> 1][64 * (i & 1) + 32 * slot : 64 * (i & 1) + 32 * slot + 32] for i in range(4)], axis=1)
        for slot in range(2)
    ]
    ell = iota((ROWS_DEV, COLS_DEV), 1)
    outer = outer_modes(ell, q)
    total, diff = t0 + t1, t0 - t1
    s1, d1 = jnp.where(outer, total, 0.0), jnp.where(outer, diff, 0.0)
    s2, d2 = total - s1, diff - d1
    fix = jnp.where(outer & (ell == 0), 2.0 * t1, 0.0)
    even = [s1 + s2, s1 + d2 - fix, s1 - s2, s1 - d2 - fix]
    odd = [d1 + d2, d1 - s2, d1 - d2, d1 + s2]
    evens, odds = [], []
    for i, (ct, st) in enumerate(turn_rows(turns, 0)):
        evens.append(ct * even[i] + st * odd[i])
        odds.append(ct * odd[i] - st * even[i])
    evens, odds = split(jnp.concatenate(evens, axis=0)), split(jnp.concatenate(odds, axis=0))
    turn = iota((1, COLS_DEV), 1) & 3
    keep_even = jnp.where((turn & 1) == 0, 1.0, 0.0).astype(bf16)
    keep_odd = jnp.where((turn & 1) == 1, 1.0, 0.0).astype(bf16)
    flip_even = jnp.where(turn == 0, 1.0, jnp.where(turn == 2, -1.0, 0.0)).astype(bf16)
    flip_odd = jnp.where(turn == 1, 1.0, jnp.where(turn == 3, -1.0, 0.0)).astype(bf16)
    f = 0.0
    for k, x, y, sign in ((0, evens, odds, flip_odd), (2, odds, evens, -flip_odd)):
        hi, lo = [
            jnp.concatenate([x[i] * keep_even, x[i] * keep_odd, x[i] * flip_even, y[i] * sign], axis=0) for i in range(2)
        ]
        f = f + (dot(hi, tables[k], NT) + (dot(lo, tables[k], NT) + dot(hi, tables[k + 1], NT)))
    f = [f[PS * i : PS * (i + 1)] for i in range(4)]
    f = [f[0] + f[1], f[2] + f[3], f[0] - f[1], f[2] - f[3]]
    rows = 32
    f = jnp.concatenate([jnp.concatenate([x[rows * i : rows * (i + 1)] for i in range(4)], axis=1) for x in f], axis=0)
    hi, lo = split(f)
    f = dot(hi, perm, NT) + dot(lo, perm, NT)
    return [f[rows * qd : rows * (qd + 1)] for qd in range(QD)]


def dip_kernel(recv, perm, tables, turns, out):
    lines = [recv[pl.ds(h, PS, stride=BACK), :] for h in range(2)]
    shares = dip_inverse_part(lines, tables, lambda i, row: turns[i, row : row + 1, :], perm[...], position()[1])
    for qd, share in enumerate(shares):
        out[qd] = share


def unpack_rows(fe, roll):
    top, bot = fe[0:CAP], fe[CAP:PS]
    left = iota((CAP, PS), 1) < CAP
    value = jnp.where(left, top, roll(bot))
    node = jnp.where(left, roll(top), bot).astype(jnp.int32)
    return value, node >> 7, node & 127


def lanes_of(x, group):
    return jnp.concatenate([x[4 * group + i : 4 * group + i + 1] for i in range(4)], axis=1)


def column_onehot(lo):
    return (iota((PS, CHUNK), 0) == lo).astype(f32).astype(bf16)


def traction_step(value, hi, onehot):
    named = iota((PS, CHUNK), 0) == hi
    v_hi = value.astype(bf16).astype(f32)
    rows = jnp.concatenate([jnp.where(named, v_hi, 0.0), jnp.where(named, value - v_hi, 0.0)], axis=0).astype(bf16)
    return dot(rows, onehot, NT)


def sample_step(rate_parts, hi, onehot):
    got = dot(rate_parts, jnp.concatenate([onehot, onehot], axis=0))
    return jnp.sum(jnp.where(iota((PS, CHUNK), 0) == hi, got, 0.0), axis=0, keepdims=True)


def roll_half(x):
    return pltpu.roll(x, CAP, 1)


def traction_kernel(recv, traction, onehots, spots):
    value, hi, lo = unpack_rows(recv[pl.ds(2, PS, stride=BACK), :], roll_half)
    spots[...] = hi
    acc = jnp.zeros((2 * PS, PS), f32)
    for g in range(CAP // 4):
        onehot = column_onehot(lanes_of(lo, g))
        onehots[g] = onehot
        acc = acc + traction_step(lanes_of(value, g), lanes_of(hi, g), onehot)
    acc = acc[:PS] + acc[PS:]
    traction[...] = jnp.concatenate([acc[32 * i : 32 * i + 32] for i in range(4)], axis=1)


def owner_kernel(
    shares, traction, onehots, spots, slip, rate, prestress, normal, flag, new_rate_out, stress_out, sampled, new_rate, stress, sems
):
    f = (shares[0] + shares[1]) + (shares[2] + shares[3])
    slip_new = slip[...] + RATE_DT * rate[...]
    total = prestress[...] + f + traction[...]
    strength = normal[...] * (0.6 - (0.6 - 0.4) * jnp.minimum(slip_new, 1.0))
    fresh = jnp.where(flag[...] == 1, jnp.maximum(total - strength, 0.0) * 2.0, 0.0)
    stress[...] = total
    new_rate[...] = fresh
    copies = [
        pltpu.make_async_copy(new_rate, new_rate_out, sems.at[0]),
        pltpu.make_async_copy(stress, stress_out, sems.at[1]),
    ]
    for copy in copies:
        copy.start()
    stacked = jnp.concatenate([fresh[:, PS * i : PS * (i + 1)] for i in range(4)], axis=0)
    parts = jnp.concatenate(split(stacked), axis=1)
    hi = spots[...]
    for g in range(CAP // 4):
        got = sample_step(parts, lanes_of(hi, g), onehots[g])
        for i in range(4):
            sampled[4 * g + i : 4 * g + i + 1, :] = got[:, PS * i : PS * (i + 1)]
    sampled[CAP:PS, :] = roll_half(sampled[0:CAP, :])
    for copy in copies:
        copy.wait()


def return_part(got, dest, rank, count):
    parts = jnp.concatenate(split(got.T[:CAP]), axis=1)
    out = []
    for i in range(ROWS // CHUNK):
        cut = slice(CHUNK * i, CHUNK * (i + 1))
        onehot = (iota((PS, CHUNK), 0) == dest[:, cut]).astype(f32).astype(bf16)
        here = dot(parts, jnp.concatenate([onehot, onehot], axis=0))
        here = jnp.sum(jnp.where(iota((CAP, CHUNK), 0) == rank[:, cut], here, 0.0), axis=0, keepdims=True)
        live = (CHUNK * i + iota((1, CHUNK), 1)) < count
        out.append(jnp.where(live, here, 0.0))
    return jnp.concatenate(out, axis=1)


def return_kernel(count, got, rank, dest, out):
    out[...] = return_part(got[...], dest[...], rank[...], count[0, 0])


def call(kernel, out_shape, operands, name, scalars=(), args=(), far=(), far_outs=0, scratch=()):
    spec = pl.BlockSpec(memory_space=pltpu.VMEM)
    hbm = pl.BlockSpec(memory_space=pltpu.HBM)
    in_specs = [pl.BlockSpec(memory_space=pltpu.SMEM)] * len(scalars) + [hbm] * len(far) + [spec] * (len(operands) + len(args))
    outs = tuple(hbm if i < far_outs else spec for i in range(len(out_shape))) if isinstance(out_shape, tuple) else spec
    far = [pltpu.with_memory_space_constraint(x, pltpu.HBM) for x in far]
    operands = [pltpu.with_memory_space_constraint(x, pltpu.VMEM) for x in operands]
    return pl.pallas_call(
        kernel,
        out_shape=out_shape,
        in_specs=in_specs,
        out_specs=outs,
        name=name,
        scratch_shapes=scratch,
        compiler_params=pltpu.CompilerParams(vmem_limit_bytes=VMEM_LIMIT),
    )(*scalars, *far, *operands, *args)


def sds(shape, dtype=f32):
    return pltpu.VMEM(shape, dtype)


def over_strike(x, width):
    unit = width if width in (1, 2, 4) else 1
    return lax.all_to_all(x.reshape(PS * width // unit, unit, PS), STRIKE, 0, 0, tiled=True).reshape(PS * width, PS)


def body(slip, rate, prestress, normal_stress, history, fric_flag, row_dest, row_node, fe_traction, fe_count):
    tables, turns = [jnp.asarray(t) for t in dip_tables()]
    strike = [jnp.asarray(t) for t in strike_tables()] + [jnp.asarray(memory_tables())]
    dest = row_dest.reshape(1, ROWS)

    slip_new = slip + RATE_DT * rate
    other = lax.ppermute(slip_new, "dip", [(i, i ^ 1) for i in range(QD)])
    mem, sums, perm, tables, turns = call(
        near_kernel,
        (
            sds((2 * PS, PS)),
            sds((8 * ROWS_DEV, COLS_DEV)),
            sds((COLS_DEV, COLS_DEV), bf16),
            sds(tables.shape, bf16),
            sds(turns.shape),
        ),
        (slip_new,),
        "near",
        far=(history, tables, turns),
        scratch=[sds(history.shape), pltpu.SemaphoreType.DMA((history.shape[0] + 2,))],
    )
    sent = call(send_kernel, sds((PS * SEND, PS)), (other, mem, sums, perm, tables, turns), "send")
    recv = over_strike(sent, SEND)
    box, rank = call(
        route_kernel, (sds((PS, PS)), sds((1, ROWS), jnp.int32)), (), "route", (fe_count,), (dest, row_node, fe_traction)
    )
    sent = call(strike_kernel, sds((PS * BACK, PS)), (recv, box), "strike", args=strike)
    recv = over_strike(sent, BACK)
    shares = call(dip_kernel, sds((QD, ROWS_DEV, COLS_DEV)), (recv, perm, tables, turns), "dip")
    shares = lax.all_to_all(shares, "dip", 0, 0, tiled=True)
    traction, onehots, spots = call(
        traction_kernel,
        (sds(slip.shape), sds((CAP // 4, PS, CHUNK), bf16), sds((CAP, PS), jnp.int32)),
        (recv,),
        "traction",
    )
    new_rate, stress, sampled = call(
        owner_kernel,
        (jax.ShapeDtypeStruct(slip.shape, f32), jax.ShapeDtypeStruct(slip.shape, f32), sds((PS, PS))),
        (shares, traction, onehots, spots),
        "owner",
        args=(slip, rate, prestress, normal_stress, fric_flag),
        far_outs=2,
        scratch=[sds(slip.shape), sds(slip.shape), pltpu.SemaphoreType.DMA((2,))],
    )
    got = over_strike(sampled, 1)
    fe_rate = call(return_kernel, jax.ShapeDtypeStruct((1, ROWS), f32), (got, rank), "back", (fe_count,), (dest,))
    return new_rate, stress, fe_rate


def solution(mesh):
    fine = Mesh(mesh.devices.reshape(8, 8, 2, 4), ("z", "y", "c", "dip"))
    field = P(STRIKE, "dip")
    rows = P("dip", STRIKE)
    in_specs = (field, field, field, field, P(None, None, STRIKE, "dip"), field, P("dip", STRIKE, None), rows, rows, rows)
    return jax.shard_map(body, mesh=fine, in_specs=in_specs, out_specs=(field, field, rows), check_vma=False)
```

```python
import math

import jax
import jax.numpy as jnp
import numpy as np
from jax import lax
from jax.experimental import pallas as pl
from jax.experimental.pallas import tpu as pltpu
from jax.sharding import Mesh
from jax.sharding import PartitionSpec as P

NS, ND = 4096, 2048
PS, QD = 128, 4
ROWS_DEV, COLS_DEV = NS // PS, ND // QD
RATE_DT = 0.5
LEVELS = 7
CAP = 64
ROWS = 4096
CHUNK = 512
VMEM_LIMIT = 24 << 20
STRIKE = ("z", "y", "c")
SEND, BACK = 4, 3
SCALE = 1.0 / math.sqrt(NS * ND)
bf16 = jnp.bfloat16
f32 = jnp.float32
NN = (((1,), (0,)), ((), ()))
NT = (((1,), (1,)), ((), ()))


def np_split(table):
    hi = table.astype(np.float32).astype(jnp.bfloat16)
    lo = (table - hi.astype(np.float64)).astype(np.float32).astype(jnp.bfloat16)
    return np.stack([hi, lo])


def np_rev(p):
    return sum(((p >> b) & 1) << (LEVELS - 1 - b) for b in range(LEVELS))


def dip_tables():
    ell = np.arange(COLS_DEV)
    ang = 2 * np.pi * ((np.arange(COLS_DEV // 4)[:, None] * ell[None, :]) % COLS_DEV) / COLS_DEV
    b = np.tile(np.arange(4), QD)[:, None]
    q = np.repeat(np.arange(QD), 4)[:, None]
    turn = 2 * np.pi * ((ell * b + COLS_DEV * q * ell) % ND) / ND
    tables = np.concatenate([np_split(np.cos(ang)), np_split(np.sin(ang))])
    return tables, np.stack([np.cos(turn), np.sin(turn)]).astype(np.float32)


def strike_tables():
    p = np.arange(PS)
    k1 = np_rev(p)
    ang = 2 * np.pi * ((k1[:, None] * p[None, :]) % PS) / PS
    first = np.concatenate([np.cos(ang), -np.sin(ang)])
    r = np.arange(ROWS_DEV)
    tw = 2 * np.pi * (k1[:, None] * r[None, :]) / NS
    twiddle = np.stack([np.tile(np.cos(tw), (1, 4)), np.tile(np.sin(tw), (1, 4))]).astype(np.float32)
    small = 2 * np.pi * ((r[:, None] * r[None, :]) % ROWS_DEV) / ROWS_DEV
    cb = np.kron(np.eye(4), np.cos(small))
    sb = np.kron(np.eye(4), np.sin(small))
    second = np.block([[cb, -sb], [sb, cb]])
    return np_split(first), np_split(first.T), twiddle, np_split(second)


def memory_tables():
    out = np.zeros((4, 2, 2, 32, 2, 2, 2, 32), np.float32)
    eye = np.eye(ROWS_DEV)
    for case in range(4):
        own = case & 1
        for parity in range(2):
            other = own if case >= 2 and parity == 0 else 1 - own
            for slot, part, w_re, w_im in ((own, 0, 0.5, 0.5), (own, 1, -0.5, 0.5), (other, 0, 0.5, -0.5), (other, 1, 0.5, 0.5)):
                out[case, parity, part, :, 0, parity, slot, :] += w_re * eye
                out[case, parity, part, :, 1, parity, slot, :] += w_im * eye
    return out.reshape(4, PS, 2 * PS).astype(jnp.bfloat16)


def dot(a, b, dims=NN):
    return lax.dot_general(a, b, dims, preferred_element_type=f32)


def split(x):
    hi = x.astype(bf16)
    return hi, (x - hi.astype(f32)).astype(bf16)


def dot_data_table(x, t_hi, t_lo):
    hi, lo = split(x)
    return dot(hi, t_hi) + (dot(lo, t_hi) + dot(hi, t_lo))


def dot_data_turned(x, t_hi, t_lo):
    hi, lo = split(x)
    return dot(hi, t_hi, NT) + (dot(lo, t_hi, NT) + dot(hi, t_lo, NT))


def dot_table_data(t_hi, t_lo, x):
    hi, lo = split(x)
    return dot(t_hi, hi) + (dot(t_hi, lo) + dot(t_lo, hi))


def iota(shape, dim):
    return lax.broadcasted_iota(jnp.int32, shape, dim)


def position():
    return lax.axis_index(STRIKE), lax.axis_index("dip")


def rev_bits(p):
    out = 0
    for b in range(LEVELS):
        out = out + (((p >> b) & 1) << (LEVELS - 1 - b))
    return out


def turn_rows(turns, q):
    return [(turns(0, 4 * q + b), turns(1, 4 * q + b)) for b in range(4)]


def interleave(dims):
    pos = iota((COLS_DEV, COLS_DEV), dims)
    return (iota((COLS_DEV, COLS_DEV), 1 - dims) == 4 * (pos & (PS - 1)) + (pos >> 7)).astype(f32).astype(bf16)


def by_class(x):
    return jnp.concatenate([x[:, PS * b : PS * (b + 1)] for b in range(4)], axis=0)


def signed(freq, length):
    return jnp.where(freq >= length // 2, freq - length, freq).astype(f32) * (1.0 / length)


def outer_modes(ell, q):
    return jnp.where(ell == 0, 1 - (q & 1), 1 - ((q ^ (q >> 1)) & 1)) == 1


def dip_forward_part(x, perm, tables, turns, q):
    parts = dot(jnp.concatenate(split(x), axis=0), perm).astype(bf16)
    hi, lo = by_class(parts[:ROWS_DEV]), by_class(parts[ROWS_DEV:])
    c = dot(hi, tables[0]) + (dot(lo, tables[0]) + dot(hi, tables[1]))
    s = dot(hi, tables[2]) + (dot(lo, tables[2]) + dot(hi, tables[3]))
    cs, ss = [], []
    for b, (ct, st) in enumerate(turn_rows(turns, q)):
        c_b, s_b = c[32 * b : 32 * b + 32], s[32 * b : 32 * b + 32]
        cs.append(ct * c_b - st * s_b)
        ss.append(st * c_b + ct * s_b)
    return jnp.concatenate(cs + ss, axis=0)


def slip_part(sums, q):
    sums = [sums[32 * i : 32 * i + 32] for i in range(8)]
    cs, ss = sums[:4], sums[4:]
    c_even, c_odd = cs[0] + cs[2], cs[1] + cs[3]
    s_sum = (ss[0] + ss[2]) + (ss[1] + ss[3])
    ell = iota((ROWS_DEV, COLS_DEV), 1)
    h_a = (c_even + c_odd) + s_sum
    h_d = (c_even + jnp.where(ell == 0, -c_odd, c_odd)) - s_sum
    even = cs[0] - cs[2] + ss[3] - ss[1]
    odd = ss[0] - ss[2] + cs[1] - cs[3]
    outer = outer_modes(ell, q)
    both = jnp.concatenate([jnp.where(outer, h_a, even + odd), jnp.where(outer, h_d, even - odd)], axis=0)
    both = [both[:, PS * i : PS * (i + 1)] for i in range(4)]
    return [jnp.concatenate(both[2 * h : 2 * h + 2], axis=0).T for h in range(2)]


def memory_weights(p, q):
    ks = rev_bits(p) + PS * iota((ROWS_DEV, COLS_DEV), 0)
    kd = q * COLS_DEV + iota((ROWS_DEV, COLS_DEV), 1)
    fs, fd = signed(ks, NS), signed(kd, ND)
    wave = (2.0 * math.pi) * jnp.sqrt(fs * fs + fd * fd)
    grow = jnp.exp(-0.15 * wave)
    ang = 0.9 * wave
    return grow * jnp.cos(ang), grow * jnp.sin(ang)


def memory_part(z_re, z_im, history, q):
    w_re, w_im = 0.5 * z_re, 0.5 * z_im
    m_re, m_im = w_re * history(0, 0), w_re * history(0, 1)
    for lag in range(1, 8):
        w_re, w_im = w_re * z_re - w_im * z_im, w_re * z_im + w_im * z_re
        m_re = m_re + w_re * history(lag, 0)
        m_im = m_im + w_re * history(lag, 1)
    both = jnp.concatenate([m_re, m_im], axis=0)
    shifted = pltpu.roll(both, COLS_DEV - 1, 1)
    near = [both[:, PS * i : PS * (i + 1)] for i in range(4)]
    far = [shifted[:, PS * i : PS * (i + 1)] for i in range(4)]
    blocks = [jnp.where(q < 2, near[i], far[3 - i]) for i in range(4)]
    row = iota((PS, PS), 0)
    perm = (iota((PS, PS), 1) == jnp.where(q < 2, row, PS - 1 - row)).astype(f32).astype(bf16)
    out = []
    for h in range(2):
        hi, lo = split(jnp.concatenate(blocks[2 * h : 2 * h + 2], axis=0))
        out.append(dot(perm, hi, NT) + dot(perm, lo, NT))
    return out


def near_kernel(history_in, tables_in, turns_in, own, mem, sums, perm, tables, turns, history, sems):
    p, q = position()
    lags = history.shape[0]
    far_tables = [
        pltpu.make_async_copy(tables_in, tables, sems.at[lags]),
        pltpu.make_async_copy(turns_in, turns, sems.at[lags + 1]),
    ]
    copies = [pltpu.make_async_copy(history_in.at[i], history.at[i], sems.at[i]) for i in range(lags)]
    for copy in far_tables + copies:
        copy.start()
    z_re, z_im = memory_weights(p, q)
    perm[...] = interleave(1)
    for copy in far_tables:
        copy.wait()
    sums[...] = dip_forward_part(own[...], perm[...], tables, lambda i, row: turns[i, pl.ds(row, 1), :], q)

    def read(lag, part):
        if part == 0:
            copies[lag].wait()
        return history[lag, part]

    for h, part in enumerate(memory_part(z_re, z_im, read, q)):
        mem[PS * h : PS * (h + 1), :] = part


def send_kernel(other, mem, sums, perm, tables, turns, out):
    q = position()[1]
    far = dip_forward_part(other[...], perm[...], tables, lambda i, row: turns[i, pl.ds(row, 1), :], q ^ 1)
    lines = slip_part(sums[...] + far, q)
    for h in range(2):
        out[pl.ds(h, PS, stride=SEND), :] = lines[h]
        out[pl.ds(2 + h, PS, stride=SEND), :] = mem[PS * h : PS * (h + 1), :]


def spectral_factor(p, q):
    n = PS
    lane = iota((n, n), 1)
    fs = signed(rev_bits(iota((n, n), 0)) + PS * (lane & 31), NS)
    fs = fs * fs
    parity, slot = lane >> 6, (lane >> 5) & 1
    factor = []
    for h in range(2):
        ell = p + PS * (2 * h + parity)
        kd = jnp.where(outer_modes(ell, q), jnp.where((ell == 0) & (slot == 1), 2 * COLS_DEV, ell), COLS_DEV + ell)
        fd = kd.astype(f32) * (1.0 / ND)
        wave = (2.0 * math.pi) * jnp.sqrt(fs + fd * fd)
        factor.append((-0.5 * SCALE) * wave)
    return jnp.concatenate(factor, axis=0)


def strike_part(lines, mems, factor, first, first_t, twiddle, second, mem_table, p, q):
    n = PS
    w = []
    for h in range(2):
        m_hi, m_lo = split(mems[h])
        alone = jnp.where((p == 0) & ((q & 1) == 0), 2, 0) if h == 0 else 0
        table = mem_table(alone + (q >> 1))
        w.append(dot(m_hi, table) + dot(m_lo, table))
    w = jnp.concatenate(w, axis=0)
    a = dot_table_data(first[0], first[1], jnp.concatenate(lines, axis=1))
    tc, ts = twiddle[0], twiddle[1]
    b = []
    for h in range(2):
        a_re, a_im = a[:n, n * h : n * (h + 1)], a[n:, n * h : n * (h + 1)]
        b.append(jnp.concatenate([a_re * tc + a_im * ts, a_im * tc - a_re * ts], axis=1))
    spec = dot_data_table(jnp.concatenate(b, axis=0), second[0], second[1])
    g = jnp.concatenate([factor, factor], axis=1) * (SCALE * spec - w)
    b = dot_data_turned(g, second[0], second[1])
    turned = []
    for h in range(2):
        b_re, b_im = b[n * h : n * (h + 1), :n], b[n * h : n * (h + 1), n:]
        turned.append(jnp.concatenate([b_re * tc - b_im * ts, b_re * ts + b_im * tc], axis=0))
    return dot_table_data(first_t[0], first_t[1], jnp.concatenate(turned, axis=1))


def strike_kernel(recv, outbox, factor, first, first_t, twiddle, second, mem_table, out):
    t = strike_part(
        [recv[pl.ds(h, PS, stride=SEND), :] for h in range(2)],
        [recv[pl.ds(2 + h, PS, stride=SEND), :] for h in range(2)],
        factor[...],
        first,
        first_t,
        twiddle,
        second,
        lambda i: mem_table[i],
        *position(),
    )
    for h in range(2):
        out[pl.ds(h, PS, stride=BACK), :] = t[:, PS * h : PS * (h + 1)]
    out[pl.ds(2, PS, stride=BACK), :] = outbox[...]


def route_part(dest, node, value, count):
    dest = [dest[:, CHUNK * i : CHUNK * (i + 1)] for i in range(ROWS // CHUNK)]
    upto = (iota((CHUNK, CHUNK), 0) <= iota((CHUNK, CHUNK), 1)).astype(f32).astype(bf16)
    carry = jnp.zeros((PS, 1), f32)
    box = jnp.zeros((PS, 2 * CAP), f32)
    ranks = []
    for i in range(ROWS // CHUNK):
        cut = slice(CHUNK * i, CHUNK * (i + 1))
        named = iota((PS, CHUNK), 0) == dest[i]
        onehot = named.astype(f32).astype(bf16)
        upto_here = dot(onehot, upto) + carry
        rank = jnp.sum(jnp.where(named, upto_here, 0.0), axis=0, keepdims=True).astype(jnp.int32) - 1
        carry = upto_here[:, CHUNK - 1 : CHUNK]
        ranks.append(rank)
        live = (CHUNK * i + iota((1, CHUNK), 1)) < count
        v = jnp.where(live, value[:, cut], 0.0)
        v_hi = v.astype(bf16).astype(f32)
        v_lo = v - v_hi
        at = node[:, cut]
        n_hi = ((((at >> 7) & 3) << 5) + (at >> 9)) << 7
        n_lo = at & 127
        here = iota((CAP, CHUNK), 0) == rank
        part_1 = jnp.concatenate([jnp.where(here, v_hi, 0.0), jnp.where(here, n_hi.astype(f32), 0.0)], axis=0)
        part_2 = jnp.concatenate([jnp.where(here, v_lo, 0.0), jnp.where(here, n_lo.astype(f32), 0.0)], axis=0)
        box = box + (dot(onehot, part_1.astype(bf16), NT) + dot(onehot, part_2.astype(bf16), NT))
    return box, jnp.concatenate(ranks, axis=1)


def route_kernel(count, tables, dest, node, value, out, rank, perm, turned, factor):
    out[...], rank[...] = route_part(dest[...], node[...], value[...], count[0, 0])
    perm[...] = interleave(0)
    for i in range(4):
        turned[i] = tables[i].astype(f32).T.astype(bf16)
    factor[...] = spectral_factor(*position())


def dip_inverse_part(lines, tables, turns, perm, q):
    lines = [x.T for x in lines]
    t0, t1 = [
        jnp.concatenate([lines[i >> 1][64 * (i & 1) + 32 * slot : 64 * (i & 1) + 32 * slot + 32] for i in range(4)], axis=1)
        for slot in range(2)
    ]
    ell = iota((ROWS_DEV, COLS_DEV), 1)
    outer = outer_modes(ell, q)
    total, diff = t0 + t1, t0 - t1
    s1, d1 = jnp.where(outer, total, 0.0), jnp.where(outer, diff, 0.0)
    s2, d2 = total - s1, diff - d1
    fix = jnp.where(outer & (ell == 0), 2.0 * t1, 0.0)
    even = [s1 + s2, s1 + d2 - fix, s1 - s2, s1 - d2 - fix]
    odd = [d1 + d2, d1 - s2, d1 - d2, d1 + s2]
    evens, odds = [], []
    for i, (ct, st) in enumerate(turn_rows(turns, 0)):
        evens.append(ct * even[i] + st * odd[i])
        odds.append(ct * odd[i] - st * even[i])
    evens, odds = split(jnp.concatenate(evens, axis=0)), split(jnp.concatenate(odds, axis=0))
    turn = iota((1, COLS_DEV), 1) & 3
    keep_even = jnp.where((turn & 1) == 0, 1.0, 0.0).astype(bf16)
    keep_odd = jnp.where((turn & 1) == 1, 1.0, 0.0).astype(bf16)
    flip_even = jnp.where(turn == 0, 1.0, jnp.where(turn == 2, -1.0, 0.0)).astype(bf16)
    flip_odd = jnp.where(turn == 1, 1.0, jnp.where(turn == 3, -1.0, 0.0)).astype(bf16)
    f = 0.0
    for k, x, y, sign in ((0, evens, odds, flip_odd), (2, odds, evens, -flip_odd)):
        hi, lo = [
            jnp.concatenate([x[i] * keep_even, x[i] * keep_odd, x[i] * flip_even, y[i] * sign], axis=0) for i in range(2)
        ]
        f = f + (dot(hi, tables[k]) + (dot(lo, tables[k]) + dot(hi, tables[k + 1])))
    f = [f[PS * i : PS * (i + 1)] for i in range(4)]
    f = [f[0] + f[1], f[2] + f[3], f[0] - f[1], f[2] - f[3]]
    rows = 32
    f = jnp.concatenate([jnp.concatenate([x[rows * i : rows * (i + 1)] for i in range(4)], axis=1) for x in f], axis=0)
    hi, lo = split(f)
    f = dot(hi, perm) + dot(lo, perm)
    return [f[rows * qd : rows * (qd + 1)] for qd in range(QD)]


def dip_kernel(recv, perm, tables, turns, out):
    lines = [recv[pl.ds(h, PS, stride=BACK), :] for h in range(2)]
    shares = dip_inverse_part(lines, tables, lambda i, row: turns[i, row : row + 1, :], perm[...], position()[1])
    for qd, share in enumerate(shares):
        out[qd] = share


def unpack_rows(fe, roll):
    top, bot = fe[0:CAP], fe[CAP:PS]
    left = iota((CAP, PS), 1) < CAP
    value = jnp.where(left, top, roll(bot))
    node = jnp.where(left, roll(top), bot).astype(jnp.int32)
    return value, node >> 7, node & 127


def lanes_of(x, group):
    return jnp.concatenate([x[4 * group + i : 4 * group + i + 1] for i in range(4)], axis=1)


def column_onehot(lo):
    return (iota((PS, CHUNK), 0) == lo).astype(f32).astype(bf16)


def traction_step(value, hi, onehot):
    named = iota((PS, CHUNK), 0) == hi
    v_hi = value.astype(bf16).astype(f32)
    rows = jnp.concatenate([jnp.where(named, v_hi, 0.0), jnp.where(named, value - v_hi, 0.0)], axis=0).astype(bf16)
    return dot(rows, onehot, NT)


def sample_step(rate_parts, hi, onehot):
    got = dot(rate_parts, jnp.concatenate([onehot, onehot], axis=0))
    return jnp.sum(jnp.where(iota((PS, CHUNK), 0) == hi, got, 0.0), axis=0, keepdims=True)


def roll_half(x):
    return pltpu.roll(x, CAP, 1)


def traction_kernel(recv, traction, onehots, spots):
    value, hi, lo = unpack_rows(recv[pl.ds(2, PS, stride=BACK), :], roll_half)
    spots[...] = hi
    acc = jnp.zeros((2 * PS, PS), f32)
    for g in range(CAP // 4):
        onehot = column_onehot(lanes_of(lo, g))
        onehots[g] = onehot
        acc = acc + traction_step(lanes_of(value, g), lanes_of(hi, g), onehot)
    acc = acc[:PS] + acc[PS:]
    traction[...] = jnp.concatenate([acc[32 * i : 32 * i + 32] for i in range(4)], axis=1)


def owner_kernel(
    shares, traction, onehots, spots, slip, rate, prestress, normal, flag, new_rate_out, stress_out, sampled, new_rate, stress, sems
):
    f = (shares[0] + shares[1]) + (shares[2] + shares[3])
    slip_new = slip[...] + RATE_DT * rate[...]
    total = prestress[...] + f + traction[...]
    strength = normal[...] * (0.6 - (0.6 - 0.4) * jnp.minimum(slip_new, 1.0))
    fresh = jnp.where(flag[...] == 1, jnp.maximum(total - strength, 0.0) * 2.0, 0.0)
    stress[...] = total
    new_rate[...] = fresh
    copies = [
        pltpu.make_async_copy(new_rate, new_rate_out, sems.at[0]),
        pltpu.make_async_copy(stress, stress_out, sems.at[1]),
    ]
    for copy in copies:
        copy.start()
    stacked = jnp.concatenate([fresh[:, PS * i : PS * (i + 1)] for i in range(4)], axis=0)
    parts = jnp.concatenate(split(stacked), axis=1)
    hi = spots[...]
    for g in range(CAP // 4):
        got = sample_step(parts, lanes_of(hi, g), onehots[g])
        for i in range(4):
            sampled[4 * g + i : 4 * g + i + 1, :] = got[:, PS * i : PS * (i + 1)]
    sampled[CAP:PS, :] = roll_half(sampled[0:CAP, :])
    for copy in copies:
        copy.wait()


def return_part(got, dest, rank, count):
    parts = jnp.concatenate(split(got.T[:CAP]), axis=1)
    out = []
    for i in range(ROWS // CHUNK):
        cut = slice(CHUNK * i, CHUNK * (i + 1))
        onehot = (iota((PS, CHUNK), 0) == dest[:, cut]).astype(f32).astype(bf16)
        here = dot(parts, jnp.concatenate([onehot, onehot], axis=0))
        here = jnp.sum(jnp.where(iota((CAP, CHUNK), 0) == rank[:, cut], here, 0.0), axis=0, keepdims=True)
        live = (CHUNK * i + iota((1, CHUNK), 1)) < count
        out.append(jnp.where(live, here, 0.0))
    return jnp.concatenate(out, axis=1)


def return_kernel(count, got, rank, dest, out):
    out[...] = return_part(got[...], dest[...], rank[...], count[0, 0])


def call(kernel, out_shape, operands, name, scalars=(), args=(), far=(), far_outs=0, scratch=()):
    spec = pl.BlockSpec(memory_space=pltpu.VMEM)
    hbm = pl.BlockSpec(memory_space=pltpu.HBM)
    in_specs = [pl.BlockSpec(memory_space=pltpu.SMEM)] * len(scalars) + [hbm] * len(far) + [spec] * (len(operands) + len(args))
    outs = tuple(hbm if i < far_outs else spec for i in range(len(out_shape))) if isinstance(out_shape, tuple) else spec
    far = [pltpu.with_memory_space_constraint(x, pltpu.HBM) for x in far]
    operands = [pltpu.with_memory_space_constraint(x, pltpu.VMEM) for x in operands]
    return pl.pallas_call(
        kernel,
        out_shape=out_shape,
        in_specs=in_specs,
        out_specs=outs,
        name=name,
        scratch_shapes=scratch,
        compiler_params=pltpu.CompilerParams(vmem_limit_bytes=VMEM_LIMIT),
    )(*scalars, *far, *operands, *args)


def sds(shape, dtype=f32):
    return pltpu.VMEM(shape, dtype)


def over_strike(x, width):
    unit = width if width in (1, 2, 4) else 1
    return lax.all_to_all(x.reshape(PS * width // unit, unit, PS), STRIKE, 0, 0, tiled=True).reshape(PS * width, PS)


def body(slip, rate, prestress, normal_stress, history, fric_flag, row_dest, row_node, fe_traction, fe_count):
    tables, turns = [jnp.asarray(t) for t in dip_tables()]
    strike = [jnp.asarray(t) for t in strike_tables()] + [jnp.asarray(memory_tables())]
    dest = row_dest.reshape(1, ROWS)

    slip_new = slip + RATE_DT * rate
    other = lax.ppermute(slip_new, "dip", [(i, i ^ 1) for i in range(QD)])
    mem, sums, perm, tables, turns = call(
        near_kernel,
        (
            sds((2 * PS, PS)),
            sds((8 * ROWS_DEV, COLS_DEV)),
            sds((COLS_DEV, COLS_DEV), bf16),
            sds(tables.shape, bf16),
            sds(turns.shape),
        ),
        (slip_new,),
        "near",
        far=(history, tables, turns),
        scratch=[sds(history.shape), pltpu.SemaphoreType.DMA((history.shape[0] + 2,))],
    )
    sent = call(send_kernel, sds((PS * SEND, PS)), (other, mem, sums, perm, tables, turns), "send")
    recv = over_strike(sent, SEND)
    box, rank, perm, turned, factor = call(
        route_kernel,
        (
            sds((PS, PS)),
            sds((1, ROWS), jnp.int32),
            sds((COLS_DEV, COLS_DEV), bf16),
            sds((4, COLS_DEV, COLS_DEV // 4), bf16),
            sds((2 * PS, PS)),
        ),
        (tables,),
        "route",
        (fe_count,),
        (dest, row_node, fe_traction),
    )
    sent = call(strike_kernel, sds((PS * BACK, PS)), (recv, box, factor), "strike", args=strike)
    recv = over_strike(sent, BACK)
    shares = call(dip_kernel, sds((QD, ROWS_DEV, COLS_DEV)), (recv, perm, turned, turns), "dip")
    shares = lax.all_to_all(shares, "dip", 0, 0, tiled=True)
    traction, onehots, spots = call(
        traction_kernel,
        (sds(slip.shape), sds((CAP // 4, PS, CHUNK), bf16), sds((CAP, PS), jnp.int32)),
        (recv,),
        "traction",
    )
    new_rate, stress, sampled = call(
        owner_kernel,
        (jax.ShapeDtypeStruct(slip.shape, f32), jax.ShapeDtypeStruct(slip.shape, f32), sds((PS, PS))),
        (shares, traction, onehots, spots),
        "owner",
        args=(slip, rate, prestress, normal_stress, fric_flag),
        far_outs=2,
        scratch=[sds(slip.shape), sds(slip.shape), pltpu.SemaphoreType.DMA((2,))],
    )
    got = over_strike(sampled, 1)
    fe_rate = call(return_kernel, jax.ShapeDtypeStruct((1, ROWS), f32), (got, rank), "back", (fe_count,), (dest,))
    return new_rate, stress, fe_rate


def solution(mesh):
    fine = Mesh(mesh.devices.reshape(8, 8, 2, 4), ("z", "y", "c", "dip"))
    field = P(STRIKE, "dip")
    rows = P("dip", STRIKE)
    in_specs = (field, field, field, field, P(None, None, STRIKE, "dip"), field, P("dip", STRIKE, None), rows, rows, rows)
    return jax.shard_map(body, mesh=fine, in_specs=in_specs, out_specs=(field, field, rows), check_vma=False)
```

```python
import math

import jax
import jax.numpy as jnp
import numpy as np
from jax import lax
from jax.experimental import pallas as pl
from jax.experimental.pallas import tpu as pltpu
from jax.sharding import Mesh
from jax.sharding import PartitionSpec as P

NS, ND = 4096, 2048
PS, QD = 128, 4
ROWS_DEV, COLS_DEV = NS // PS, ND // QD
RATE_DT = 0.5
LEVELS = 7
CAP = 64
ROWS = 4096
CHUNK = 512
VMEM_LIMIT = 24 << 20
STRIKE = ("z", "y", "c")
SEND, BACK = 4, 3
SCALE = 1.0 / math.sqrt(NS * ND)
bf16 = jnp.bfloat16
f32 = jnp.float32
NN = (((1,), (0,)), ((), ()))
NT = (((1,), (1,)), ((), ()))


def np_split(table):
    hi = table.astype(np.float32).astype(jnp.bfloat16)
    lo = (table - hi.astype(np.float64)).astype(np.float32).astype(jnp.bfloat16)
    return np.stack([hi, lo])


def np_rev(p):
    return sum(((p >> b) & 1) << (LEVELS - 1 - b) for b in range(LEVELS))


def dip_tables():
    ell = np.arange(COLS_DEV)
    ang = 2 * np.pi * ((np.arange(COLS_DEV // 4)[:, None] * ell[None, :]) % COLS_DEV) / COLS_DEV
    b = np.tile(np.arange(4), QD)[:, None]
    q = np.repeat(np.arange(QD), 4)[:, None]
    turn = 2 * np.pi * ((ell * b + COLS_DEV * q * ell) % ND) / ND
    tables = np.concatenate([np_split(np.cos(ang)), np_split(np.sin(ang))])
    return tables, np.stack([np.cos(turn), np.sin(turn)]).astype(np.float32)


def strike_tables():
    p = np.arange(PS)
    k1 = np_rev(p)
    ang = 2 * np.pi * ((k1[:, None] * p[None, :]) % PS) / PS
    first = np.concatenate([np.cos(ang), -np.sin(ang)])
    r = np.arange(ROWS_DEV)
    tw = 2 * np.pi * (k1[:, None] * r[None, :]) / NS
    twiddle = np.stack([np.tile(np.cos(tw), (1, 4)), np.tile(np.sin(tw), (1, 4))]).astype(np.float32)
    small = 2 * np.pi * ((r[:, None] * r[None, :]) % ROWS_DEV) / ROWS_DEV
    cb = np.kron(np.eye(4), np.cos(small))
    sb = np.kron(np.eye(4), np.sin(small))
    second = np.block([[cb, -sb], [sb, cb]])
    return np_split(first), np_split(first.T), twiddle, np_split(second)


def memory_tables():
    out = np.zeros((4, 2, 2, 32, 2, 2, 2, 32), np.float32)
    eye = np.eye(ROWS_DEV)
    for case in range(4):
        own = case & 1
        for parity in range(2):
            other = own if case >= 2 and parity == 0 else 1 - own
            for slot, part, w_re, w_im in ((own, 0, 0.5, 0.5), (own, 1, -0.5, 0.5), (other, 0, 0.5, -0.5), (other, 1, 0.5, 0.5)):
                out[case, parity, part, :, 0, parity, slot, :] += w_re * eye
                out[case, parity, part, :, 1, parity, slot, :] += w_im * eye
    return out.reshape(4, PS, 2 * PS).astype(jnp.bfloat16)


def dot(a, b, dims=NN):
    return lax.dot_general(a, b, dims, preferred_element_type=f32)


def split(x):
    hi = x.astype(bf16)
    return hi, (x - hi.astype(f32)).astype(bf16)


def dot_data_table(x, t_hi, t_lo):
    hi, lo = split(x)
    return dot(hi, t_hi) + (dot(lo, t_hi) + dot(hi, t_lo))


def dot_data_turned(x, t_hi, t_lo):
    hi, lo = split(x)
    return dot(hi, t_hi, NT) + (dot(lo, t_hi, NT) + dot(hi, t_lo, NT))


def dot_table_data(t_hi, t_lo, x):
    hi, lo = split(x)
    return dot(t_hi, hi) + (dot(t_hi, lo) + dot(t_lo, hi))


def iota(shape, dim):
    return lax.broadcasted_iota(jnp.int32, shape, dim)


def position():
    return lax.axis_index(STRIKE), lax.axis_index("dip")


def rev_bits(p):
    out = 0
    for b in range(LEVELS):
        out = out + (((p >> b) & 1) << (LEVELS - 1 - b))
    return out


def turn_rows(turns, q):
    return [(turns(0, 4 * q + b), turns(1, 4 * q + b)) for b in range(4)]


def interleave(dims):
    pos = iota((COLS_DEV, COLS_DEV), dims)
    return (iota((COLS_DEV, COLS_DEV), 1 - dims) == 4 * (pos & (PS - 1)) + (pos >> 7)).astype(f32).astype(bf16)


def by_class(x):
    return jnp.concatenate([x[:, PS * b : PS * (b + 1)] for b in range(4)], axis=0)


def signed(freq, length):
    return jnp.where(freq >= length // 2, freq - length, freq).astype(f32) * (1.0 / length)


def outer_modes(ell, q):
    return jnp.where(ell == 0, 1 - (q & 1), 1 - ((q ^ (q >> 1)) & 1)) == 1


def dip_forward_part(x, perm, tables, turns, q):
    parts = dot(jnp.concatenate(split(x), axis=0), perm).astype(bf16)
    hi, lo = by_class(parts[:ROWS_DEV]), by_class(parts[ROWS_DEV:])
    c = dot(hi, tables[0]) + (dot(lo, tables[0]) + dot(hi, tables[1]))
    s = dot(hi, tables[2]) + (dot(lo, tables[2]) + dot(hi, tables[3]))
    cs, ss = [], []
    for b, (ct, st) in enumerate(turn_rows(turns, q)):
        c_b, s_b = c[32 * b : 32 * b + 32], s[32 * b : 32 * b + 32]
        cs.append(ct * c_b - st * s_b)
        ss.append(st * c_b + ct * s_b)
    return jnp.concatenate(cs + ss, axis=0)


def slip_part(sums, q):
    sums = [sums[32 * i : 32 * i + 32] for i in range(8)]
    cs, ss = sums[:4], sums[4:]
    c_even, c_odd = cs[0] + cs[2], cs[1] + cs[3]
    s_sum = (ss[0] + ss[2]) + (ss[1] + ss[3])
    ell = iota((ROWS_DEV, COLS_DEV), 1)
    h_a = (c_even + c_odd) + s_sum
    h_d = (c_even + jnp.where(ell == 0, -c_odd, c_odd)) - s_sum
    even = cs[0] - cs[2] + ss[3] - ss[1]
    odd = ss[0] - ss[2] + cs[1] - cs[3]
    outer = outer_modes(ell, q)
    both = jnp.concatenate([jnp.where(outer, h_a, even + odd), jnp.where(outer, h_d, even - odd)], axis=0)
    both = [both[:, PS * i : PS * (i + 1)] for i in range(4)]
    return [jnp.concatenate(both[2 * h : 2 * h + 2], axis=0).T for h in range(2)]


def memory_weights(p, q):
    ks = rev_bits(p) + PS * iota((ROWS_DEV, COLS_DEV), 0)
    kd = q * COLS_DEV + iota((ROWS_DEV, COLS_DEV), 1)
    fs, fd = signed(ks, NS), signed(kd, ND)
    wave = (2.0 * math.pi) * jnp.sqrt(fs * fs + fd * fd)
    grow = jnp.exp(-0.15 * wave)
    ang = 0.9 * wave
    return grow * jnp.cos(ang), grow * jnp.sin(ang)


def memory_part(z_re, z_im, history, q):
    w_re, w_im = 0.5 * z_re, 0.5 * z_im
    m_re, m_im = w_re * history(0, 0), w_re * history(0, 1)
    for lag in range(1, 8):
        w_re, w_im = w_re * z_re - w_im * z_im, w_re * z_im + w_im * z_re
        m_re = m_re + w_re * history(lag, 0)
        m_im = m_im + w_re * history(lag, 1)
    both = jnp.concatenate([m_re, m_im], axis=0)
    shifted = pltpu.roll(both, COLS_DEV - 1, 1)
    near = [both[:, PS * i : PS * (i + 1)] for i in range(4)]
    far = [shifted[:, PS * i : PS * (i + 1)] for i in range(4)]
    blocks = [jnp.where(q < 2, near[i], far[3 - i]) for i in range(4)]
    row = iota((PS, PS), 0)
    perm = (iota((PS, PS), 1) == jnp.where(q < 2, row, PS - 1 - row)).astype(f32).astype(bf16)
    out = []
    for h in range(2):
        hi, lo = split(jnp.concatenate(blocks[2 * h : 2 * h + 2], axis=0))
        out.append(dot(perm, hi, NT) + dot(perm, lo, NT))
    return out


def near_kernel(history_in, tables_in, turns_in, own, mem, sums, perm, tables, turns, history, sems):
    p, q = position()
    lags = history.shape[0]
    far_tables = [
        pltpu.make_async_copy(tables_in, tables, sems.at[lags]),
        pltpu.make_async_copy(turns_in, turns, sems.at[lags + 1]),
    ]
    copies = [pltpu.make_async_copy(history_in.at[i], history.at[i], sems.at[i]) for i in range(lags)]
    for copy in far_tables + copies:
        copy.start()
    z_re, z_im = memory_weights(p, q)
    perm[...] = interleave(1)
    for copy in far_tables:
        copy.wait()
    sums[...] = dip_forward_part(own[...], perm[...], tables, lambda i, row: turns[i, pl.ds(row, 1), :], q)

    def read(lag, part):
        if part == 0:
            copies[lag].wait()
        return history[lag, part]

    for h, part in enumerate(memory_part(z_re, z_im, read, q)):
        mem[PS * h : PS * (h + 1), :] = part


def send_kernel(other, mem, sums, perm, tables, turns, out):
    q = position()[1]
    far = dip_forward_part(other[...], perm[...], tables, lambda i, row: turns[i, pl.ds(row, 1), :], q ^ 1)
    lines = slip_part(sums[...] + far, q)
    for h in range(2):
        out[pl.ds(h, PS, stride=SEND), :] = lines[h]
        out[pl.ds(2 + h, PS, stride=SEND), :] = mem[PS * h : PS * (h + 1), :]


def spectral_factor(p, q):
    n = PS
    lane = iota((n, n), 1)
    fs = signed(rev_bits(iota((n, n), 0)) + PS * (lane & 31), NS)
    fs = fs * fs
    parity, slot = lane >> 6, (lane >> 5) & 1
    factor = []
    for h in range(2):
        ell = p + PS * (2 * h + parity)
        kd = jnp.where(outer_modes(ell, q), jnp.where((ell == 0) & (slot == 1), 2 * COLS_DEV, ell), COLS_DEV + ell)
        fd = kd.astype(f32) * (1.0 / ND)
        wave = (2.0 * math.pi) * jnp.sqrt(fs + fd * fd)
        factor.append((-0.5 * SCALE) * wave)
    return jnp.concatenate(factor, axis=0)


def strike_part(lines, mems, factor, first, first_t, twiddle, second, mem_table, p, q):
    n = PS
    w = []
    for h in range(2):
        m_hi, m_lo = split(mems[h])
        alone = jnp.where((p == 0) & ((q & 1) == 0), 2, 0) if h == 0 else 0
        table = mem_table(alone + (q >> 1))
        w.append(dot(m_hi, table) + dot(m_lo, table))
    w = jnp.concatenate(w, axis=0)
    a = dot_table_data(first[0], first[1], jnp.concatenate(lines, axis=1))
    tc, ts = twiddle[0], twiddle[1]
    b = []
    for h in range(2):
        a_re, a_im = a[:n, n * h : n * (h + 1)], a[n:, n * h : n * (h + 1)]
        b.append(jnp.concatenate([a_re * tc + a_im * ts, a_im * tc - a_re * ts], axis=1))
    spec = dot_data_table(jnp.concatenate(b, axis=0), second[0], second[1])
    g = jnp.concatenate([factor, factor], axis=1) * (SCALE * spec - w)
    b = dot_data_turned(g, second[0], second[1])
    turned = []
    for h in range(2):
        b_re, b_im = b[n * h : n * (h + 1), :n], b[n * h : n * (h + 1), n:]
        turned.append(jnp.concatenate([b_re * tc - b_im * ts, b_re * ts + b_im * tc], axis=0))
    return dot_table_data(first_t[0], first_t[1], jnp.concatenate(turned, axis=1))


def strike_kernel(recv, outbox, factor, first, first_t, twiddle, second, mem_table, out):
    t = strike_part(
        [recv[pl.ds(h, PS, stride=SEND), :] for h in range(2)],
        [recv[pl.ds(2 + h, PS, stride=SEND), :] for h in range(2)],
        factor[...],
        first,
        first_t,
        twiddle,
        second,
        lambda i: mem_table[i],
        *position(),
    )
    for h in range(2):
        out[pl.ds(h, PS, stride=BACK), :] = t[:, PS * h : PS * (h + 1)]
    out[pl.ds(2, PS, stride=BACK), :] = outbox[...]


def route_part(dest, node, value, count):
    dest = [dest[:, CHUNK * i : CHUNK * (i + 1)] for i in range(ROWS // CHUNK)]
    upto = (iota((CHUNK, CHUNK), 0) <= iota((CHUNK, CHUNK), 1)).astype(f32).astype(bf16)
    carry = jnp.zeros((PS, 1), f32)
    box = jnp.zeros((PS, 2 * CAP), f32)
    ranks = []
    for i in range(ROWS // CHUNK):
        cut = slice(CHUNK * i, CHUNK * (i + 1))
        named = iota((PS, CHUNK), 0) == dest[i]
        onehot = named.astype(f32).astype(bf16)
        upto_here = dot(onehot, upto) + carry
        rank = jnp.sum(jnp.where(named, upto_here, 0.0), axis=0, keepdims=True).astype(jnp.int32) - 1
        carry = upto_here[:, CHUNK - 1 : CHUNK]
        ranks.append(rank)
        live = (CHUNK * i + iota((1, CHUNK), 1)) < count
        v = jnp.where(live, value[:, cut], 0.0)
        v_hi = v.astype(bf16).astype(f32)
        v_lo = v - v_hi
        at = node[:, cut]
        n_hi = ((((at >> 7) & 3) << 5) + (at >> 9)) << 7
        n_lo = at & 127
        here = iota((CAP, CHUNK), 0) == rank
        part_1 = jnp.concatenate([jnp.where(here, v_hi, 0.0), jnp.where(here, n_hi.astype(f32), 0.0)], axis=0)
        part_2 = jnp.concatenate([jnp.where(here, v_lo, 0.0), jnp.where(here, n_lo.astype(f32), 0.0)], axis=0)
        box = box + (dot(onehot, part_1.astype(bf16), NT) + dot(onehot, part_2.astype(bf16), NT))
    return box, jnp.concatenate(ranks, axis=1)


def route_kernel(count, tables, dest, node, value, out, rank, perm, turned, factor):
    out[...], rank[...] = route_part(dest[...], node[...], value[...], count[0, 0])
    perm[...] = interleave(0)
    for i in range(4):
        turned[i] = tables[i].astype(f32).T.astype(bf16)
    factor[...] = spectral_factor(*position())


def dip_inverse_part(lines, tables, turns, q):
    lines = [x.T for x in lines]
    t0, t1 = [
        jnp.concatenate([lines[i >> 1][64 * (i & 1) + 32 * slot : 64 * (i & 1) + 32 * slot + 32] for i in range(4)], axis=1)
        for slot in range(2)
    ]
    ell = iota((ROWS_DEV, COLS_DEV), 1)
    outer = outer_modes(ell, q)
    total, diff = t0 + t1, t0 - t1
    s1, d1 = jnp.where(outer, total, 0.0), jnp.where(outer, diff, 0.0)
    s2, d2 = total - s1, diff - d1
    fix = jnp.where(outer & (ell == 0), 2.0 * t1, 0.0)
    even = [s1 + s2, s1 + d2 - fix, s1 - s2, s1 - d2 - fix]
    odd = [d1 + d2, d1 - s2, d1 - d2, d1 + s2]
    evens, odds = [], []
    for i, (ct, st) in enumerate(turn_rows(turns, 0)):
        evens.append(ct * even[i] + st * odd[i])
        odds.append(ct * odd[i] - st * even[i])
    evens, odds = split(jnp.concatenate(evens, axis=0)), split(jnp.concatenate(odds, axis=0))
    turn = iota((1, COLS_DEV), 1) & 3
    keep_even = jnp.where((turn & 1) == 0, 1.0, 0.0).astype(bf16)
    keep_odd = jnp.where((turn & 1) == 1, 1.0, 0.0).astype(bf16)
    flip_even = jnp.where(turn == 0, 1.0, jnp.where(turn == 2, -1.0, 0.0)).astype(bf16)
    flip_odd = jnp.where(turn == 1, 1.0, jnp.where(turn == 3, -1.0, 0.0)).astype(bf16)
    f = 0.0
    for k, x, y, sign in ((0, evens, odds, flip_odd), (2, odds, evens, -flip_odd)):
        hi, lo = [
            jnp.concatenate([x[i] * keep_even, x[i] * keep_odd, x[i] * flip_even, y[i] * sign], axis=0) for i in range(2)
        ]
        f = f + (dot(hi, tables[k]) + (dot(lo, tables[k]) + dot(hi, tables[k + 1])))
    f = [f[PS * i : PS * (i + 1)] for i in range(4)]
    f = [f[0] + f[1], f[2] + f[3], f[0] - f[1], f[2] - f[3]]
    rows = 32
    f = jnp.concatenate([jnp.concatenate([x[rows * i : rows * (i + 1)] for i in range(4)], axis=1) for x in f], axis=0)
    hi, lo = split(f)
    return hi, lo


def dip_kernel(recv, perm, tables, turns, out, halves, sems):
    lines = [recv[pl.ds(h, PS, stride=BACK), :] for h in range(2)]
    hi, lo = dip_inverse_part(lines, tables, lambda i, row: turns[i, row : row + 1, :], position()[1])
    half = COLS_DEV // 2
    copies = []
    for i in range(2):
        cols = perm[:, half * i : half * (i + 1)]
        share = dot(hi, cols) + dot(lo, cols)
        for qd in range(QD):
            halves[i, qd] = share[ROWS_DEV * qd : ROWS_DEV * (qd + 1)]
        copies.append(pltpu.make_async_copy(halves.at[i], out.at[:, :, pl.ds(half * i, half)], sems.at[i]))
        copies[i].start()
    for copy in copies:
        copy.wait()


def unpack_rows(fe, roll):
    top, bot = fe[0:CAP], fe[CAP:PS]
    left = iota((CAP, PS), 1) < CAP
    value = jnp.where(left, top, roll(bot))
    node = jnp.where(left, roll(top), bot).astype(jnp.int32)
    return value, node >> 7, node & 127


def lanes_of(x, group):
    return jnp.concatenate([x[4 * group + i : 4 * group + i + 1] for i in range(4)], axis=1)


def column_onehot(lo):
    return (iota((PS, CHUNK), 0) == lo).astype(f32).astype(bf16)


def traction_step(value, hi, onehot):
    named = iota((PS, CHUNK), 0) == hi
    v_hi = value.astype(bf16).astype(f32)
    rows = jnp.concatenate([jnp.where(named, v_hi, 0.0), jnp.where(named, value - v_hi, 0.0)], axis=0).astype(bf16)
    return dot(rows, onehot, NT)


def sample_step(rate_parts, hi, onehot):
    got = dot(rate_parts, jnp.concatenate([onehot, onehot], axis=0))
    return jnp.sum(jnp.where(iota((PS, CHUNK), 0) == hi, got, 0.0), axis=0, keepdims=True)


def roll_half(x):
    return pltpu.roll(x, CAP, 1)


def traction_kernel(recv, traction, onehots, spots):
    value, hi, lo = unpack_rows(recv[pl.ds(2, PS, stride=BACK), :], roll_half)
    spots[...] = hi
    acc = jnp.zeros((2 * PS, PS), f32)
    for g in range(CAP // 4):
        onehot = column_onehot(lanes_of(lo, g))
        onehots[g] = onehot
        acc = acc + traction_step(lanes_of(value, g), lanes_of(hi, g), onehot)
    acc = acc[:PS] + acc[PS:]
    traction[...] = jnp.concatenate([acc[32 * i : 32 * i + 32] for i in range(4)], axis=1)


def owner_kernel(
    shares, traction, onehots, spots, slip, rate, prestress, normal, flag, new_rate_out, stress_out, sampled, new_rate, stress, sems
):
    f = (shares[0] + shares[1]) + (shares[2] + shares[3])
    slip_new = slip[...] + RATE_DT * rate[...]
    total = prestress[...] + f + traction[...]
    strength = normal[...] * (0.6 - (0.6 - 0.4) * jnp.minimum(slip_new, 1.0))
    fresh = jnp.where(flag[...] == 1, jnp.maximum(total - strength, 0.0) * 2.0, 0.0)
    stress[...] = total
    new_rate[...] = fresh
    copies = [
        pltpu.make_async_copy(new_rate, new_rate_out, sems.at[0]),
        pltpu.make_async_copy(stress, stress_out, sems.at[1]),
    ]
    for copy in copies:
        copy.start()
    stacked = jnp.concatenate([fresh[:, PS * i : PS * (i + 1)] for i in range(4)], axis=0)
    parts = jnp.concatenate(split(stacked), axis=1)
    hi = spots[...]
    for g in range(CAP // 4):
        got = sample_step(parts, lanes_of(hi, g), onehots[g])
        for i in range(4):
            sampled[4 * g + i : 4 * g + i + 1, :] = got[:, PS * i : PS * (i + 1)]
    sampled[CAP:PS, :] = roll_half(sampled[0:CAP, :])
    for copy in copies:
        copy.wait()


def return_part(got, dest, rank, count):
    parts = jnp.concatenate(split(got.T[:CAP]), axis=1)
    out = []
    for i in range(ROWS // CHUNK):
        cut = slice(CHUNK * i, CHUNK * (i + 1))
        onehot = (iota((PS, CHUNK), 0) == dest[:, cut]).astype(f32).astype(bf16)
        here = dot(parts, jnp.concatenate([onehot, onehot], axis=0))
        here = jnp.sum(jnp.where(iota((CAP, CHUNK), 0) == rank[:, cut], here, 0.0), axis=0, keepdims=True)
        live = (CHUNK * i + iota((1, CHUNK), 1)) < count
        out.append(jnp.where(live, here, 0.0))
    return jnp.concatenate(out, axis=1)


def return_kernel(count, got, rank, dest, out):
    out[...] = return_part(got[...], dest[...], rank[...], count[0, 0])


def call(kernel, out_shape, operands, name, scalars=(), args=(), far=(), far_outs=0, scratch=()):
    spec = pl.BlockSpec(memory_space=pltpu.VMEM)
    hbm = pl.BlockSpec(memory_space=pltpu.HBM)
    in_specs = [pl.BlockSpec(memory_space=pltpu.SMEM)] * len(scalars) + [hbm] * len(far) + [spec] * (len(operands) + len(args))
    outs = tuple(hbm if i < far_outs else spec for i in range(len(out_shape))) if isinstance(out_shape, tuple) else hbm if far_outs else spec
    far = [pltpu.with_memory_space_constraint(x, pltpu.HBM) for x in far]
    operands = [pltpu.with_memory_space_constraint(x, pltpu.VMEM) for x in operands]
    return pl.pallas_call(
        kernel,
        out_shape=out_shape,
        in_specs=in_specs,
        out_specs=outs,
        name=name,
        scratch_shapes=scratch,
        compiler_params=pltpu.CompilerParams(vmem_limit_bytes=VMEM_LIMIT),
    )(*scalars, *far, *operands, *args)


def sds(shape, dtype=f32):
    return pltpu.VMEM(shape, dtype)


def over_strike(x, width):
    unit = width if width in (1, 2, 4) else 1
    return lax.all_to_all(x.reshape(PS * width // unit, unit, PS), STRIKE, 0, 0, tiled=True).reshape(PS * width, PS)


def body(slip, rate, prestress, normal_stress, history, fric_flag, row_dest, row_node, fe_traction, fe_count):
    tables, turns = [jnp.asarray(t) for t in dip_tables()]
    strike = [jnp.asarray(t) for t in strike_tables()] + [jnp.asarray(memory_tables())]
    dest = row_dest.reshape(1, ROWS)

    slip_new = slip + RATE_DT * rate
    other = lax.ppermute(slip_new, "dip", [(i, i ^ 1) for i in range(QD)])
    mem, sums, perm, tables, turns = call(
        near_kernel,
        (
            sds((2 * PS, PS)),
            sds((8 * ROWS_DEV, COLS_DEV)),
            sds((COLS_DEV, COLS_DEV), bf16),
            sds(tables.shape, bf16),
            sds(turns.shape),
        ),
        (slip_new,),
        "near",
        far=(history, tables, turns),
        scratch=[sds(history.shape), pltpu.SemaphoreType.DMA((history.shape[0] + 2,))],
    )
    sent = call(send_kernel, sds((PS * SEND, PS)), (other, mem, sums, perm, tables, turns), "send")
    recv = over_strike(sent, SEND)
    box, rank, perm, turned, factor = call(
        route_kernel,
        (
            sds((PS, PS)),
            sds((1, ROWS), jnp.int32),
            sds((COLS_DEV, COLS_DEV), bf16),
            sds((4, COLS_DEV, COLS_DEV // 4), bf16),
            sds((2 * PS, PS)),
        ),
        (tables,),
        "route",
        (fe_count,),
        (dest, row_node, fe_traction),
    )
    sent = call(strike_kernel, sds((PS * BACK, PS)), (recv, box, factor), "strike", args=strike)
    recv = over_strike(sent, BACK)
    shares = call(
        dip_kernel,
        jax.ShapeDtypeStruct((QD, *slip.shape), f32),
        (recv, perm, turned, turns),
        "dip",
        far_outs=1,
        scratch=[sds((2, QD, ROWS_DEV, COLS_DEV // 2)), pltpu.SemaphoreType.DMA((2,))],
    )
    shares = lax.all_to_all(shares, "dip", 0, 0, tiled=True)
    traction, onehots, spots = call(
        traction_kernel,
        (sds(slip.shape), sds((CAP // 4, PS, CHUNK), bf16), sds((CAP, PS), jnp.int32)),
        (recv,),
        "traction",
    )
    new_rate, stress, sampled = call(
        owner_kernel,
        (jax.ShapeDtypeStruct(slip.shape, f32), jax.ShapeDtypeStruct(slip.shape, f32), sds((PS, PS))),
        (shares, traction, onehots, spots),
        "owner",
        args=(slip, rate, prestress, normal_stress, fric_flag),
        far_outs=2,
        scratch=[sds(slip.shape), sds(slip.shape), pltpu.SemaphoreType.DMA((2,))],
    )
    got = over_strike(sampled, 1)
    fe_rate = call(return_kernel, jax.ShapeDtypeStruct((1, ROWS), f32), (got, rank), "back", (fe_count,), (dest,))
    return new_rate, stress, fe_rate


def solution(mesh):
    fine = Mesh(mesh.devices.reshape(8, 8, 2, 4), ("z", "y", "c", "dip"))
    field = P(STRIKE, "dip")
    rows = P("dip", STRIKE)
    in_specs = (field, field, field, field, P(None, None, STRIKE, "dip"), field, P("dip", STRIKE, None), rows, rows, rows)
    return jax.shard_map(body, mesh=fine, in_specs=in_specs, out_specs=(field, field, rows), check_vma=False)
```

```python
import math

import jax
import jax.numpy as jnp
import numpy as np
from jax import lax
from jax.experimental import pallas as pl
from jax.experimental.pallas import tpu as pltpu
from jax.sharding import Mesh
from jax.sharding import PartitionSpec as P

NS, ND = 4096, 2048
PS, QD = 128, 4
ROWS_DEV, COLS_DEV = NS // PS, ND // QD
RATE_DT = 0.5
LEVELS = 7
CAP = 64
ROWS = 4096
CHUNK = 512
VMEM_LIMIT = 24 << 20
STRIKE = ("z", "y", "c")
SEND, BACK = 4, 3
SCALE = 1.0 / math.sqrt(NS * ND)
bf16 = jnp.bfloat16
f32 = jnp.float32
NN = (((1,), (0,)), ((), ()))
NT = (((1,), (1,)), ((), ()))


def np_split(table):
    hi = table.astype(np.float32).astype(jnp.bfloat16)
    lo = (table - hi.astype(np.float64)).astype(np.float32).astype(jnp.bfloat16)
    return np.stack([hi, lo])


def np_rev(p):
    return sum(((p >> b) & 1) << (LEVELS - 1 - b) for b in range(LEVELS))


def dip_tables():
    ell = np.arange(COLS_DEV)
    ang = 2 * np.pi * ((np.arange(COLS_DEV // 4)[:, None] * ell[None, :]) % COLS_DEV) / COLS_DEV
    b = np.tile(np.arange(4), QD)[:, None]
    q = np.repeat(np.arange(QD), 4)[:, None]
    turn = 2 * np.pi * ((ell * b + COLS_DEV * q * ell) % ND) / ND
    tables = np.concatenate([np_split(np.cos(ang)), np_split(np.sin(ang))])
    return tables, np.stack([np.cos(turn), np.sin(turn)]).astype(np.float32)


def strike_tables():
    p = np.arange(PS)
    k1 = np_rev(p)
    ang = 2 * np.pi * ((k1[:, None] * p[None, :]) % PS) / PS
    first = np.concatenate([np.cos(ang), -np.sin(ang)])
    r = np.arange(ROWS_DEV)
    tw = 2 * np.pi * (k1[:, None] * r[None, :]) / NS
    twiddle = np.stack([np.tile(np.cos(tw), (1, 4)), np.tile(np.sin(tw), (1, 4))]).astype(np.float32)
    small = 2 * np.pi * ((r[:, None] * r[None, :]) % ROWS_DEV) / ROWS_DEV
    cb = np.kron(np.eye(4), np.cos(small))
    sb = np.kron(np.eye(4), np.sin(small))
    second = np.block([[cb, -sb], [sb, cb]])
    return np_split(first), np_split(first.T), twiddle, np_split(second)


def memory_tables():
    out = np.zeros((4, 2, 2, 32, 2, 2, 2, 32), np.float32)
    eye = np.eye(ROWS_DEV)
    for case in range(4):
        own = case & 1
        for parity in range(2):
            other = own if case >= 2 and parity == 0 else 1 - own
            for slot, part, w_re, w_im in ((own, 0, 0.5, 0.5), (own, 1, -0.5, 0.5), (other, 0, 0.5, -0.5), (other, 1, 0.5, 0.5)):
                out[case, parity, part, :, 0, parity, slot, :] += w_re * eye
                out[case, parity, part, :, 1, parity, slot, :] += w_im * eye
    return out.reshape(4, PS, 2 * PS).astype(jnp.bfloat16)


def dot(a, b, dims=NN):
    return lax.dot_general(a, b, dims, preferred_element_type=f32)


def split(x):
    hi = x.astype(bf16)
    return hi, (x - hi.astype(f32)).astype(bf16)


def dot_data_table(x, t_hi, t_lo):
    hi, lo = split(x)
    return dot(hi, t_hi) + (dot(lo, t_hi) + dot(hi, t_lo))


def dot_data_turned(x, t_hi, t_lo):
    hi, lo = split(x)
    return dot(hi, t_hi, NT) + (dot(lo, t_hi, NT) + dot(hi, t_lo, NT))


def dot_table_data(t_hi, t_lo, x):
    hi, lo = split(x)
    return dot(t_hi, hi) + (dot(t_hi, lo) + dot(t_lo, hi))


def iota(shape, dim):
    return lax.broadcasted_iota(jnp.int32, shape, dim)


def position():
    return lax.axis_index(STRIKE), lax.axis_index("dip")


def rev_bits(p):
    out = 0
    for b in range(LEVELS):
        out = out + (((p >> b) & 1) << (LEVELS - 1 - b))
    return out


def turn_rows(turns, q):
    return [(turns(0, 4 * q + b), turns(1, 4 * q + b)) for b in range(4)]


def interleave(dims):
    pos = iota((COLS_DEV, COLS_DEV), dims)
    return (iota((COLS_DEV, COLS_DEV), 1 - dims) == 4 * (pos & (PS - 1)) + (pos >> 7)).astype(f32).astype(bf16)


def by_class(x):
    return jnp.concatenate([x[:, PS * b : PS * (b + 1)] for b in range(4)], axis=0)


def signed(freq, length):
    return jnp.where(freq >= length // 2, freq - length, freq).astype(f32) * (1.0 / length)


def outer_modes(ell, q):
    return jnp.where(ell == 0, 1 - (q & 1), 1 - ((q ^ (q >> 1)) & 1)) == 1


def dip_forward_part(x, perm, tables, turns, q):
    parts = dot(jnp.concatenate(split(x), axis=0), perm).astype(bf16)
    hi, lo = by_class(parts[:ROWS_DEV]), by_class(parts[ROWS_DEV:])
    c = dot(hi, tables[0]) + (dot(lo, tables[0]) + dot(hi, tables[1]))
    s = dot(hi, tables[2]) + (dot(lo, tables[2]) + dot(hi, tables[3]))
    cs, ss = [], []
    for b, (ct, st) in enumerate(turn_rows(turns, q)):
        c_b, s_b = c[32 * b : 32 * b + 32], s[32 * b : 32 * b + 32]
        cs.append(ct * c_b - st * s_b)
        ss.append(st * c_b + ct * s_b)
    return jnp.concatenate(cs + ss, axis=0)


def slip_part(sums, q):
    sums = [sums[32 * i : 32 * i + 32] for i in range(8)]
    cs, ss = sums[:4], sums[4:]
    c_even, c_odd = cs[0] + cs[2], cs[1] + cs[3]
    s_sum = (ss[0] + ss[2]) + (ss[1] + ss[3])
    ell = iota((ROWS_DEV, COLS_DEV), 1)
    h_a = (c_even + c_odd) + s_sum
    h_d = (c_even + jnp.where(ell == 0, -c_odd, c_odd)) - s_sum
    even = cs[0] - cs[2] + ss[3] - ss[1]
    odd = ss[0] - ss[2] + cs[1] - cs[3]
    outer = outer_modes(ell, q)
    both = jnp.concatenate([jnp.where(outer, h_a, even + odd), jnp.where(outer, h_d, even - odd)], axis=0)
    both = [both[:, PS * i : PS * (i + 1)] for i in range(4)]
    return [jnp.concatenate(both[2 * h : 2 * h + 2], axis=0).T for h in range(2)]


def memory_weights(p, q):
    ks = rev_bits(p) + PS * iota((ROWS_DEV, COLS_DEV), 0)
    kd = q * COLS_DEV + iota((ROWS_DEV, COLS_DEV), 1)
    fs, fd = signed(ks, NS), signed(kd, ND)
    wave = (2.0 * math.pi) * jnp.sqrt(fs * fs + fd * fd)
    grow = jnp.exp(-0.15 * wave)
    ang = 0.9 * wave
    return grow * jnp.cos(ang), grow * jnp.sin(ang)


def memory_part(z_re, z_im, history, q):
    w_re, w_im = 0.5 * z_re, 0.5 * z_im
    m_re, m_im = w_re * history(0, 0), w_re * history(0, 1)
    for lag in range(1, 8):
        w_re, w_im = w_re * z_re - w_im * z_im, w_re * z_im + w_im * z_re
        m_re = m_re + w_re * history(lag, 0)
        m_im = m_im + w_re * history(lag, 1)
    both = jnp.concatenate([m_re, m_im], axis=0)
    shifted = pltpu.roll(both, COLS_DEV - 1, 1)
    near = [both[:, PS * i : PS * (i + 1)] for i in range(4)]
    far = [shifted[:, PS * i : PS * (i + 1)] for i in range(4)]
    blocks = [jnp.where(q < 2, near[i], far[3 - i]) for i in range(4)]
    row = iota((PS, PS), 0)
    perm = (iota((PS, PS), 1) == jnp.where(q < 2, row, PS - 1 - row)).astype(f32).astype(bf16)
    out = []
    for h in range(2):
        hi, lo = split(jnp.concatenate(blocks[2 * h : 2 * h + 2], axis=0))
        out.append(dot(perm, hi, NT) + dot(perm, lo, NT))
    return out


def near_kernel(history_in, tables_in, turns_in, own, mem, sums, perm, tables, turns, history, sems):
    p, q = position()
    lags = history.shape[0]
    far_tables = [
        pltpu.make_async_copy(tables_in, tables, sems.at[lags]),
        pltpu.make_async_copy(turns_in, turns, sems.at[lags + 1]),
    ]
    copies = [pltpu.make_async_copy(history_in.at[i], history.at[i], sems.at[i]) for i in range(lags)]
    for copy in far_tables + copies:
        copy.start()
    z_re, z_im = memory_weights(p, q)
    perm[...] = interleave(1)
    for copy in far_tables:
        copy.wait()
    sums[...] = dip_forward_part(own[...], perm[...], tables, lambda i, row: turns[i, pl.ds(row, 1), :], q)

    def read(lag, part):
        if part == 0:
            copies[lag].wait()
        return history[lag, part]

    for h, part in enumerate(memory_part(z_re, z_im, read, q)):
        mem[PS * h : PS * (h + 1), :] = part


def send_kernel(other, mem, sums, perm, tables, turns, out):
    q = position()[1]
    far = dip_forward_part(other[...], perm[...], tables, lambda i, row: turns[i, pl.ds(row, 1), :], q ^ 1)
    lines = slip_part(sums[...] + far, q)
    for h in range(2):
        out[pl.ds(h, PS, stride=SEND), :] = lines[h]
        out[pl.ds(2 + h, PS, stride=SEND), :] = mem[PS * h : PS * (h + 1), :]


def spectral_factor(p, q):
    n = PS
    lane = iota((n, n), 1)
    fs = signed(rev_bits(iota((n, n), 0)) + PS * (lane & 31), NS)
    fs = fs * fs
    parity, slot = lane >> 6, (lane >> 5) & 1
    factor = []
    for h in range(2):
        ell = p + PS * (2 * h + parity)
        kd = jnp.where(outer_modes(ell, q), jnp.where((ell == 0) & (slot == 1), 2 * COLS_DEV, ell), COLS_DEV + ell)
        fd = kd.astype(f32) * (1.0 / ND)
        wave = (2.0 * math.pi) * jnp.sqrt(fs + fd * fd)
        factor.append((-0.5 * SCALE) * wave)
    return jnp.concatenate(factor, axis=0)


def strike_part(lines, mems, factor, first, first_t, twiddle, second, mem_table, p, q):
    n = PS
    w = []
    for h in range(2):
        m_hi, m_lo = split(mems[h])
        alone = jnp.where((p == 0) & ((q & 1) == 0), 2, 0) if h == 0 else 0
        table = mem_table(alone + (q >> 1))
        w.append(dot(m_hi, table) + dot(m_lo, table))
    w = jnp.concatenate(w, axis=0)
    a = dot_table_data(first[0], first[1], jnp.concatenate(lines, axis=1))
    tc, ts = twiddle[0], twiddle[1]
    b = []
    for h in range(2):
        a_re, a_im = a[:n, n * h : n * (h + 1)], a[n:, n * h : n * (h + 1)]
        b.append(jnp.concatenate([a_re * tc + a_im * ts, a_im * tc - a_re * ts], axis=1))
    spec = dot_data_table(jnp.concatenate(b, axis=0), second[0], second[1])
    g = jnp.concatenate([factor, factor], axis=1) * (SCALE * spec - w)
    b = dot_data_turned(g, second[0], second[1])
    turned = []
    for h in range(2):
        b_re, b_im = b[n * h : n * (h + 1), :n], b[n * h : n * (h + 1), n:]
        turned.append(jnp.concatenate([b_re * tc - b_im * ts, b_re * ts + b_im * tc], axis=0))
    return dot_table_data(first_t[0], first_t[1], jnp.concatenate(turned, axis=1))


def strike_kernel(recv, outbox, factor, first, first_t, twiddle, second, mem_table, out):
    t = strike_part(
        [recv[pl.ds(h, PS, stride=SEND), :] for h in range(2)],
        [recv[pl.ds(2 + h, PS, stride=SEND), :] for h in range(2)],
        factor[...],
        first,
        first_t,
        twiddle,
        second,
        lambda i: mem_table[i],
        *position(),
    )
    for h in range(2):
        out[pl.ds(h, PS, stride=BACK), :] = t[:, PS * h : PS * (h + 1)]
    out[pl.ds(2, PS, stride=BACK), :] = outbox[...]


def route_part(dest, node, value, count):
    dest = [dest[:, CHUNK * i : CHUNK * (i + 1)] for i in range(ROWS // CHUNK)]
    upto = (iota((CHUNK, CHUNK), 0) <= iota((CHUNK, CHUNK), 1)).astype(f32).astype(bf16)
    carry = jnp.zeros((PS, 1), f32)
    box = jnp.zeros((PS, 2 * CAP), f32)
    ranks = []
    for i in range(ROWS // CHUNK):
        cut = slice(CHUNK * i, CHUNK * (i + 1))
        named = iota((PS, CHUNK), 0) == dest[i]
        onehot = named.astype(f32).astype(bf16)
        upto_here = dot(onehot, upto) + carry
        rank = jnp.sum(jnp.where(named, upto_here, 0.0), axis=0, keepdims=True).astype(jnp.int32) - 1
        carry = upto_here[:, CHUNK - 1 : CHUNK]
        ranks.append(rank)
        live = (CHUNK * i + iota((1, CHUNK), 1)) < count
        v = jnp.where(live, value[:, cut], 0.0)
        v_hi = v.astype(bf16).astype(f32)
        v_lo = v - v_hi
        at = node[:, cut]
        n_hi = ((((at >> 7) & 3) << 5) + (at >> 9)) << 7
        n_lo = at & 127
        here = iota((CAP, CHUNK), 0) == rank
        part_1 = jnp.concatenate([jnp.where(here, v_hi, 0.0), jnp.where(here, n_hi.astype(f32), 0.0)], axis=0)
        part_2 = jnp.concatenate([jnp.where(here, v_lo, 0.0), jnp.where(here, n_lo.astype(f32), 0.0)], axis=0)
        box = box + (dot(onehot, part_1.astype(bf16), NT) + dot(onehot, part_2.astype(bf16), NT))
    return box, jnp.concatenate(ranks, axis=1)


def route_kernel(count, tables, dest, node, value, out, rank, perm, turned, factor):
    out[...], rank[...] = route_part(dest[...], node[...], value[...], count[0, 0])
    perm[...] = interleave(0)
    for i in range(4):
        turned[i] = tables[i].astype(f32).T.astype(bf16)
    factor[...] = spectral_factor(*position())


def dip_inverse_part(lines, tables, turns, perm, q):
    lines = [x.T for x in lines]
    t0, t1 = [
        jnp.concatenate([lines[i >> 1][64 * (i & 1) + 32 * slot : 64 * (i & 1) + 32 * slot + 32] for i in range(4)], axis=1)
        for slot in range(2)
    ]
    ell = iota((ROWS_DEV, COLS_DEV), 1)
    outer = outer_modes(ell, q)
    total, diff = t0 + t1, t0 - t1
    s1, d1 = jnp.where(outer, total, 0.0), jnp.where(outer, diff, 0.0)
    s2, d2 = total - s1, diff - d1
    fix = jnp.where(outer & (ell == 0), 2.0 * t1, 0.0)
    even = [s1 + s2, s1 + d2 - fix, s1 - s2, s1 - d2 - fix]
    odd = [d1 + d2, d1 - s2, d1 - d2, d1 + s2]
    evens, odds = [], []
    for i, (ct, st) in enumerate(turn_rows(turns, 0)):
        evens.append(ct * even[i] + st * odd[i])
        odds.append(ct * odd[i] - st * even[i])
    evens, odds = split(jnp.concatenate(evens, axis=0)), split(jnp.concatenate(odds, axis=0))
    turn = iota((1, COLS_DEV), 1) & 3
    keep_even = jnp.where((turn & 1) == 0, 1.0, 0.0).astype(bf16)
    keep_odd = jnp.where((turn & 1) == 1, 1.0, 0.0).astype(bf16)
    flip_even = jnp.where(turn == 0, 1.0, jnp.where(turn == 2, -1.0, 0.0)).astype(bf16)
    flip_odd = jnp.where(turn == 1, 1.0, jnp.where(turn == 3, -1.0, 0.0)).astype(bf16)
    f = 0.0
    for k, x, y, sign in ((0, evens, odds, flip_odd), (2, odds, evens, -flip_odd)):
        hi, lo = [
            jnp.concatenate([x[i] * keep_even, x[i] * keep_odd, x[i] * flip_even, y[i] * sign], axis=0) for i in range(2)
        ]
        f = f + (dot(hi, tables[k]) + (dot(lo, tables[k]) + dot(hi, tables[k + 1])))
    f = [f[PS * i : PS * (i + 1)] for i in range(4)]
    f = [f[0] + f[1], f[2] + f[3], f[0] - f[1], f[2] - f[3]]
    rows = 32
    f = jnp.concatenate([jnp.concatenate([x[rows * i : rows * (i + 1)] for i in range(4)], axis=1) for x in f], axis=0)
    hi, lo = split(f)
    f = dot(hi, perm) + dot(lo, perm)
    return [f[rows * qd : rows * (qd + 1)] for qd in range(QD)]


def dip_kernel(recv, perm, tables, turns, out):
    lines = [recv[pl.ds(h, PS, stride=BACK), :] for h in range(2)]
    shares = dip_inverse_part(lines, tables, lambda i, row: turns[i, row : row + 1, :], perm[...], position()[1])
    for qd, share in enumerate(shares):
        out[qd] = share


def unpack_rows(fe, roll):
    top, bot = fe[0:CAP], fe[CAP:PS]
    left = iota((CAP, PS), 1) < CAP
    value = jnp.where(left, top, roll(bot))
    node = jnp.where(left, roll(top), bot).astype(jnp.int32)
    return value, node >> 7, node & 127


def lanes_of(x, group):
    return jnp.concatenate([x[4 * group + i : 4 * group + i + 1] for i in range(4)], axis=1)


def column_onehot(lo):
    return (iota((PS, CHUNK), 0) == lo).astype(f32).astype(bf16)


def traction_step(value, hi, onehot):
    named = iota((PS, CHUNK), 0) == hi
    v_hi = value.astype(bf16).astype(f32)
    rows = jnp.concatenate([jnp.where(named, v_hi, 0.0), jnp.where(named, value - v_hi, 0.0)], axis=0).astype(bf16)
    return dot(rows, onehot, NT)


def sample_step(rate_parts, hi, onehot):
    got = dot(rate_parts, jnp.concatenate([onehot, onehot], axis=0))
    return jnp.sum(jnp.where(iota((PS, CHUNK), 0) == hi, got, 0.0), axis=0, keepdims=True)


def roll_half(x):
    return pltpu.roll(x, CAP, 1)


def traction_kernel(recv, traction, onehots, spots):
    value, hi, lo = unpack_rows(recv[pl.ds(2, PS, stride=BACK), :], roll_half)
    spots[...] = hi
    acc = jnp.zeros((2 * PS, PS), f32)
    for g in range(CAP // 4):
        onehot = column_onehot(lanes_of(lo, g))
        onehots[g] = onehot
        acc = acc + traction_step(lanes_of(value, g), lanes_of(hi, g), onehot)
    acc = acc[:PS] + acc[PS:]
    traction[...] = jnp.concatenate([acc[32 * i : 32 * i + 32] for i in range(4)], axis=1)


def owner_kernel(
    shares, traction, onehots, spots, slip, rate, prestress, normal, flag, new_rate_out, stress_out, sampled, new_rate, stress, sems
):
    f = (shares[0] + shares[1]) + (shares[2] + shares[3])
    slip_new = slip[...] + RATE_DT * rate[...]
    total = prestress[...] + f + traction[...]
    strength = normal[...] * (0.6 - (0.6 - 0.4) * jnp.minimum(slip_new, 1.0))
    fresh = jnp.where(flag[...] == 1, jnp.maximum(total - strength, 0.0) * 2.0, 0.0)
    stress[...] = total
    new_rate[...] = fresh
    copies = [
        pltpu.make_async_copy(new_rate, new_rate_out, sems.at[0]),
        pltpu.make_async_copy(stress, stress_out, sems.at[1]),
    ]
    for copy in copies:
        copy.start()
    stacked = jnp.concatenate([fresh[:, PS * i : PS * (i + 1)] for i in range(4)], axis=0)
    parts = jnp.concatenate(split(stacked), axis=1)
    hi = spots[...]
    for g in range(CAP // 4):
        got = sample_step(parts, lanes_of(hi, g), onehots[g])
        for i in range(4):
            sampled[4 * g + i : 4 * g + i + 1, :] = got[:, PS * i : PS * (i + 1)]
    sampled[CAP:PS, :] = roll_half(sampled[0:CAP, :])
    for copy in copies:
        copy.wait()


def return_part(got, dest, rank, count):
    parts = jnp.concatenate(split(got[:, :CAP]), axis=1)
    out = []
    for i in range(ROWS // CHUNK):
        cut = slice(CHUNK * i, CHUNK * (i + 1))
        onehot = (iota((CAP, CHUNK), 0) == rank[:, cut]).astype(f32).astype(bf16)
        here = dot(parts, jnp.concatenate([onehot, onehot], axis=0))
        here = jnp.sum(jnp.where(iota((PS, CHUNK), 0) == dest[:, cut], here, 0.0), axis=0, keepdims=True)
        live = (CHUNK * i + iota((1, CHUNK), 1)) < count
        out.append(jnp.where(live, here, 0.0))
    return jnp.concatenate(out, axis=1)


def return_kernel(count, got, rank, dest, out):
    out[...] = return_part(got[...], dest[...], rank[...], count[0, 0])


def call(kernel, out_shape, operands, name, scalars=(), args=(), far=(), far_outs=0, scratch=()):
    spec = pl.BlockSpec(memory_space=pltpu.VMEM)
    hbm = pl.BlockSpec(memory_space=pltpu.HBM)
    in_specs = [pl.BlockSpec(memory_space=pltpu.SMEM)] * len(scalars) + [hbm] * len(far) + [spec] * (len(operands) + len(args))
    outs = tuple(hbm if i < far_outs else spec for i in range(len(out_shape))) if isinstance(out_shape, tuple) else spec
    far = [pltpu.with_memory_space_constraint(x, pltpu.HBM) for x in far]
    operands = [pltpu.with_memory_space_constraint(x, pltpu.VMEM) for x in operands]
    return pl.pallas_call(
        kernel,
        out_shape=out_shape,
        in_specs=in_specs,
        out_specs=outs,
        name=name,
        scratch_shapes=scratch,
        compiler_params=pltpu.CompilerParams(vmem_limit_bytes=VMEM_LIMIT),
    )(*scalars, *far, *operands, *args)


def sds(shape, dtype=f32):
    return pltpu.VMEM(shape, dtype)


def over_strike(x, width):
    unit = width if width in (1, 2, 4) else 1
    return lax.all_to_all(x.reshape(PS * width // unit, unit, PS), STRIKE, 0, 0, tiled=True).reshape(PS * width, PS)


def body(slip, rate, prestress, normal_stress, history, fric_flag, row_dest, row_node, fe_traction, fe_count):
    tables, turns = [jnp.asarray(t) for t in dip_tables()]
    strike = [jnp.asarray(t) for t in strike_tables()] + [jnp.asarray(memory_tables())]
    dest = row_dest.reshape(1, ROWS)

    slip_new = slip + RATE_DT * rate
    other = lax.ppermute(slip_new, "dip", [(i, i ^ 1) for i in range(QD)])
    mem, sums, perm, tables, turns = call(
        near_kernel,
        (
            sds((2 * PS, PS)),
            sds((8 * ROWS_DEV, COLS_DEV)),
            sds((COLS_DEV, COLS_DEV), bf16),
            sds(tables.shape, bf16),
            sds(turns.shape),
        ),
        (slip_new,),
        "near",
        far=(history, tables, turns),
        scratch=[sds(history.shape), pltpu.SemaphoreType.DMA((history.shape[0] + 2,))],
    )
    sent = call(send_kernel, sds((PS * SEND, PS)), (other, mem, sums, perm, tables, turns), "send")
    recv = over_strike(sent, SEND)
    box, rank, perm, turned, factor = call(
        route_kernel,
        (
            sds((PS, PS)),
            sds((1, ROWS), jnp.int32),
            sds((COLS_DEV, COLS_DEV), bf16),
            sds((4, COLS_DEV, COLS_DEV // 4), bf16),
            sds((2 * PS, PS)),
        ),
        (tables,),
        "route",
        (fe_count,),
        (dest, row_node, fe_traction),
    )
    sent = call(strike_kernel, sds((PS * BACK, PS)), (recv, box, factor), "strike", args=strike)
    recv = over_strike(sent, BACK)
    shares = call(dip_kernel, sds((QD, ROWS_DEV, COLS_DEV)), (recv, perm, turned, turns), "dip")
    shares = lax.all_to_all(shares, "dip", 0, 0, tiled=True)
    traction, onehots, spots = call(
        traction_kernel,
        (sds(slip.shape), sds((CAP // 4, PS, CHUNK), bf16), sds((CAP, PS), jnp.int32)),
        (recv,),
        "traction",
    )
    new_rate, stress, sampled = call(
        owner_kernel,
        (jax.ShapeDtypeStruct(slip.shape, f32), jax.ShapeDtypeStruct(slip.shape, f32), sds((PS, PS))),
        (shares, traction, onehots, spots),
        "owner",
        args=(slip, rate, prestress, normal_stress, fric_flag),
        far_outs=2,
        scratch=[sds(slip.shape), sds(slip.shape), pltpu.SemaphoreType.DMA((2,))],
    )
    got = over_strike(sampled, 1)
    fe_rate = call(return_kernel, jax.ShapeDtypeStruct((1, ROWS), f32), (got, rank), "back", (fe_count,), (dest,))
    return new_rate, stress, fe_rate


def solution(mesh):
    fine = Mesh(mesh.devices.reshape(8, 8, 2, 4), ("z", "y", "c", "dip"))
    field = P(STRIKE, "dip")
    rows = P("dip", STRIKE)
    in_specs = (field, field, field, field, P(None, None, STRIKE, "dip"), field, P("dip", STRIKE, None), rows, rows, rows)
    return jax.shard_map(body, mesh=fine, in_specs=in_specs, out_specs=(field, field, rows), check_vma=False)
```
